32 devices in a mesh: rows: 8 (over z, y), cols: 4 (over x, core).
Axes of the slice: x: 2, y: 2, z: 4, core: 2. Of those that a mesh axis runs over, the one named last changes fastest.
Arguments:
- sketch: float32 [32768, 256], P(('rows', 'cols'))
- tiles: bfloat16 [1280, 512, 512], P(('rows', 'cols')), may hold values from -48 to 48
- tile_user: int32 [1280], P(('rows', 'cols')), may hold values from 0 to 7
- tile_item: int32 [1280], P(('rows', 'cols')), may hold values from 0 to 7
- tile_count: int32 [32], P(('rows', 'cols')), may hold values from 5 to 40, as said below
- item_owner: int32 [4, 8], P('cols'), may hold values from 0 to 7, each once within a row
Outputs:
- projected: float32 [8, 4, 256, 512], P('rows', 'cols')
The draws below stay inside these ranges and needn't reach their ends.
Inputs may be any that keep to these rules, and one draw needn't show every extreme that they name: `tile_count`: live slots of a device are its first slots; some device has all 40 live in every draw.
All inputs are finite; a program needn't handle non-finite values.
Results may differ from the reference program's by a relative error of at most 0.0029.
Values may be sent and summed in bfloat16 or wider, within the bound.
No kernel may reach another device: no remote copies, remote signals or barrier semaphores. Data moves between devices by JAX's collectives and lax.ppermute only.
A program may use at most 192 MiB of HBM per device.

```python
import jax
import jax.numpy as jnp
from jax import lax

K = 256
TILE = 512
U_DEV = 1024
TILES_MAX = 40
USERS = 32768
IBS = 8
UB_GROUP = 8
TILE_SLOTS = 1280
N_COLS = 4


def draw_sketch(key, part):
    key_base = jax.random.fold_in(key, 0)
    devices_all = USERS // U_DEV
    device_of_row = jnp.arange(USERS) // U_DEV
    ramp = 1.0 + 2.0 * device_of_row.astype(jnp.float32) / max(devices_all - 1, 1)
    values = jax.random.normal(key_base, (USERS, K), jnp.float32) * ramp[:, None]
    return values.astype(jnp.float32)


def draw_tile_count(key, part):
    key_base, key_busy = jax.random.split(key)
    devices_all = TILE_SLOTS // TILES_MAX
    lowest = max(1, TILES_MAX // 8)
    highest = max(lowest + 1, TILES_MAX // 3 + 1)
    counts = jax.random.randint(key_base, (devices_all,), lowest, highest)
    chosen = jax.random.permutation(key_busy, devices_all)[:max(1, devices_all // 8)]
    counts = counts.at[chosen].set(TILES_MAX)
    return counts.astype(jnp.int32)


def set_ends(values, stream_key, low, top_value):
    longest = values.shape.index(max(values.shape))
    spots = []
    for shift in (0, 1):
        where = [jax.random.randint(jax.random.fold_in(stream_key, axis), (), 0, length) for axis, length in enumerate(values.shape)]
        where[longest] = (where[longest] + shift) % values.shape[longest]
        spots.append(tuple(where))
    return values.at[spots[0]].set(low).at[spots[1]].set(top_value)


def block_levels(rng, extent, cuts, smallest, largest):
    def one(dim, blocks):
        heights = jax.random.uniform(jax.random.fold_in(jax.random.fold_in(rng, 6), dim), (blocks,), jnp.float32, smallest / len(cuts), largest / len(cuts))
        return jnp.repeat(jnp.exp(heights), extent[dim] // blocks).reshape((-1,) + (1,) * (len(extent) - dim - 1))

    loudness = one(*cuts[0])
    for cut in cuts[1:]:
        loudness = loudness * one(*cut)
    return loudness


def bell_draw(stream_key, shape, width, reach, cuts=(), kind=jnp.bfloat16):
    level = block_levels(stream_key, shape, cuts, -0.22, 0.18) if cuts else 1.0
    values = jax.random.normal(stream_key, shape, jnp.float32) * width * level
    return jnp.minimum(jnp.maximum(values, -reach), reach).astype(kind)


def setup_inputs(seed: int = 0) -> dict:
    keys = jax.random.split(jax.random.key(seed), 7)
    sketch = draw_sketch(jax.random.fold_in(keys[6], 71), 0)
    tiles = bell_draw(keys[1], (TILE_SLOTS, TILE, TILE), ((USERS // TILE) ** 0.5), 48.0, ((0, 32),))
    tile_user = set_ends(jax.random.randint(keys[2], (TILE_SLOTS,), 0, UB_GROUP), jax.random.fold_in(keys[2], 1), 0, UB_GROUP - 1).astype(jnp.int32)
    tile_item = set_ends(jax.random.randint(keys[3], (TILE_SLOTS,), 0, IBS), jax.random.fold_in(keys[3], 1), 0, IBS - 1).astype(jnp.int32)
    tile_count = draw_tile_count(jax.random.fold_in(keys[6], 71), 0)
    item_owner = jax.vmap(lambda own: jax.random.permutation(own, IBS))(jax.random.split(keys[5], N_COLS)).reshape((N_COLS, IBS)).astype(jnp.int32)
    return dict(sketch=sketch, tiles=tiles, tile_user=tile_user, tile_item=tile_item, tile_count=tile_count, item_owner=item_owner)


def reference(sketch, tiles, tile_user, tile_item, tile_count, item_owner):
    gram = lax.dot_general(sketch.astype(jnp.float32), sketch.astype(jnp.float32), (((0,), (0,)), ((), ())), precision=lax.Precision.HIGHEST, preferred_element_type=jnp.float32)
    lower_factor = jnp.linalg.cholesky(gram)
    basis_full = lax.linalg.triangular_solve(lower_factor, sketch, left_side=False, lower=True, transpose_a=True)
    basis = basis_full.astype(jnp.bfloat16)
    result = jnp.zeros((IBS, N_COLS, K, TILE), jnp.float32)

    def step(index, totals):
        device = index // TILES_MAX
        slot_pos = index % TILES_MAX
        group = device // N_COLS
        stripe = device % N_COLS
        start = ((group * UB_GROUP + tile_user[index]) * TILE).astype(jnp.int32)
        basis_rows = lax.dynamic_slice_in_dim(basis, start, TILE, 0)
        partial_value = lax.dot_general(basis_rows.astype(jnp.float32), tiles[index].astype(jnp.float32), (((0,), (0,)), ((), ())), preferred_element_type=jnp.float32)
        partial_value = jnp.where(slot_pos < tile_count[device], partial_value, jnp.zeros_like(partial_value))
        target = item_owner[stripe, tile_item[index]]
        current = totals[target, stripe]
        return totals.at[target, stripe].set(current + partial_value)
    return lax.fori_loop(0, TILE_SLOTS, step, result)
```

```python
import functools

import jax
import jax.numpy as jnp
from jax import lax
from jax.experimental import pallas as pl
from jax.experimental.pallas import tpu as pltpu
from jax.sharding import PartitionSpec as P

F32 = jnp.float32
BF16 = jnp.bfloat16
HIGH = lax.Precision.HIGHEST
SLOTS = 6
CHUNKS = 2
NEWTON = 3


def swap(x, axis, count, bit):
    return lax.ppermute(x, axis, [(i, i ^ bit) for i in range(count)])


def places(order, parity):
    found = [parity << order[0]]
    for bit in reversed(order[1:]):
        found = found + [p | (1 << bit) for p in found]
    return found


def tile_kernel(orders, users, items, owner, meta, *refs):
    piece_count = (len(refs) - 1 - 2 * len(orders) - 4)
    pieces = refs[:piece_count]
    tiles = refs[piece_count]
    outs = refs[piece_count + 1 : piece_count + 1 + 2 * len(orders)]
    slab, acc, buf, sems = refs[-4:]
    count, row, col = meta[0], meta[1], meta[2]
    tile_size = tiles.shape[1]
    kc = pieces[0].shape[1]
    per_piece = pieces[0].shape[0] // tile_size

    def fetch(t):
        slot = lax.rem(t, SLOTS)
        return pltpu.make_async_copy(tiles.at[t], buf.at[slot], sems.at[slot])

    for t in range(SLOTS):
        @pl.when(t < count)
        def _():
            fetch(t).start()

    acc[...] = jnp.zeros_like(acc)
    for c in range(piece_count):
        for h in range(per_piece):
            block = pieces[c][h * tile_size : (h + 1) * tile_size, :].T
            high = block.astype(BF16)
            slab[c * per_piece + h, :kc, :] = high
            slab[c * per_piece + h, kc:, :] = (block - high.astype(F32)).astype(BF16)

    def step(t, _):
        user = users[t]
        which = lax.bitwise_xor(user // per_piece, col) * per_piece + lax.rem(user, per_piece)
        place = lax.bitwise_xor(owner[items[t]], row)
        fetch(t).wait()
        both = jnp.dot(slab[which], buf[lax.rem(t, SLOTS)], preferred_element_type=F32)
        acc[place] += both[:kc] + both[kc:]

        @pl.when(t + SLOTS < count)
        def _():
            fetch(t + SLOTS).start()

        return 0

    lax.fori_loop(0, count, step, 0)
    width = tile_size // len(orders)
    for o, order in enumerate(orders):
        cut = slice(o * width, (o + 1) * width)
        for k, place in enumerate(places(order, 0)):
            outs[2 * o][k] = acc[place, :, cut]
        for k, place in enumerate(places(order, 1)):
            outs[2 * o + 1][k] = acc[place, :, cut].astype(BF16)


def tile_sums(orders, row_count, users, items, owner, meta, pieces, tiles):
    kc = pieces[0].shape[1]
    tile_size = tiles.shape[1]
    width = tile_size // len(orders)
    half = row_count // 2
    shapes = []
    for _ in orders:
        shapes.append(jax.ShapeDtypeStruct((half, kc, width), F32))
        shapes.append(jax.ShapeDtypeStruct((half, kc, width), BF16))
    blocks = len(pieces) * pieces[0].shape[0] // tile_size
    smem = pl.BlockSpec(memory_space=pltpu.SMEM)
    vmem = pl.BlockSpec(memory_space=pltpu.VMEM)
    return pl.pallas_call(
        functools.partial(tile_kernel, orders),
        out_shape=shapes,
        in_specs=[smem] * 4 + [vmem] * len(pieces) + [pl.BlockSpec(memory_space=pl.ANY)],
        out_specs=[vmem] * len(shapes),
        scratch_shapes=[
            pltpu.VMEM((blocks, 2 * kc, tile_size), BF16),
            pltpu.VMEM((row_count, kc, tile_size), F32),
            pltpu.VMEM((SLOTS, tile_size, tile_size), BF16),
            pltpu.SemaphoreType.DMA((SLOTS,)),
        ],
        compiler_params=pltpu.CompilerParams(vmem_limit_bytes=48 * 2**20),
        cost_estimate=pl.CostEstimate(
            flops=20 * 4 * kc * tile_size**2, bytes_accessed=20 * 2 * tile_size**2, transcendentals=0
        ),
    )(users, items, owner, meta, *pieces, tiles)


def mm(a, b):
    return lax.dot_general(a, b, (((1,), (0,)), ((), ())), precision=HIGH, preferred_element_type=F32)


def mmt(a, b):
    return lax.dot_general(a, b, (((1,), (1,)), ((), ())), precision=HIGH, preferred_element_type=F32)


def factor_kernel(packed, inverse, check):
    n = packed.shape[1]
    r = lax.broadcasted_iota(jnp.int32, (n, n), 0)
    c = lax.broadcasted_iota(jnp.int32, (n, n), 1)
    mixed = packed[:n]
    flipped = mixed.T
    side = packed[n : 2 * n]
    tail = jnp.broadcast_to(packed[2 * n : 2 * n + 1], (n, n))
    first = jnp.where(r >= c, mixed, flipped)
    second = jnp.where(r < c, mixed, jnp.where(r > c, flipped, tail))
    gram = jnp.concatenate(
        [jnp.concatenate([first, side.T], axis=1), jnp.concatenate([side, second], axis=1)], axis=0
    )
    m = 2 * n
    rr = lax.broadcasted_iota(jnp.int32, (m, m), 0)
    cc = lax.broadcasted_iota(jnp.int32, (m, m), 1)
    on = rr == cc
    eye = jnp.where(on, 1.0, 0.0).astype(F32)
    low = jnp.where(rr > cc, 1.0, jnp.where(on, 0.5, 0.0)).astype(F32)
    diag = jnp.where(on, gram, 0.0)
    scale_row = lax.rsqrt(jnp.sum(diag, axis=0, keepdims=True))
    scale_col = lax.rsqrt(jnp.sum(diag, axis=1, keepdims=True))
    unit = gram * scale_row * scale_col
    off = unit - eye
    spread = jnp.max(jnp.sum(jnp.abs(mm(off, off)), axis=1))
    w = eye - low * off
    for _ in range(NEWTON):
        err = mmt(mm(w, unit), w) - eye
        w = w - mm(low * err, w)
    last = jnp.max(jnp.sum(jnp.abs(err), axis=1))
    inflation = jnp.max(jnp.sum(w * w, axis=0))
    inverse[...] = w * scale_row
    check[0] = spread
    check[1] = last
    check[2] = inflation


def factor(packed):
    n = packed.shape[1]
    return pl.pallas_call(
        factor_kernel,
        out_shape=[jax.ShapeDtypeStruct((2 * n, 2 * n), F32), jax.ShapeDtypeStruct((3,), F32)],
        in_specs=[pl.BlockSpec(memory_space=pltpu.VMEM)],
        out_specs=[pl.BlockSpec(memory_space=pltpu.VMEM), pl.BlockSpec(memory_space=pltpu.SMEM)],
        compiler_params=pltpu.CompilerParams(vmem_limit_bytes=24 * 2**20),
        cost_estimate=pl.CostEstimate(
            flops=11 * 6 * 2 * 8 * n**3, bytes_accessed=6 * 4 * n * n, transcendentals=0
        ),
    )(packed)


def pack(gram):
    n = gram.shape[0] // 2
    r = lax.broadcasted_iota(jnp.int32, (n, n), 0)
    c = lax.broadcasted_iota(jnp.int32, (n, n), 1)
    mixed = jnp.where(r >= c, gram[:n, :n], gram[n:, n:])
    tail = jnp.sum(jnp.where(r == c, gram[n:, n:], 0.0), axis=0, keepdims=True)
    return jnp.concatenate([mixed, gram[n:, :n], jnp.broadcast_to(tail, (8, n))], axis=0)


def full_path(sketch, tiles, tile_user, tile_item, tile_count, item_owner, packed):
    n = packed.shape[1]
    r = lax.broadcasted_iota(jnp.int32, (n, n), 0)
    c = lax.broadcasted_iota(jnp.int32, (n, n), 1)
    mixed, side, tail = packed[:n], packed[n : 2 * n], packed[2 * n : 2 * n + 1]
    first = jnp.where(r >= c, mixed, mixed.T)
    second = jnp.where(r < c, mixed, jnp.where(r > c, mixed.T, tail))
    gram = jnp.block([[first, side.T], [side, second]])
    lower = jnp.linalg.cholesky(gram)
    basis = lax.linalg.triangular_solve(lower, sketch, left_side=False, lower=True, transpose_a=True).astype(BF16)
    slab = lax.all_gather(basis, "cols", axis=0, tiled=True)
    owner = item_owner[0]
    tile_size = tiles.shape[2]

    def step(index, sums):
        rows = lax.dynamic_slice_in_dim(slab, tile_user[index] * tile_size, tile_size, 0)
        part = lax.dot_general(rows, tiles[index], (((0,), (0,)), ((), ())), preferred_element_type=F32)
        place = owner[tile_item[index]]
        now = lax.dynamic_index_in_dim(sums, place, 0, keepdims=False)
        return lax.dynamic_update_index_in_dim(sums, now + part, place, 0)

    totals = jnp.zeros((owner.shape[0], sketch.shape[1], tile_size), F32)
    totals = lax.fori_loop(0, tile_count[0], step, totals)
    return lax.psum_scatter(totals, "rows", scatter_dimension=0, tiled=True)[0]


def body(rows, cols, sketch, tiles, tile_user, tile_item, tile_count, item_owner):
    width = sketch.shape[1]
    row_bits = rows.bit_length() - 1
    first_order = tuple(range(row_bits))
    orders = (first_order, (1, 0) + first_order[2:])
    row = lax.axis_index("rows")
    col = lax.axis_index("cols")
    meta = jnp.stack([tile_count[0], row, col]).astype(jnp.int32)
    owner = item_owner[0]

    kc = width // CHUNKS
    gathered = []
    for k in range(CHUNKS):
        pieces = [sketch[:, k * kc : (k + 1) * kc]]
        gathered.append(pieces)
    bits = []
    bit = cols // 2
    while bit:
        bits.append(bit)
        bit //= 2
    for k in range(CHUNKS):
        have = {0: gathered[k][0]}
        for bit in bits:
            for place in list(have):
                have[place | bit] = swap(have[place], "cols", cols, bit)
        gathered[k] = [have[i] for i in range(cols)]

    gram = lax.dot_general(
        sketch, sketch, (((0,), (0,)), ((), ())), precision=HIGH, preferred_element_type=F32
    )
    packed = pack(gram)
    for bit in reversed(bits):
        packed = packed + swap(packed, "cols", cols, bit)
    for b in range(row_bits):
        packed = packed + swap(packed, "rows", rows, 1 << b)
    inverse, check = factor(packed)

    halves = []
    for k in range(CHUNKS):
        outs = tile_sums(orders, rows, tile_user, tile_item, owner, meta, gathered[k], tiles)
        done = []
        for o, order in enumerate(orders):
            keep, send = outs[2 * o], outs[2 * o + 1]
            for pos, b in enumerate(order):
                got = swap(send, "rows", rows, 1 << b)
                total = keep + got.astype(F32)
                if pos + 1 < len(order):
                    half = total.shape[0] // 2
                    keep, send = total[:half], total[half:].astype(BF16)
            done.append(total[0])
        halves.append(jnp.concatenate(done, axis=1))
    sums = jnp.concatenate(halves, axis=0)
    good = (check[0] < 0.16) & (check[1] < 1e-3) & (check[2] < 1.1)
    out = lax.cond(
        good,
        lambda: mm(inverse, sums),
        lambda: full_path(sketch, tiles, tile_user, tile_item, tile_count, item_owner, packed),
    )
    return out[None, None]


def solution(mesh):
    placed = (
        P(("rows", "cols"), None),
        P(("rows", "cols"), None, None),
        P(("rows", "cols")),
        P(("rows", "cols")),
        P(("rows", "cols")),
        P("cols", None),
    )
    return jax.shard_map(
        functools.partial(body, mesh.shape["rows"], mesh.shape["cols"]),
        mesh=mesh,
        in_specs=placed,
        out_specs=P("rows", "cols", None, None),
        check_vma=False,
    )
```

```python
import functools

import jax
import jax.numpy as jnp
from jax import lax
from jax.experimental import pallas as pl
from jax.experimental.pallas import tpu as pltpu
from jax.sharding import PartitionSpec as P

F32 = jnp.float32
BF16 = jnp.bfloat16
HIGH = lax.Precision.HIGHEST
SLOTS = 6
CHUNKS = 2
NEWTON = 2


def swap(x, axis, count, bit):
    return lax.ppermute(x, axis, [(i, i ^ bit) for i in range(count)])


def places(order, parity):
    found = [parity << order[0]]
    for bit in reversed(order[1:]):
        found = found + [p | (1 << bit) for p in found]
    return found


def tile_kernel(orders, users, items, owner, meta, *refs):
    piece_count = (len(refs) - 1 - 2 * len(orders) - 4)
    pieces = refs[:piece_count]
    tiles = refs[piece_count]
    outs = refs[piece_count + 1 : piece_count + 1 + 2 * len(orders)]
    slab, acc, buf, sems = refs[-4:]
    count, row, col = meta[0], meta[1], meta[2]
    tile_size = tiles.shape[1]
    kc = pieces[0].shape[1]
    per_piece = pieces[0].shape[0] // tile_size

    def fetch(t):
        slot = lax.rem(t, SLOTS)
        return pltpu.make_async_copy(tiles.at[t], buf.at[slot], sems.at[slot])

    for t in range(SLOTS):
        @pl.when(t < count)
        def _():
            fetch(t).start()

    acc[...] = jnp.zeros_like(acc)
    for c in range(piece_count):
        for h in range(per_piece):
            block = pieces[c][h * tile_size : (h + 1) * tile_size, :].T
            high = block.astype(BF16)
            slab[c * per_piece + h, :kc, :] = high
            slab[c * per_piece + h, kc:, :] = (block - high.astype(F32)).astype(BF16)

    def step(t, _):
        user = users[t]
        which = lax.bitwise_xor(user // per_piece, col) * per_piece + lax.rem(user, per_piece)
        place = lax.bitwise_xor(owner[items[t]], row)
        fetch(t).wait()
        both = jnp.dot(slab[which], buf[lax.rem(t, SLOTS)], preferred_element_type=F32)
        acc[place] += both[:kc] + both[kc:]

        @pl.when(t + SLOTS < count)
        def _():
            fetch(t + SLOTS).start()

        return 0

    lax.fori_loop(0, count, step, 0)
    width = tile_size // len(orders)
    for o, order in enumerate(orders):
        cut = slice(o * width, (o + 1) * width)
        for k, place in enumerate(places(order, 0)):
            outs[2 * o][k] = acc[place, :, cut]
        for k, place in enumerate(places(order, 1)):
            outs[2 * o + 1][k] = acc[place, :, cut].astype(BF16)


def tile_sums(orders, row_count, users, items, owner, meta, pieces, tiles):
    kc = pieces[0].shape[1]
    tile_size = tiles.shape[1]
    width = tile_size // len(orders)
    half = row_count // 2
    shapes = []
    for _ in orders:
        shapes.append(jax.ShapeDtypeStruct((half, kc, width), F32))
        shapes.append(jax.ShapeDtypeStruct((half, kc, width), BF16))
    blocks = len(pieces) * pieces[0].shape[0] // tile_size
    smem = pl.BlockSpec(memory_space=pltpu.SMEM)
    vmem = pl.BlockSpec(memory_space=pltpu.VMEM)
    return pl.pallas_call(
        functools.partial(tile_kernel, orders),
        out_shape=shapes,
        in_specs=[smem] * 4 + [vmem] * len(pieces) + [pl.BlockSpec(memory_space=pl.ANY)],
        out_specs=[vmem] * len(shapes),
        scratch_shapes=[
            pltpu.VMEM((blocks, 2 * kc, tile_size), BF16),
            pltpu.VMEM((row_count, kc, tile_size), F32),
            pltpu.VMEM((SLOTS, tile_size, tile_size), BF16),
            pltpu.SemaphoreType.DMA((SLOTS,)),
        ],
        compiler_params=pltpu.CompilerParams(vmem_limit_bytes=48 * 2**20),
        cost_estimate=pl.CostEstimate(
            flops=20 * 4 * kc * tile_size**2, bytes_accessed=20 * 2 * tile_size**2, transcendentals=0
        ),
    )(users, items, owner, meta, *pieces, tiles)


def mm(a, b):
    return lax.dot_general(a, b, (((1,), (0,)), ((), ())), precision=HIGH, preferred_element_type=F32)


def mmt(a, b):
    return lax.dot_general(a, b, (((1,), (1,)), ((), ())), precision=HIGH, preferred_element_type=F32)


def factor_kernel(packed, inverse, check):
    n = packed.shape[1]
    r = lax.broadcasted_iota(jnp.int32, (n, n), 0)
    c = lax.broadcasted_iota(jnp.int32, (n, n), 1)
    mixed = packed[:n]
    flipped = mixed.T
    side = packed[n : 2 * n]
    tail = jnp.broadcast_to(packed[2 * n : 2 * n + 1], (n, n))
    first = jnp.where(r >= c, mixed, flipped)
    second = jnp.where(r < c, mixed, jnp.where(r > c, flipped, tail))
    gram = jnp.concatenate(
        [jnp.concatenate([first, side.T], axis=1), jnp.concatenate([side, second], axis=1)], axis=0
    )
    m = 2 * n
    rr = lax.broadcasted_iota(jnp.int32, (m, m), 0)
    cc = lax.broadcasted_iota(jnp.int32, (m, m), 1)
    on = rr == cc
    eye = jnp.where(on, 1.0, 0.0).astype(F32)
    low = jnp.where(rr > cc, 1.0, jnp.where(on, 0.5, 0.0)).astype(F32)
    diag = jnp.where(on, gram, 0.0)
    scale_row = lax.rsqrt(jnp.sum(diag, axis=0, keepdims=True))
    scale_col = lax.rsqrt(jnp.sum(diag, axis=1, keepdims=True))
    unit = gram * scale_row * scale_col
    off = unit - eye
    square = jnp.dot(off, off, preferred_element_type=F32)
    spread = jnp.max(jnp.sum(jnp.abs(jnp.dot(square, square, preferred_element_type=F32)), axis=1))
    w = eye - low * off
    for _ in range(NEWTON):
        err = mmt(mm(w, unit), w) - eye
        w = w - mm(low * err, w)
    last = jnp.max(jnp.sum(jnp.abs(err), axis=1))
    inflation = jnp.max(jnp.sum(w * w, axis=0))
    inverse[...] = w * scale_row
    check[0] = spread
    check[1] = last
    check[2] = inflation


def factor(packed):
    n = packed.shape[1]
    return pl.pallas_call(
        factor_kernel,
        out_shape=[jax.ShapeDtypeStruct((2 * n, 2 * n), F32), jax.ShapeDtypeStruct((3,), F32)],
        in_specs=[pl.BlockSpec(memory_space=pltpu.VMEM)],
        out_specs=[pl.BlockSpec(memory_space=pltpu.VMEM), pl.BlockSpec(memory_space=pltpu.SMEM)],
        compiler_params=pltpu.CompilerParams(vmem_limit_bytes=24 * 2**20),
        cost_estimate=pl.CostEstimate(
            flops=11 * 6 * 2 * 8 * n**3, bytes_accessed=6 * 4 * n * n, transcendentals=0
        ),
    )(packed)


def pack(gram):
    n = gram.shape[0] // 2
    r = lax.broadcasted_iota(jnp.int32, (n, n), 0)
    c = lax.broadcasted_iota(jnp.int32, (n, n), 1)
    mixed = jnp.where(r >= c, gram[:n, :n], gram[n:, n:])
    tail = jnp.sum(jnp.where(r == c, gram[n:, n:], 0.0), axis=0, keepdims=True)
    return jnp.concatenate([mixed, gram[n:, :n], jnp.broadcast_to(tail, (8, n))], axis=0)


def full_path(sketch, tiles, tile_user, tile_item, tile_count, item_owner, packed):
    n = packed.shape[1]
    r = lax.broadcasted_iota(jnp.int32, (n, n), 0)
    c = lax.broadcasted_iota(jnp.int32, (n, n), 1)
    mixed, side, tail = packed[:n], packed[n : 2 * n], packed[2 * n : 2 * n + 1]
    first = jnp.where(r >= c, mixed, mixed.T)
    second = jnp.where(r < c, mixed, jnp.where(r > c, mixed.T, tail))
    gram = jnp.block([[first, side.T], [side, second]])
    lower = jnp.linalg.cholesky(gram)
    basis = lax.linalg.triangular_solve(lower, sketch, left_side=False, lower=True, transpose_a=True).astype(BF16)
    slab = lax.all_gather(basis, "cols", axis=0, tiled=True)
    owner = item_owner[0]
    tile_size = tiles.shape[2]

    def step(index, sums):
        rows = lax.dynamic_slice_in_dim(slab, tile_user[index] * tile_size, tile_size, 0)
        part = lax.dot_general(rows, tiles[index], (((0,), (0,)), ((), ())), preferred_element_type=F32)
        place = owner[tile_item[index]]
        now = lax.dynamic_index_in_dim(sums, place, 0, keepdims=False)
        return lax.dynamic_update_index_in_dim(sums, now + part, place, 0)

    totals = jnp.zeros((owner.shape[0], sketch.shape[1], tile_size), F32)
    totals = lax.fori_loop(0, tile_count[0], step, totals)
    return lax.psum_scatter(totals, "rows", scatter_dimension=0, tiled=True)[0]


def body(rows, cols, sketch, tiles, tile_user, tile_item, tile_count, item_owner):
    width = sketch.shape[1]
    row_bits = rows.bit_length() - 1
    first_order = tuple(range(row_bits))
    orders = (first_order, (1, 0) + first_order[2:])
    row = lax.axis_index("rows")
    col = lax.axis_index("cols")
    meta = jnp.stack([tile_count[0], row, col]).astype(jnp.int32)
    owner = item_owner[0]

    kc = width // CHUNKS
    gathered = []
    for k in range(CHUNKS):
        pieces = [sketch[:, k * kc : (k + 1) * kc]]
        gathered.append(pieces)
    bits = []
    bit = cols // 2
    while bit:
        bits.append(bit)
        bit //= 2
    for k in range(CHUNKS):
        have = {0: gathered[k][0]}
        for bit in bits:
            for place in list(have):
                have[place | bit] = swap(have[place], "cols", cols, bit)
        gathered[k] = [have[i] for i in range(cols)]

    gram = lax.dot_general(
        sketch, sketch, (((0,), (0,)), ((), ())), precision=HIGH, preferred_element_type=F32
    )
    packed = pack(gram)
    for bit in reversed(bits):
        packed = packed + swap(packed, "cols", cols, bit)
    for b in range(row_bits):
        packed = packed + swap(packed, "rows", rows, 1 << b)
    inverse, check = factor(packed)

    halves = []
    for k in range(CHUNKS):
        outs = tile_sums(orders, rows, tile_user, tile_item, owner, meta, gathered[k], tiles)
        done = []
        for o, order in enumerate(orders):
            keep, send = outs[2 * o], outs[2 * o + 1]
            for pos, b in enumerate(order):
                got = swap(send, "rows", rows, 1 << b)
                total = keep + got.astype(F32)
                if pos + 1 < len(order):
                    half = total.shape[0] // 2
                    keep, send = total[:half], total[half:].astype(BF16)
            done.append(total[0])
        halves.append(jnp.concatenate(done, axis=1))
    sums = jnp.concatenate(halves, axis=0)
    good = (check[0] < 0.025) & (check[1] < 0.01) & (check[2] < 1.1)
    out = lax.cond(
        good,
        lambda: mm(inverse, sums),
        lambda: full_path(sketch, tiles, tile_user, tile_item, tile_count, item_owner, packed),
    )
    return out[None, None]


def solution(mesh):
    placed = (
        P(("rows", "cols"), None),
        P(("rows", "cols"), None, None),
        P(("rows", "cols")),
        P(("rows", "cols")),
        P(("rows", "cols")),
        P("cols", None),
    )
    return jax.shard_map(
        functools.partial(body, mesh.shape["rows"], mesh.shape["cols"]),
        mesh=mesh,
        in_specs=placed,
        out_specs=P("rows", "cols", None, None),
        check_vma=False,
    )
```

```python
import functools

import jax
import jax.numpy as jnp
from jax import lax
from jax.experimental import pallas as pl
from jax.experimental.pallas import tpu as pltpu
from jax.sharding import PartitionSpec as P

F32 = jnp.float32
BF16 = jnp.bfloat16
HIGH = lax.Precision.HIGHEST
SLOTS = 12
GROUP = 4
NEAR_COST = 200 * 2**20
FAR_COST = 200 * 2**20
CHUNKS = 2
NEWTON = 2


def bits_of(count):
    return [1 << b for b in reversed(range(count.bit_length() - 1))]


def swap(x, axis, count, bit):
    return lax.ppermute(x, axis, [(i, i ^ bit) for i in range(count)])


def places(order, parity):
    found = [parity << order[0]]
    for bit in reversed(order[1:]):
        found = found + [p | (1 << bit) for p in found]
    return found


def run_tiles(base, span, per_piece, users, items, owner, meta, tiles, slab, add, buf, sems, order):
    count, row, col = meta[0], meta[1], meta[2]

    def relative(t):
        user = users[t]
        return lax.bitwise_xor(user // per_piece, col) - base, lax.rem(user, per_piece)

    def choose(t, n):
        piece, _ = relative(t)
        order[n] = t
        return n + jnp.where((piece >= 0) & (piece < span), 1, 0)

    live = lax.fori_loop(0, count, choose, 0)

    def fetch(i):
        slot = lax.rem(i, SLOTS)
        return pltpu.make_async_copy(tiles.at[order[i]], buf.at[slot], sems.at[slot])

    for i in range(SLOTS):
        @pl.when(i < live)
        def _():
            fetch(i).start()

    def group(first, size):
        for q in range(size):
            fetch(first + q).wait()
        found = []
        for q in range(size):
            piece, part = relative(order[first + q])
            both = jnp.dot(
                slab[piece * per_piece + part],
                buf[lax.rem(first + q, SLOTS)],
                preferred_element_type=F32,
            )
            half = both.shape[0] // 2
            found.append(both[:half] + both[half:])
        for q in range(size):
            add(lax.bitwise_xor(owner[items[order[first + q]]], row), found[q])
        for q in range(size):
            @pl.when(first + q + SLOTS < live)
            def _():
                fetch(first + q + SLOTS).start()

    def finish():
        groups = live // GROUP

        def many(g, _):
            group(g * GROUP, GROUP)
            return 0

        def one(i, _):
            group(i, 1)
            return 0

        lax.fori_loop(0, groups, many, 0)
        lax.fori_loop(groups * GROUP, live, one, 0)

    return finish


def fill(slab, pieces, per_piece):
    tile_size = slab.shape[2]
    kc = slab.shape[1] // 2
    for c, piece in enumerate(pieces):
        for h in range(per_piece):
            block = piece[h * tile_size : (h + 1) * tile_size, :].T
            high = block.astype(BF16)
            slab[c * per_piece + h, :kc, :] = high
            slab[c * per_piece + h, kc:, :] = (block - high.astype(F32)).astype(BF16)


def near_kernel(span, users, items, owner, meta, *refs):
    pieces = refs[:span]
    tiles = refs[span]
    sums = refs[span + 1 : -4]
    slab, buf, sems, order = refs[-4:]
    per_piece = pieces[0].shape[0] // tiles.shape[1]
    kc = sums[0].shape[1]

    def add(place, value):
        for k, part in enumerate(sums):
            part[place] += value[k * kc : (k + 1) * kc]

    finish = run_tiles(
        0, span, per_piece, users, items, owner, meta, tiles, slab, add, buf, sems, order
    )
    for part in sums:
        part[...] = jnp.zeros_like(part)
    fill(slab, pieces, per_piece)
    finish()


def far_kernel(span, orders, users, items, owner, meta, *refs):
    pieces = refs[:span]
    start, tiles = refs[span], refs[span + 1]
    outs = refs[span + 2 : -5]
    slab, buf, sems, order, acc = refs[-5:]
    tile_size = tiles.shape[1]
    per_piece = pieces[0].shape[0] // tile_size

    def add(place, value):
        acc[place] += value

    finish = run_tiles(
        span, span, per_piece, users, items, owner, meta, tiles, slab, add, buf, sems, order
    )
    acc[...] = start[...]
    fill(slab, pieces, per_piece)
    finish()
    width = tile_size // len(orders)
    for o, bits in enumerate(orders):
        cut = slice(o * width, (o + 1) * width)
        for k, place in enumerate(places(bits, 0)):
            outs[2 * o][k] = acc[place, :, cut]
        for k, place in enumerate(places(bits, 1)):
            outs[2 * o + 1][k] = acc[place, :, cut].astype(BF16)


def tile_call(kernel, scalars, pieces, extra, tiles, shapes, scratch, seconds):
    users = scalars[0].shape[0]
    tile_size = tiles.shape[1]
    blocks = len(pieces) * pieces[0].shape[0] // tile_size
    smem = pl.BlockSpec(memory_space=pltpu.SMEM)
    vmem = pl.BlockSpec(memory_space=pltpu.VMEM)
    return pl.pallas_call(
        kernel,
        out_shape=shapes,
        in_specs=[smem] * len(scalars)
        + [vmem] * (len(pieces) + len(extra))
        + [pl.BlockSpec(memory_space=pl.ANY)],
        out_specs=[vmem] * len(shapes),
        scratch_shapes=[
            pltpu.VMEM((blocks, 2 * pieces[0].shape[1], tile_size), BF16),
            pltpu.VMEM((SLOTS, tile_size, tile_size), BF16),
            pltpu.SemaphoreType.DMA((SLOTS,)),
            pltpu.SMEM((users,), jnp.int32),
        ]
        + scratch,
        compiler_params=pltpu.CompilerParams(vmem_limit_bytes=32 * 2**20),
        cost_estimate=pl.CostEstimate(
            flops=0, bytes_accessed=seconds, transcendentals=0
        ),
    )(*scalars, *pieces, *extra, tiles)


def near_sums(scalars, pieces, tiles, rows):
    tile_size = tiles.shape[1]
    kc = pieces[0].shape[1] // CHUNKS
    shapes = [jax.ShapeDtypeStruct((rows, kc, tile_size), F32)] * CHUNKS
    return tile_call(
        functools.partial(near_kernel, len(pieces)), scalars, pieces, [], tiles, shapes, [], NEAR_COST
    )


def far_sums(scalars, pieces, start, tiles, orders):
    rows, kc, tile_size = start.shape
    width = tile_size // len(orders)
    shapes = []
    for _ in orders:
        shapes.append(jax.ShapeDtypeStruct((rows // 2, kc, width), F32))
        shapes.append(jax.ShapeDtypeStruct((rows // 2, kc, width), BF16))
    return tile_call(
        functools.partial(far_kernel, len(pieces), orders),
        scalars,
        pieces,
        [start],
        tiles,
        shapes,
        [pltpu.VMEM(start.shape, F32)],
        FAR_COST,
    )


def mm(a, b):
    return lax.dot_general(a, b, (((1,), (0,)), ((), ())), precision=HIGH, preferred_element_type=F32)


def mmt(a, b):
    return lax.dot_general(a, b, (((1,), (1,)), ((), ())), precision=HIGH, preferred_element_type=F32)


def factor_kernel(packed, inverse, check):
    n = packed.shape[1]
    r = lax.broadcasted_iota(jnp.int32, (n, n), 0)
    c = lax.broadcasted_iota(jnp.int32, (n, n), 1)
    mixed = packed[:n]
    flipped = mixed.T
    side = packed[n : 2 * n]
    tail = jnp.broadcast_to(packed[2 * n : 2 * n + 1], (n, n))
    first = jnp.where(r >= c, mixed, flipped)
    second = jnp.where(r < c, mixed, jnp.where(r > c, flipped, tail))
    gram = jnp.concatenate(
        [jnp.concatenate([first, side.T], axis=1), jnp.concatenate([side, second], axis=1)], axis=0
    )
    m = 2 * n
    rr = lax.broadcasted_iota(jnp.int32, (m, m), 0)
    cc = lax.broadcasted_iota(jnp.int32, (m, m), 1)
    on = rr == cc
    eye = jnp.where(on, 1.0, 0.0).astype(F32)
    low = jnp.where(rr > cc, 1.0, jnp.where(on, 0.5, 0.0)).astype(F32)
    diag = jnp.where(on, gram, 0.0)
    scale_row = lax.rsqrt(jnp.sum(diag, axis=0, keepdims=True))
    scale_col = lax.rsqrt(jnp.sum(diag, axis=1, keepdims=True))
    unit = gram * scale_row * scale_col
    off = unit - eye
    square = jnp.dot(off, off, preferred_element_type=F32)
    spread = jnp.max(jnp.sum(jnp.abs(jnp.dot(square, square, preferred_element_type=F32)), axis=1))
    w = eye - low * off
    for _ in range(NEWTON):
        err = mmt(mm(w, unit), w) - eye
        w = w - mm(low * err, w)
    last = jnp.max(jnp.sum(jnp.abs(err), axis=1))
    inflation = jnp.max(jnp.sum(w * w, axis=0))
    inverse[...] = w * scale_row
    check[0] = spread
    check[1] = last
    check[2] = inflation


def factor(packed):
    n = packed.shape[1]
    return pl.pallas_call(
        factor_kernel,
        out_shape=[jax.ShapeDtypeStruct((2 * n, 2 * n), F32), jax.ShapeDtypeStruct((3,), F32)],
        in_specs=[pl.BlockSpec(memory_space=pltpu.VMEM)],
        out_specs=[pl.BlockSpec(memory_space=pltpu.VMEM), pl.BlockSpec(memory_space=pltpu.SMEM)],
        compiler_params=pltpu.CompilerParams(vmem_limit_bytes=24 * 2**20),
        cost_estimate=pl.CostEstimate(
            flops=11 * 6 * 2 * 8 * n**3, bytes_accessed=6 * 4 * n * n, transcendentals=0
        ),
    )(packed)


def pack(gram):
    n = gram.shape[0] // 2
    r = lax.broadcasted_iota(jnp.int32, (n, n), 0)
    c = lax.broadcasted_iota(jnp.int32, (n, n), 1)
    mixed = jnp.where(r >= c, gram[:n, :n], gram[n:, n:])
    tail = jnp.sum(jnp.where(r == c, gram[n:, n:], 0.0), axis=0, keepdims=True)
    return jnp.concatenate([mixed, gram[n:, :n], jnp.broadcast_to(tail, (8, n))], axis=0)


def full_path(rows, cols, sketch, tiles, tile_user, tile_item, tile_count, item_owner, packed):
    n = packed.shape[1]
    r = lax.broadcasted_iota(jnp.int32, (n, n), 0)
    c = lax.broadcasted_iota(jnp.int32, (n, n), 1)
    mixed, side, tail = packed[:n], packed[n : 2 * n], packed[2 * n : 2 * n + 1]
    first = jnp.where(r >= c, mixed, mixed.T)
    second = jnp.where(r < c, mixed, jnp.where(r > c, mixed.T, tail))
    gram = jnp.block([[first, side.T], [side, second]])
    lower = jnp.linalg.cholesky(gram)
    basis = lax.linalg.triangular_solve(lower, sketch, left_side=False, lower=True, transpose_a=True).astype(BF16)
    have = {0: basis}
    for bit in bits_of(cols):
        for place in list(have):
            have[place | bit] = swap(have[place], "cols", cols, bit)
    slab = jnp.concatenate([have[i] for i in range(cols)], axis=0)
    col = lax.axis_index("cols")
    row = lax.axis_index("rows")
    per_piece = sketch.shape[0] // tiles.shape[2]
    owner = item_owner[0]
    tile_size = tiles.shape[2]

    def step(index, sums):
        user = tile_user[index]
        block = lax.bitwise_xor(user // per_piece, col) * per_piece + user % per_piece
        part_rows = lax.dynamic_slice_in_dim(slab, block * tile_size, tile_size, 0)
        part = lax.dot_general(part_rows, tiles[index], (((0,), (0,)), ((), ())), preferred_element_type=F32)
        place = lax.bitwise_xor(owner[tile_item[index]], row)
        now = lax.dynamic_index_in_dim(sums, place, 0, keepdims=False)
        return lax.dynamic_update_index_in_dim(sums, now + part, place, 0)

    totals = jnp.zeros((owner.shape[0], sketch.shape[1], tile_size), F32)
    totals = lax.fori_loop(0, tile_count[0], step, totals)
    for bit in bits_of(rows):
        totals = totals[:bit] + swap(totals[bit:], "rows", rows, bit)
    return totals[0]


def exchange(keep, send, bit, rows):
    return keep + swap(send, "rows", rows, 1 << bit).astype(F32)


def firsts(outs, orders, rows):
    return [exchange(outs[2 * o], outs[2 * o + 1], order[0], rows) for o, order in enumerate(orders)]


def split(total):
    half = total.shape[0] // 2
    return total[:half], total[half:].astype(BF16)


def body(rows, cols, sketch, tiles, tile_user, tile_item, tile_count, item_owner):
    width = sketch.shape[1]
    row_bits = rows.bit_length() - 1
    first_order = tuple(range(row_bits))
    orders = (first_order, (1, 0) + first_order[2:])
    row = lax.axis_index("rows")
    col = lax.axis_index("cols")
    meta = jnp.stack([tile_count[0], row, col]).astype(jnp.int32)
    scalars = (tile_user, tile_item, item_owner[0], meta)
    kc = width // CHUNKS
    far_bit, *near_bits = bits_of(cols)

    def spread(piece):
        have = {0: piece}
        for bit in near_bits:
            for place in list(have):
                have[place | bit] = swap(have[place], "cols", cols, bit)
        return [have[i] for i in range(cols // 2)]

    fence = lax.optimization_barrier
    crossed = [swap(sketch[:, k * kc : (k + 1) * kc], "cols", cols, far_bit) for k in range(CHUNKS)]
    near = spread(sketch)
    gram = lax.dot_general(
        sketch, sketch, (((0,), (0,)), ((), ())), precision=HIGH, preferred_element_type=F32
    )
    packed = pack(gram)
    for bit in near_bits:
        packed = packed + swap(packed, "cols", cols, bit)
    got = swap(packed, "rows", rows, 1)
    sums = near_sums(scalars, near, tiles, rows)
    crossed[0], packed, got, *sums = fence((crossed[0], packed, got, *sums))
    packed = packed + got
    got = swap(packed, "rows", rows, 2)
    outs = far_sums(scalars, spread(crossed[0]), sums[0], tiles, orders)
    crossed[1], packed, got, *outs = fence((crossed[1], packed, got, *outs))
    packed = packed + got
    got = swap(packed, "rows", rows, 4)
    totals = firsts(outs, orders, rows)
    crossed[1], *totals = fence((crossed[1], *totals))
    halves = [split(t) for t in totals]
    came = [swap(h[1], "rows", rows, 1 << order[1]) for h, order in zip(halves, orders)]
    outs = far_sums(scalars, spread(crossed[1]), sums[1], tiles, orders)
    packed, got, *rest = fence((packed, got, *outs, *[h[0] for h in halves]))
    outs, keeps = rest[: len(outs)], rest[len(outs) :]
    packed = packed + got
    packed = packed + swap(packed, "cols", cols, far_bit)
    for b in range(3, row_bits):
        packed = packed + swap(packed, "rows", rows, 1 << b)
    inverse, check = factor(packed)
    early = [keep + c.astype(F32) for keep, c in zip(keeps, came)]
    late = [exchange(*split(t), order[1], rows) for t, order in zip(firsts(outs, orders, rows), orders)]
    done = []
    for pair in (early, late):
        for pos in range(2, row_bits):
            pair = [exchange(*split(t), order[pos], rows) for t, order in zip(pair, orders)]
        done.append(jnp.concatenate([t[0] for t in pair], axis=1))
    total = jnp.concatenate(done, axis=0)
    good = (check[0] < 0.025) & (check[1] < 0.01) & (check[2] < 1.1)
    out = lax.cond(
        good,
        lambda: mm(inverse, total),
        lambda: full_path(rows, cols, sketch, tiles, tile_user, tile_item, tile_count, item_owner, packed),
    )
    return out[None, None]


def solution(mesh):
    placed = (
        P(("rows", "cols"), None),
        P(("rows", "cols"), None, None),
        P(("rows", "cols")),
        P(("rows", "cols")),
        P(("rows", "cols")),
        P("cols", None),
    )
    return jax.shard_map(
        functools.partial(body, mesh.shape["rows"], mesh.shape["cols"]),
        mesh=mesh,
        in_specs=placed,
        out_specs=P("rows", "cols", None, None),
        check_vma=False,
    )
```

```python
import functools

import jax
import jax.numpy as jnp
from jax import lax
from jax.experimental import pallas as pl
from jax.experimental.pallas import tpu as pltpu
from jax.sharding import PartitionSpec as P

F32 = jnp.float32
BF16 = jnp.bfloat16
HIGH = lax.Precision.HIGHEST
SLOTS = 12
GROUP = 4
NEAR_COST = 200 * 2**20
EARLY_COST = 1024
LATE_COST = 200 * 2**20
CHUNKS = 2
NEWTON = 2


def bits_of(count):
    return [1 << b for b in reversed(range(count.bit_length() - 1))]


def swap(x, axis, count, bit):
    return lax.ppermute(x, axis, [(i, i ^ bit) for i in range(count)])


def places(order, parity):
    found = [parity << order[0]]
    for bit in reversed(order[1:]):
        found = found + [p | (1 << bit) for p in found]
    return found


def run_tiles(base, span, per_piece, users, items, owner, meta, tiles, slab, add, buf, sems, order):
    count, row, col = meta[0], meta[1], meta[2]

    def relative(t):
        user = users[t]
        return lax.bitwise_xor(user // per_piece, col) - base, lax.rem(user, per_piece)

    def choose(t, n):
        piece, _ = relative(t)
        order[n] = t
        return n + jnp.where((piece >= 0) & (piece < span), 1, 0)

    live = lax.fori_loop(0, count, choose, 0)

    def fetch(i):
        slot = lax.rem(i, SLOTS)
        return pltpu.make_async_copy(tiles.at[order[i]], buf.at[slot], sems.at[slot])

    for i in range(SLOTS):
        @pl.when(i < live)
        def _():
            fetch(i).start()

    def group(first, size):
        for q in range(size):
            fetch(first + q).wait()
        found = []
        for q in range(size):
            piece, part = relative(order[first + q])
            both = jnp.dot(
                slab[piece * per_piece + part],
                buf[lax.rem(first + q, SLOTS)],
                preferred_element_type=F32,
            )
            half = both.shape[0] // 2
            found.append(both[:half] + both[half:])
        for q in range(size):
            add(lax.bitwise_xor(owner[items[order[first + q]]], row), found[q])
        for q in range(size):
            @pl.when(first + q + SLOTS < live)
            def _():
                fetch(first + q + SLOTS).start()

    def finish():
        groups = live // GROUP

        def many(g, _):
            group(g * GROUP, GROUP)
            return 0

        def one(i, _):
            group(i, 1)
            return 0

        lax.fori_loop(0, groups, many, 0)
        lax.fori_loop(groups * GROUP, live, one, 0)

    return finish


def fill(slab, pieces, per_piece):
    tile_size = slab.shape[2]
    kc = slab.shape[1] // 2
    for c, piece in enumerate(pieces):
        for h in range(per_piece):
            block = piece[h * tile_size : (h + 1) * tile_size, :].T
            high = block.astype(BF16)
            slab[c * per_piece + h, :kc, :] = high
            slab[c * per_piece + h, kc:, :] = (block - high.astype(F32)).astype(BF16)


def near_kernel(span, users, items, owner, meta, *refs):
    pieces = refs[:span]
    tiles = refs[span]
    sums = refs[span + 1 : -4]
    slab, buf, sems, order = refs[-4:]
    per_piece = pieces[0].shape[0] // tiles.shape[1]
    kc = sums[0].shape[1]

    def add(place, value):
        for k, part in enumerate(sums):
            part[place] += value[k * kc : (k + 1) * kc]

    finish = run_tiles(
        0, span, per_piece, users, items, owner, meta, tiles, slab, add, buf, sems, order
    )
    for part in sums:
        part[...] = jnp.zeros_like(part)
    fill(slab, pieces, per_piece)
    finish()


def far_kernel(span, orders, users, items, owner, meta, *refs):
    pieces = refs[:span]
    start, tiles = refs[span], refs[span + 1]
    outs = refs[span + 2 : -5]
    slab, buf, sems, order, acc = refs[-5:]
    tile_size = tiles.shape[1]
    per_piece = pieces[0].shape[0] // tile_size

    def add(place, value):
        acc[place] += value

    finish = run_tiles(
        span, span, per_piece, users, items, owner, meta, tiles, slab, add, buf, sems, order
    )
    acc[...] = start[...]
    fill(slab, pieces, per_piece)
    finish()
    width = tile_size // len(orders)
    for o, bits in enumerate(orders):
        cut = slice(o * width, (o + 1) * width)
        for k, place in enumerate(places(bits, 0)):
            outs[2 * o][k] = acc[place, :, cut]
        for k, place in enumerate(places(bits, 1)):
            outs[2 * o + 1][k] = acc[place, :, cut].astype(BF16)


def tile_call(kernel, scalars, pieces, extra, tiles, shapes, scratch, seconds):
    users = scalars[0].shape[0]
    tile_size = tiles.shape[1]
    blocks = len(pieces) * pieces[0].shape[0] // tile_size
    smem = pl.BlockSpec(memory_space=pltpu.SMEM)
    vmem = pl.BlockSpec(memory_space=pltpu.VMEM)
    return pl.pallas_call(
        kernel,
        out_shape=shapes,
        in_specs=[smem] * len(scalars)
        + [vmem] * (len(pieces) + len(extra))
        + [pl.BlockSpec(memory_space=pl.ANY)],
        out_specs=[vmem] * len(shapes),
        scratch_shapes=[
            pltpu.VMEM((blocks, 2 * pieces[0].shape[1], tile_size), BF16),
            pltpu.VMEM((SLOTS, tile_size, tile_size), BF16),
            pltpu.SemaphoreType.DMA((SLOTS,)),
            pltpu.SMEM((users,), jnp.int32),
        ]
        + scratch,
        compiler_params=pltpu.CompilerParams(vmem_limit_bytes=32 * 2**20),
        cost_estimate=pl.CostEstimate(
            flops=0, bytes_accessed=seconds, transcendentals=0
        ),
    )(*scalars, *pieces, *extra, tiles)


def near_sums(scalars, pieces, tiles, rows):
    tile_size = tiles.shape[1]
    kc = pieces[0].shape[1] // CHUNKS
    shapes = [jax.ShapeDtypeStruct((rows, kc, tile_size), F32)] * CHUNKS
    return tile_call(
        functools.partial(near_kernel, len(pieces)), scalars, pieces, [], tiles, shapes, [], NEAR_COST
    )


def far_sums(scalars, pieces, start, tiles, orders, cost):
    rows, kc, tile_size = start.shape
    width = tile_size // len(orders)
    shapes = []
    for _ in orders:
        shapes.append(jax.ShapeDtypeStruct((rows // 2, kc, width), F32))
        shapes.append(jax.ShapeDtypeStruct((rows // 2, kc, width), BF16))
    return tile_call(
        functools.partial(far_kernel, len(pieces), orders),
        scalars,
        pieces,
        [start],
        tiles,
        shapes,
        [pltpu.VMEM(start.shape, F32)],
        cost,
    )


def mm(a, b):
    return lax.dot_general(a, b, (((1,), (0,)), ((), ())), precision=HIGH, preferred_element_type=F32)


def mmt(a, b):
    return lax.dot_general(a, b, (((1,), (1,)), ((), ())), precision=HIGH, preferred_element_type=F32)


def factor_kernel(packed, inverse, good):
    n = packed.shape[1]
    r = lax.broadcasted_iota(jnp.int32, (n, n), 0)
    c = lax.broadcasted_iota(jnp.int32, (n, n), 1)
    mixed = packed[:n]
    flipped = mixed.T
    side = packed[n : 2 * n]
    tail = jnp.broadcast_to(packed[2 * n : 2 * n + 1], (n, n))
    first = jnp.where(r >= c, mixed, flipped)
    second = jnp.where(r < c, mixed, jnp.where(r > c, flipped, tail))
    gram = jnp.concatenate(
        [jnp.concatenate([first, side.T], axis=1), jnp.concatenate([side, second], axis=1)], axis=0
    )
    m = 2 * n
    rr = lax.broadcasted_iota(jnp.int32, (m, m), 0)
    cc = lax.broadcasted_iota(jnp.int32, (m, m), 1)
    on = rr == cc
    eye = jnp.where(on, 1.0, 0.0).astype(F32)
    low = jnp.where(rr > cc, 1.0, jnp.where(on, 0.5, 0.0)).astype(F32)
    diag = jnp.where(on, gram, 0.0)
    scale_row = lax.rsqrt(jnp.sum(diag, axis=0, keepdims=True))
    scale_col = lax.rsqrt(jnp.sum(diag, axis=1, keepdims=True))
    unit = gram * scale_row * scale_col
    off = unit - eye
    square = jnp.dot(off, off, preferred_element_type=F32)
    spread = jnp.max(jnp.sum(jnp.abs(jnp.dot(square, square, preferred_element_type=F32)), axis=1))
    w = eye - low * off
    for _ in range(NEWTON):
        err = mmt(mm(w, unit), w) - eye
        w = w - mm(low * err, w)
    last = jnp.max(jnp.sum(jnp.abs(err), axis=1))
    inflation = jnp.max(jnp.sum(w * w, axis=0))
    inverse[...] = w * scale_row
    good[0] = jnp.where((spread < 0.025) & (last < 0.01) & (inflation < 1.1), 1, 0)


def factor(packed):
    n = packed.shape[1]
    return pl.pallas_call(
        factor_kernel,
        out_shape=[jax.ShapeDtypeStruct((2 * n, 2 * n), F32), jax.ShapeDtypeStruct((1,), jnp.int32)],
        in_specs=[pl.BlockSpec(memory_space=pltpu.VMEM)],
        out_specs=[pl.BlockSpec(memory_space=pltpu.VMEM), pl.BlockSpec(memory_space=pltpu.SMEM)],
        compiler_params=pltpu.CompilerParams(vmem_limit_bytes=24 * 2**20),
        cost_estimate=pl.CostEstimate(
            flops=11 * 6 * 2 * 8 * n**3, bytes_accessed=6 * 4 * n * n, transcendentals=0
        ),
    )(packed)


def pack(gram):
    n = gram.shape[0] // 2
    r = lax.broadcasted_iota(jnp.int32, (n, n), 0)
    c = lax.broadcasted_iota(jnp.int32, (n, n), 1)
    mixed = jnp.where(r >= c, gram[:n, :n], gram[n:, n:])
    tail = jnp.sum(jnp.where(r == c, gram[n:, n:], 0.0), axis=0, keepdims=True)
    return jnp.concatenate([mixed, gram[n:, :n], jnp.broadcast_to(tail, (8, n))], axis=0)


def full_path(rows, cols, sketch, tiles, tile_user, tile_item, tile_count, item_owner, packed):
    n = packed.shape[1]
    r = lax.broadcasted_iota(jnp.int32, (n, n), 0)
    c = lax.broadcasted_iota(jnp.int32, (n, n), 1)
    mixed, side, tail = packed[:n], packed[n : 2 * n], packed[2 * n : 2 * n + 1]
    first = jnp.where(r >= c, mixed, mixed.T)
    second = jnp.where(r < c, mixed, jnp.where(r > c, mixed.T, tail))
    gram = jnp.block([[first, side.T], [side, second]])
    lower = jnp.linalg.cholesky(gram)
    basis = lax.linalg.triangular_solve(lower, sketch, left_side=False, lower=True, transpose_a=True).astype(BF16)
    have = {0: basis}
    for bit in bits_of(cols):
        for place in list(have):
            have[place | bit] = swap(have[place], "cols", cols, bit)
    slab = jnp.concatenate([have[i] for i in range(cols)], axis=0)
    col = lax.axis_index("cols")
    row = lax.axis_index("rows")
    per_piece = sketch.shape[0] // tiles.shape[2]
    owner = item_owner[0]
    tile_size = tiles.shape[2]

    def step(index, sums):
        user = tile_user[index]
        block = lax.bitwise_xor(user // per_piece, col) * per_piece + user % per_piece
        part_rows = lax.dynamic_slice_in_dim(slab, block * tile_size, tile_size, 0)
        part = lax.dot_general(part_rows, tiles[index], (((0,), (0,)), ((), ())), preferred_element_type=F32)
        place = lax.bitwise_xor(owner[tile_item[index]], row)
        now = lax.dynamic_index_in_dim(sums, place, 0, keepdims=False)
        return lax.dynamic_update_index_in_dim(sums, now + part, place, 0)

    totals = jnp.zeros((owner.shape[0], sketch.shape[1], tile_size), F32)
    totals = lax.fori_loop(0, tile_count[0], step, totals)
    for bit in bits_of(rows):
        totals = totals[:bit] + swap(totals[bit:], "rows", rows, bit)
    return totals[0]


def after(value, *others):
    return lax.optimization_barrier((value, *others))[0]


def exchange(lanes, rows):
    got = [None] * len(lanes)
    for bit in sorted({lane[2] for lane in lanes}):
        members = [i for i, lane in enumerate(lanes) if lane[2] == bit]
        came = swap(jnp.concatenate([lanes[i][1] for i in members], axis=0), "rows", rows, 1 << bit)
        first = 0
        for i in members:
            last = first + lanes[i][1].shape[0]
            got[i] = came[first:last]
            first = last
    return got


def split(total):
    half = total.shape[0] // 2
    return total[:half], total[half:].astype(BF16)


def body(rows, cols, sketch, tiles, tile_user, tile_item, tile_count, item_owner):
    width = sketch.shape[1]
    row_bits = rows.bit_length() - 1
    first_order = tuple(range(row_bits))
    orders = (first_order, (1, 0) + first_order[2:])
    row = lax.axis_index("rows")
    col = lax.axis_index("cols")
    meta = jnp.stack([tile_count[0], row, col]).astype(jnp.int32)
    scalars = (tile_user, tile_item, item_owner[0], meta)
    kc = width // CHUNKS
    far_bit, *near_bits = bits_of(cols)

    def spread(piece):
        have = {0: piece}
        for bit in near_bits:
            for place in list(have):
                have[place | bit] = swap(have[place], "cols", cols, bit)
        return [have[i] for i in range(cols // 2)]

    fence = lax.optimization_barrier
    far = far_bit
    crossed = [swap(sketch[:, :kc], "cols", cols, far)]
    near = spread(sketch)
    crossed.append(swap(after(sketch, near[-1])[:, kc:], "cols", cols, far))
    sums = near_sums(scalars, near, tiles, rows)
    crossed[0] = after(crossed[0], sums[0])
    outs = far_sums(scalars, spread(crossed[0]), sums[0], tiles, orders, EARLY_COST)
    lanes = [(outs[2 * o], outs[2 * o + 1], order[0]) for o, order in enumerate(orders)]
    got = exchange(lanes, rows)

    source = after(sketch, outs[1])
    gram = lax.dot_general(
        source, source, (((0,), (0,)), ((), ())), precision=HIGH, preferred_element_type=F32
    )
    packed = pack(gram)
    for bit in near_bits:
        packed = packed + swap(packed, "cols", cols, bit)
    came = swap(packed, "rows", rows, 1)
    crossed[1] = after(crossed[1], packed)
    later = far_sums(scalars, spread(crossed[1]), sums[1], tiles, orders, LATE_COST)
    packed, came, *rest = fence((packed, came, *got, *later))
    got, later = rest[: len(got)], rest[len(got) :]
    packed = packed + came
    stages = [("rows", 1 << b) for b in range(1, row_bits)] + [("cols", far)]

    totals = [lane[0] + g.astype(F32) for lane, g in zip(lanes, got)]
    late = [(later[2 * o], later[2 * o + 1]) for o in range(len(orders))]
    done = []
    inverse = None
    for step in range(1, row_bits + 1):
        lanes = []
        if step < row_bits:
            lanes += [(*split(t), order[step]) for t, order in zip(totals, orders)]
        lanes += [(*pair, order[step - 1]) for pair, order in zip(late, orders)]
        got = exchange(lanes, rows)
        ready = False
        for _ in range(2 if step == 1 else 1):
            if stages:
                axis, bit = stages.pop(0)
                packed = packed + swap(packed, axis, rows if axis == "rows" else cols, bit)
                ready = not stages
        if ready or step < row_bits:
            packed, *got = fence((packed, *got))
        new = [lane[0] + g.astype(F32) for lane, g in zip(lanes, got)]
        if step < row_bits:
            totals, new = new[: len(orders)], new[len(orders) :]
            if step == row_bits - 1:
                done.append(jnp.concatenate([t[0] for t in totals], axis=1))
        if step == row_bits:
            done.append(jnp.concatenate([t[0] for t in new], axis=1))
        else:
            late = [split(t) for t in new]
        if ready:
            inverse, good = factor(packed)
    head = mm(inverse[:, :kc], done[0])
    out = lax.cond(
        good[0] > 0,
        lambda: jnp.concatenate([head[:kc], head[kc:] + mm(inverse[kc:, kc:], done[1])], axis=0),
        lambda: full_path(rows, cols, sketch, tiles, tile_user, tile_item, tile_count, item_owner, packed),
    )
    return out[None, None]


def solution(mesh):
    placed = (
        P(("rows", "cols"), None),
        P(("rows", "cols"), None, None),
        P(("rows", "cols")),
        P(("rows", "cols")),
        P(("rows", "cols")),
        P("cols", None),
    )
    return jax.shard_map(
        functools.partial(body, mesh.shape["rows"], mesh.shape["cols"]),
        mesh=mesh,
        in_specs=placed,
        out_specs=P("rows", "cols", None, None),
        check_vma=False,
    )
```

```python
import functools

import jax
import jax.numpy as jnp
from jax import lax
from jax.experimental import pallas as pl
from jax.experimental.pallas import tpu as pltpu
from jax.sharding import PartitionSpec as P

F32 = jnp.float32
BF16 = jnp.bfloat16
HIGH = lax.Precision.HIGHEST
SLOTS = 12
GROUP = 4
NEAR_COST = 200 * 2**20
EARLY_COST = 1024
LATE_COST = 200 * 2**20
CHUNKS = 2
NEWTON = 2


def bits_of(count):
    return [1 << b for b in reversed(range(count.bit_length() - 1))]


def swap(x, axis, count, bit):
    return lax.ppermute(x, axis, [(i, i ^ bit) for i in range(count)])


def places(order, parity):
    found = [parity << order[0]]
    for bit in reversed(order[1:]):
        found = found + [p | (1 << bit) for p in found]
    return found


def run_tiles(base, span, per_piece, users, items, owner, meta, tiles, slab, add, buf, sems, order):
    count, row, col = meta[0], meta[1], meta[2]

    def relative(t):
        user = users[t]
        return lax.bitwise_xor(user // per_piece, col) - base, lax.rem(user, per_piece)

    def choose(t, n):
        piece, _ = relative(t)
        order[n] = t
        return n + jnp.where((piece >= 0) & (piece < span), 1, 0)

    live = lax.fori_loop(0, count, choose, 0)

    def fetch(i):
        slot = lax.rem(i, SLOTS)
        return pltpu.make_async_copy(tiles.at[order[i]], buf.at[slot], sems.at[slot])

    for i in range(SLOTS):
        @pl.when(i < live)
        def _():
            fetch(i).start()

    def group(first, size):
        for q in range(size):
            fetch(first + q).wait()
        found = []
        for q in range(size):
            piece, part = relative(order[first + q])
            both = jnp.dot(
                slab[piece * per_piece + part],
                buf[lax.rem(first + q, SLOTS)],
                preferred_element_type=F32,
            )
            half = both.shape[0] // 2
            found.append(both[:half] + both[half:])
        for q in range(size):
            add(lax.bitwise_xor(owner[items[order[first + q]]], row), found[q])
        for q in range(size):
            @pl.when(first + q + SLOTS < live)
            def _():
                fetch(first + q + SLOTS).start()

    def finish():
        groups = live // GROUP

        def many(g, _):
            group(g * GROUP, GROUP)
            return 0

        def one(i, _):
            group(i, 1)
            return 0

        lax.fori_loop(0, groups, many, 0)
        lax.fori_loop(groups * GROUP, live, one, 0)

    return finish


def fill(slab, pieces, per_piece):
    tile_size = slab.shape[2]
    kc = slab.shape[1] // 2
    for c, piece in enumerate(pieces):
        for h in range(per_piece):
            block = piece[h * tile_size : (h + 1) * tile_size, :].T
            high = block.astype(BF16)
            slab[c * per_piece + h, :kc, :] = high
            slab[c * per_piece + h, kc:, :] = (block - high.astype(F32)).astype(BF16)


def near_kernel(span, users, items, owner, meta, *refs):
    pieces = refs[:span]
    tiles = refs[span]
    sums = refs[span + 1 : -4]
    slab, buf, sems, order = refs[-4:]
    per_piece = pieces[0].shape[0] // tiles.shape[1]
    kc = sums[0].shape[1]

    def add(place, value):
        for k, part in enumerate(sums):
            part[place] += value[k * kc : (k + 1) * kc]

    finish = run_tiles(
        0, span, per_piece, users, items, owner, meta, tiles, slab, add, buf, sems, order
    )
    for part in sums:
        part[...] = jnp.zeros_like(part)
    fill(slab, pieces, per_piece)
    finish()


def far_kernel(span, orders, users, items, owner, meta, *refs):
    pieces = refs[:span]
    start, tiles = refs[span], refs[span + 1]
    outs = refs[span + 2 : -5]
    slab, buf, sems, order, acc = refs[-5:]
    tile_size = tiles.shape[1]
    per_piece = pieces[0].shape[0] // tile_size

    def add(place, value):
        acc[place] += value

    finish = run_tiles(
        span, span, per_piece, users, items, owner, meta, tiles, slab, add, buf, sems, order
    )
    acc[...] = start[...]
    fill(slab, pieces, per_piece)
    finish()
    width = tile_size // len(orders)
    for o, bits in enumerate(orders):
        cut = slice(o * width, (o + 1) * width)
        for k, place in enumerate(places(bits, 0)):
            outs[2 * o][k] = acc[place, :, cut]
        for k, place in enumerate(places(bits, 1)):
            outs[2 * o + 1][k] = acc[place, :, cut].astype(BF16)


def tile_call(kernel, scalars, pieces, extra, tiles, shapes, scratch, seconds):
    users = scalars[0].shape[0]
    tile_size = tiles.shape[1]
    blocks = len(pieces) * pieces[0].shape[0] // tile_size
    smem = pl.BlockSpec(memory_space=pltpu.SMEM)
    vmem = pl.BlockSpec(memory_space=pltpu.VMEM)
    return pl.pallas_call(
        kernel,
        out_shape=shapes,
        in_specs=[smem] * len(scalars)
        + [vmem] * (len(pieces) + len(extra))
        + [pl.BlockSpec(memory_space=pl.ANY)],
        out_specs=[vmem] * len(shapes),
        scratch_shapes=[
            pltpu.VMEM((blocks, 2 * pieces[0].shape[1], tile_size), BF16),
            pltpu.VMEM((SLOTS, tile_size, tile_size), BF16),
            pltpu.SemaphoreType.DMA((SLOTS,)),
            pltpu.SMEM((users,), jnp.int32),
        ]
        + scratch,
        compiler_params=pltpu.CompilerParams(vmem_limit_bytes=32 * 2**20),
        cost_estimate=pl.CostEstimate(
            flops=0, bytes_accessed=seconds, transcendentals=0
        ),
    )(*scalars, *pieces, *extra, tiles)


def near_sums(scalars, pieces, tiles, rows):
    tile_size = tiles.shape[1]
    kc = pieces[0].shape[1] // CHUNKS
    shapes = [jax.ShapeDtypeStruct((rows, kc, tile_size), F32)] * CHUNKS
    return tile_call(
        functools.partial(near_kernel, len(pieces)), scalars, pieces, [], tiles, shapes, [], NEAR_COST
    )


def far_sums(scalars, pieces, start, tiles, orders, cost):
    rows, kc, tile_size = start.shape
    width = tile_size // len(orders)
    shapes = []
    for _ in orders:
        shapes.append(jax.ShapeDtypeStruct((rows // 2, kc, width), F32))
        shapes.append(jax.ShapeDtypeStruct((rows // 2, kc, width), BF16))
    return tile_call(
        functools.partial(far_kernel, len(pieces), orders),
        scalars,
        pieces,
        [start],
        tiles,
        shapes,
        [pltpu.VMEM(start.shape, F32)],
        cost,
    )


def mm(a, b):
    return lax.dot_general(a, b, (((1,), (0,)), ((), ())), precision=HIGH, preferred_element_type=F32)


def mmt(a, b):
    return lax.dot_general(a, b, (((1,), (1,)), ((), ())), precision=HIGH, preferred_element_type=F32)


def factor_kernel(packed, inverse, good):
    n = packed.shape[1]
    r = lax.broadcasted_iota(jnp.int32, (n, n), 0)
    c = lax.broadcasted_iota(jnp.int32, (n, n), 1)
    mixed = packed[:n]
    flipped = mixed.T
    side = packed[n : 2 * n]
    tail = jnp.broadcast_to(packed[2 * n : 2 * n + 1], (n, n))
    first = jnp.where(r >= c, mixed, flipped)
    second = jnp.where(r < c, mixed, jnp.where(r > c, flipped, tail))
    gram = jnp.concatenate(
        [jnp.concatenate([first, side.T], axis=1), jnp.concatenate([side, second], axis=1)], axis=0
    )
    m = 2 * n
    rr = lax.broadcasted_iota(jnp.int32, (m, m), 0)
    cc = lax.broadcasted_iota(jnp.int32, (m, m), 1)
    on = rr == cc
    eye = jnp.where(on, 1.0, 0.0).astype(F32)
    low = jnp.where(rr > cc, 1.0, jnp.where(on, 0.5, 0.0)).astype(F32)
    diag = jnp.where(on, gram, 0.0)
    scale_row = lax.rsqrt(jnp.sum(diag, axis=0, keepdims=True))
    scale_col = lax.rsqrt(jnp.sum(diag, axis=1, keepdims=True))
    unit = gram * scale_row * scale_col
    off = unit - eye
    square = jnp.dot(off, off, preferred_element_type=F32)
    spread = jnp.max(jnp.sum(jnp.abs(jnp.dot(square, square, preferred_element_type=F32)), axis=1))
    w = eye - low * off
    for _ in range(NEWTON):
        err = mmt(mm(w, unit), w) - eye
        w = w - mm(low * err, w)
    last = jnp.max(jnp.sum(jnp.abs(err), axis=1))
    inflation = jnp.max(jnp.sum(w * w, axis=0))
    inverse[...] = w * scale_row
    good[0] = jnp.where((spread < 0.025) & (last < 0.01) & (inflation < 1.1), 1, 0)


def factor(packed):
    n = packed.shape[1]
    return pl.pallas_call(
        factor_kernel,
        out_shape=[jax.ShapeDtypeStruct((2 * n, 2 * n), F32), jax.ShapeDtypeStruct((1,), jnp.int32)],
        in_specs=[pl.BlockSpec(memory_space=pltpu.VMEM)],
        out_specs=[pl.BlockSpec(memory_space=pltpu.VMEM), pl.BlockSpec(memory_space=pltpu.SMEM)],
        compiler_params=pltpu.CompilerParams(vmem_limit_bytes=24 * 2**20),
        cost_estimate=pl.CostEstimate(
            flops=0, bytes_accessed=LATE_COST, transcendentals=0
        ),
    )(packed)


def pack(gram):
    n = gram.shape[0] // 2
    r = lax.broadcasted_iota(jnp.int32, (n, n), 0)
    c = lax.broadcasted_iota(jnp.int32, (n, n), 1)
    mixed = jnp.where(r >= c, gram[:n, :n], gram[n:, n:])
    tail = jnp.sum(jnp.where(r == c, gram[n:, n:], 0.0), axis=0, keepdims=True)
    return jnp.concatenate([mixed, gram[n:, :n], jnp.broadcast_to(tail, (8, n))], axis=0)


def full_path(rows, cols, sketch, tiles, tile_user, tile_item, tile_count, item_owner, packed):
    n = packed.shape[1]
    r = lax.broadcasted_iota(jnp.int32, (n, n), 0)
    c = lax.broadcasted_iota(jnp.int32, (n, n), 1)
    mixed, side, tail = packed[:n], packed[n : 2 * n], packed[2 * n : 2 * n + 1]
    first = jnp.where(r >= c, mixed, mixed.T)
    second = jnp.where(r < c, mixed, jnp.where(r > c, mixed.T, tail))
    gram = jnp.block([[first, side.T], [side, second]])
    lower = jnp.linalg.cholesky(gram)
    basis = lax.linalg.triangular_solve(lower, sketch, left_side=False, lower=True, transpose_a=True).astype(BF16)
    have = {0: basis}
    for bit in bits_of(cols):
        for place in list(have):
            have[place | bit] = swap(have[place], "cols", cols, bit)
    slab = jnp.concatenate([have[i] for i in range(cols)], axis=0)
    col = lax.axis_index("cols")
    row = lax.axis_index("rows")
    per_piece = sketch.shape[0] // tiles.shape[2]
    owner = item_owner[0]
    tile_size = tiles.shape[2]

    def step(index, sums):
        user = tile_user[index]
        block = lax.bitwise_xor(user // per_piece, col) * per_piece + user % per_piece
        part_rows = lax.dynamic_slice_in_dim(slab, block * tile_size, tile_size, 0)
        part = lax.dot_general(part_rows, tiles[index], (((0,), (0,)), ((), ())), preferred_element_type=F32)
        place = lax.bitwise_xor(owner[tile_item[index]], row)
        now = lax.dynamic_index_in_dim(sums, place, 0, keepdims=False)
        return lax.dynamic_update_index_in_dim(sums, now + part, place, 0)

    totals = jnp.zeros((owner.shape[0], sketch.shape[1], tile_size), F32)
    totals = lax.fori_loop(0, tile_count[0], step, totals)
    for bit in bits_of(rows):
        totals = totals[:bit] + swap(totals[bit:], "rows", rows, bit)
    return totals[0]


def after(value, *others):
    return lax.optimization_barrier((value, *others))[0]


def exchange(lanes, rows):
    got = [None] * len(lanes)
    for bit in sorted({lane[2] for lane in lanes}):
        members = [i for i, lane in enumerate(lanes) if lane[2] == bit]
        came = swap(jnp.concatenate([lanes[i][1] for i in members], axis=0), "rows", rows, 1 << bit)
        first = 0
        for i in members:
            last = first + lanes[i][1].shape[0]
            got[i] = came[first:last]
            first = last
    return got


def split(total):
    half = total.shape[0] // 2
    return total[:half], total[half:].astype(BF16)


def body(rows, cols, sketch, tiles, tile_user, tile_item, tile_count, item_owner):
    width = sketch.shape[1]
    row_bits = rows.bit_length() - 1
    first_order = tuple(range(row_bits))
    orders = (first_order, (1, 0) + first_order[2:])
    row = lax.axis_index("rows")
    col = lax.axis_index("cols")
    meta = jnp.stack([tile_count[0], row, col]).astype(jnp.int32)
    scalars = (tile_user, tile_item, item_owner[0], meta)
    kc = width // CHUNKS
    far_bit, *near_bits = bits_of(cols)

    def spread(piece):
        have = {0: piece}
        for bit in near_bits:
            for place in list(have):
                have[place | bit] = swap(have[place], "cols", cols, bit)
        return [have[i] for i in range(cols // 2)]

    fence = lax.optimization_barrier
    far = far_bit
    crossed = [swap(sketch[:, :kc], "cols", cols, far)]
    near = spread(sketch)
    crossed.append(swap(after(sketch, near[-1])[:, kc:], "cols", cols, far))
    sums = near_sums(scalars, near, tiles, rows)
    source = after(sketch, sums[0])
    gram = lax.dot_general(
        source, source, (((0,), (0,)), ((), ())), precision=HIGH, preferred_element_type=F32
    )
    packed = pack(gram)
    for bit in near_bits:
        packed = packed + swap(packed, "cols", cols, bit)
    came = swap(packed, "rows", rows, 1)
    crossed[0] = after(crossed[0], packed)
    outs = far_sums(scalars, spread(crossed[0]), sums[0], tiles, orders, EARLY_COST)
    packed, came, *outs = fence((packed, came, *outs))
    packed = packed + came
    came = swap(packed, "rows", rows, 2)
    lanes = [(outs[2 * o], outs[2 * o + 1], order[0]) for o, order in enumerate(orders)]
    got = exchange(lanes, rows)
    crossed[1] = after(crossed[1], packed)
    later = far_sums(scalars, spread(crossed[1]), sums[1], tiles, orders, LATE_COST)
    packed, came, *rest = fence((packed, came, *got, *later))
    got, later = rest[: len(got)], rest[len(got) :]
    packed = packed + came
    stages = [("rows", 1 << b) for b in range(2, row_bits)] + [("cols", far)]

    totals = [lane[0] + g.astype(F32) for lane, g in zip(lanes, got)]
    late = [(later[2 * o], later[2 * o + 1]) for o in range(len(orders))]
    done = []
    for step in range(1, row_bits + 1):
        lanes = []
        if step < row_bits:
            lanes += [(*split(t), order[step]) for t, order in zip(totals, orders)]
        lanes += [(*pair, order[step - 1]) for pair, order in zip(late, orders)]
        if step < row_bits:
            axis, bit = stages[step - 1]
            came = swap(packed, axis, rows if axis == "rows" else cols, bit)
            got = exchange(lanes, rows)
            packed, came, *got = fence((packed, came, *got))
            packed = packed + came
        else:
            got = exchange(lanes, rows)
            inverse, good = factor(packed)
        new = [lane[0] + g.astype(F32) for lane, g in zip(lanes, got)]
        if step < row_bits:
            totals, new = new[: len(orders)], new[len(orders) :]
            late = [split(t) for t in new]
        if step >= row_bits - 1:
            done.append(jnp.concatenate([t[0] for t in (totals if step < row_bits else new)], axis=1))
    head = mm(inverse[:, :kc], done[0])
    out = lax.cond(
        good[0] > 0,
        lambda: jnp.concatenate([head[:kc], head[kc:] + mm(inverse[kc:, kc:], done[1])], axis=0),
        lambda: full_path(rows, cols, sketch, tiles, tile_user, tile_item, tile_count, item_owner, packed),
    )
    return out[None, None]


def solution(mesh):
    placed = (
        P(("rows", "cols"), None),
        P(("rows", "cols"), None, None),
        P(("rows", "cols")),
        P(("rows", "cols")),
        P(("rows", "cols")),
        P("cols", None),
    )
    return jax.shard_map(
        functools.partial(body, mesh.shape["rows"], mesh.shape["cols"]),
        mesh=mesh,
        in_specs=placed,
        out_specs=P("rows", "cols", None, None),
        check_vma=False,
    )
```

```python
import functools

import jax
import jax.numpy as jnp
from jax import lax
from jax.experimental import pallas as pl
from jax.experimental.pallas import tpu as pltpu
from jax.sharding import PartitionSpec as P

F32 = jnp.float32
BF16 = jnp.bfloat16
HIGH = lax.Precision.HIGHEST
SLOTS = 12
GROUP = 4
NEAR_COST = 200 * 2**20
EARLY_COST = 1024
LATE_COST = 1024
FACTOR_COST = 200 * 2**20
CHUNKS = 2
NEWTON = 2


def bits_of(count):
    return [1 << b for b in reversed(range(count.bit_length() - 1))]


def swap(x, axis, count, bit):
    return lax.ppermute(x, axis, [(i, i ^ bit) for i in range(count)])


def places(order, parity):
    found = [parity << order[0]]
    for bit in reversed(order[1:]):
        found = found + [p | (1 << bit) for p in found]
    return found


def run_tiles(base, span, per_piece, users, items, owner, meta, tiles, slab, add, buf, sems, order):
    count, row, col = meta[0], meta[1], meta[2]

    def relative(t):
        user = users[t]
        return lax.bitwise_xor(user // per_piece, col) - base, lax.rem(user, per_piece)

    def choose(t, n):
        piece, _ = relative(t)
        order[n] = t
        return n + jnp.where((piece >= 0) & (piece < span), 1, 0)

    live = lax.fori_loop(0, count, choose, 0)

    def fetch(i):
        slot = lax.rem(i, SLOTS)
        return pltpu.make_async_copy(tiles.at[order[i]], buf.at[slot], sems.at[slot])

    for i in range(SLOTS):
        @pl.when(i < live)
        def _():
            fetch(i).start()

    def group(first, size):
        for q in range(size):
            fetch(first + q).wait()
        found = []
        for q in range(size):
            piece, part = relative(order[first + q])
            both = jnp.dot(
                slab[piece * per_piece + part],
                buf[lax.rem(first + q, SLOTS)],
                preferred_element_type=F32,
            )
            half = both.shape[0] // 2
            found.append(both[:half] + both[half:])
        for q in range(size):
            add(lax.bitwise_xor(owner[items[order[first + q]]], row), found[q])
        for q in range(size):
            @pl.when(first + q + SLOTS < live)
            def _():
                fetch(first + q + SLOTS).start()

    def finish():
        groups = live // GROUP

        def many(g, _):
            group(g * GROUP, GROUP)
            return 0

        def one(i, _):
            group(i, 1)
            return 0

        lax.fori_loop(0, groups, many, 0)
        lax.fori_loop(groups * GROUP, live, one, 0)

    return finish


def fill(slab, pieces, per_piece):
    tile_size = slab.shape[2]
    kc = slab.shape[1] // 2
    for c, piece in enumerate(pieces):
        for h in range(per_piece):
            block = piece[h * tile_size : (h + 1) * tile_size, :].T
            high = block.astype(BF16)
            slab[c * per_piece + h, :kc, :] = high
            slab[c * per_piece + h, kc:, :] = (block - high.astype(F32)).astype(BF16)


def near_kernel(span, users, items, owner, meta, *refs):
    pieces = refs[:span]
    tiles = refs[span]
    sums = refs[span + 1 : -4]
    slab, buf, sems, order = refs[-4:]
    per_piece = pieces[0].shape[0] // tiles.shape[1]
    kc = sums[0].shape[1]

    def add(place, value):
        for k, part in enumerate(sums):
            part[place] += value[k * kc : (k + 1) * kc]

    finish = run_tiles(
        0, span, per_piece, users, items, owner, meta, tiles, slab, add, buf, sems, order
    )
    for part in sums:
        part[...] = jnp.zeros_like(part)
    fill(slab, pieces, per_piece)
    finish()


def far_kernel(span, orders, users, items, owner, meta, *refs):
    pieces = refs[:span]
    start, tiles = refs[span], refs[span + 1]
    outs = refs[span + 2 : -5]
    slab, buf, sems, order, acc = refs[-5:]
    tile_size = tiles.shape[1]
    per_piece = pieces[0].shape[0] // tile_size

    def add(place, value):
        acc[place] += value

    finish = run_tiles(
        span, span, per_piece, users, items, owner, meta, tiles, slab, add, buf, sems, order
    )
    acc[...] = start[...]
    fill(slab, pieces, per_piece)
    finish()
    width = tile_size // len(orders)
    for o, bits in enumerate(orders):
        cut = slice(o * width, (o + 1) * width)
        for k, place in enumerate(places(bits, 0)):
            outs[2 * o][k] = acc[place, :, cut]
        for k, place in enumerate(places(bits, 1)):
            outs[2 * o + 1][k] = acc[place, :, cut].astype(BF16)


def tile_call(kernel, scalars, pieces, extra, tiles, shapes, scratch, seconds):
    users = scalars[0].shape[0]
    tile_size = tiles.shape[1]
    blocks = len(pieces) * pieces[0].shape[0] // tile_size
    smem = pl.BlockSpec(memory_space=pltpu.SMEM)
    vmem = pl.BlockSpec(memory_space=pltpu.VMEM)
    return pl.pallas_call(
        kernel,
        out_shape=shapes,
        in_specs=[smem] * len(scalars)
        + [vmem] * (len(pieces) + len(extra))
        + [pl.BlockSpec(memory_space=pl.ANY)],
        out_specs=[vmem] * len(shapes),
        scratch_shapes=[
            pltpu.VMEM((blocks, 2 * pieces[0].shape[1], tile_size), BF16),
            pltpu.VMEM((SLOTS, tile_size, tile_size), BF16),
            pltpu.SemaphoreType.DMA((SLOTS,)),
            pltpu.SMEM((users,), jnp.int32),
        ]
        + scratch,
        compiler_params=pltpu.CompilerParams(vmem_limit_bytes=32 * 2**20),
        cost_estimate=pl.CostEstimate(
            flops=0, bytes_accessed=seconds, transcendentals=0
        ),
    )(*scalars, *pieces, *extra, tiles)


def near_sums(scalars, pieces, tiles, rows):
    tile_size = tiles.shape[1]
    kc = pieces[0].shape[1] // CHUNKS
    shapes = [jax.ShapeDtypeStruct((rows, kc, tile_size), F32)] * CHUNKS
    return tile_call(
        functools.partial(near_kernel, len(pieces)), scalars, pieces, [], tiles, shapes, [], NEAR_COST
    )


def far_sums(scalars, pieces, start, tiles, orders, cost):
    rows, kc, tile_size = start.shape
    width = tile_size // len(orders)
    shapes = []
    for _ in orders:
        shapes.append(jax.ShapeDtypeStruct((rows // 2, kc, width), F32))
        shapes.append(jax.ShapeDtypeStruct((rows // 2, kc, width), BF16))
    return tile_call(
        functools.partial(far_kernel, len(pieces), orders),
        scalars,
        pieces,
        [start],
        tiles,
        shapes,
        [pltpu.VMEM(start.shape, F32)],
        cost,
    )


def mm(a, b):
    return lax.dot_general(a, b, (((1,), (0,)), ((), ())), precision=HIGH, preferred_element_type=F32)


def mmt(a, b):
    return lax.dot_general(a, b, (((1,), (1,)), ((), ())), precision=HIGH, preferred_element_type=F32)


def factor_kernel(packed, inverse, good):
    n = packed.shape[1]
    r = lax.broadcasted_iota(jnp.int32, (n, n), 0)
    c = lax.broadcasted_iota(jnp.int32, (n, n), 1)
    mixed = packed[:n]
    flipped = mixed.T
    side = packed[n : 2 * n]
    tail = jnp.broadcast_to(packed[2 * n : 2 * n + 1], (n, n))
    first = jnp.where(r >= c, mixed, flipped)
    second = jnp.where(r < c, mixed, jnp.where(r > c, flipped, tail))
    gram = jnp.concatenate(
        [jnp.concatenate([first, side.T], axis=1), jnp.concatenate([side, second], axis=1)], axis=0
    )
    m = 2 * n
    rr = lax.broadcasted_iota(jnp.int32, (m, m), 0)
    cc = lax.broadcasted_iota(jnp.int32, (m, m), 1)
    on = rr == cc
    eye = jnp.where(on, 1.0, 0.0).astype(F32)
    low = jnp.where(rr > cc, 1.0, jnp.where(on, 0.5, 0.0)).astype(F32)
    diag = jnp.where(on, gram, 0.0)
    scale_row = lax.rsqrt(jnp.sum(diag, axis=0, keepdims=True))
    scale_col = lax.rsqrt(jnp.sum(diag, axis=1, keepdims=True))
    unit = gram * scale_row * scale_col
    off = unit - eye
    square = jnp.dot(off, off, preferred_element_type=F32)
    spread = jnp.max(jnp.sum(jnp.abs(jnp.dot(square, square, preferred_element_type=F32)), axis=1))
    w = eye - low * off
    for _ in range(NEWTON):
        err = mmt(mm(w, unit), w) - eye
        w = w - mm(low * err, w)
    last = jnp.max(jnp.sum(jnp.abs(err), axis=1))
    inflation = jnp.max(jnp.sum(w * w, axis=0))
    inverse[...] = w * scale_row
    good[0] = jnp.where((spread < 0.025) & (last < 0.01) & (inflation < 1.1), 1, 0)


def factor(packed):
    n = packed.shape[1]
    return pl.pallas_call(
        factor_kernel,
        out_shape=[jax.ShapeDtypeStruct((2 * n, 2 * n), F32), jax.ShapeDtypeStruct((1,), jnp.int32)],
        in_specs=[pl.BlockSpec(memory_space=pltpu.VMEM)],
        out_specs=[pl.BlockSpec(memory_space=pltpu.VMEM), pl.BlockSpec(memory_space=pltpu.SMEM)],
        compiler_params=pltpu.CompilerParams(vmem_limit_bytes=24 * 2**20),
        cost_estimate=pl.CostEstimate(
            flops=0, bytes_accessed=FACTOR_COST, transcendentals=0
        ),
    )(packed)


def pack(gram):
    n = gram.shape[0] // 2
    r = lax.broadcasted_iota(jnp.int32, (n, n), 0)
    c = lax.broadcasted_iota(jnp.int32, (n, n), 1)
    mixed = jnp.where(r >= c, gram[:n, :n], gram[n:, n:])
    tail = jnp.sum(jnp.where(r == c, gram[n:, n:], 0.0), axis=0, keepdims=True)
    return jnp.concatenate([mixed, gram[n:, :n], jnp.broadcast_to(tail, (8, n))], axis=0)


def full_path(rows, cols, sketch, tiles, tile_user, tile_item, tile_count, item_owner, packed):
    n = packed.shape[1]
    r = lax.broadcasted_iota(jnp.int32, (n, n), 0)
    c = lax.broadcasted_iota(jnp.int32, (n, n), 1)
    mixed, side, tail = packed[:n], packed[n : 2 * n], packed[2 * n : 2 * n + 1]
    first = jnp.where(r >= c, mixed, mixed.T)
    second = jnp.where(r < c, mixed, jnp.where(r > c, mixed.T, tail))
    gram = jnp.block([[first, side.T], [side, second]])
    lower = jnp.linalg.cholesky(gram)
    basis = lax.linalg.triangular_solve(lower, sketch, left_side=False, lower=True, transpose_a=True).astype(BF16)
    have = {0: basis}
    for bit in bits_of(cols):
        for place in list(have):
            have[place | bit] = swap(have[place], "cols", cols, bit)
    slab = jnp.concatenate([have[i] for i in range(cols)], axis=0)
    col = lax.axis_index("cols")
    row = lax.axis_index("rows")
    per_piece = sketch.shape[0] // tiles.shape[2]
    owner = item_owner[0]
    tile_size = tiles.shape[2]

    def step(index, sums):
        user = tile_user[index]
        block = lax.bitwise_xor(user // per_piece, col) * per_piece + user % per_piece
        part_rows = lax.dynamic_slice_in_dim(slab, block * tile_size, tile_size, 0)
        part = lax.dot_general(part_rows, tiles[index], (((0,), (0,)), ((), ())), preferred_element_type=F32)
        place = lax.bitwise_xor(owner[tile_item[index]], row)
        now = lax.dynamic_index_in_dim(sums, place, 0, keepdims=False)
        return lax.dynamic_update_index_in_dim(sums, now + part, place, 0)

    totals = jnp.zeros((owner.shape[0], sketch.shape[1], tile_size), F32)
    totals = lax.fori_loop(0, tile_count[0], step, totals)
    for bit in bits_of(rows):
        totals = totals[:bit] + swap(totals[bit:], "rows", rows, bit)
    return totals[0]


def after(value, *others):
    return lax.optimization_barrier((value, *others))[0]


def exchange(lanes, rows):
    got = [None] * len(lanes)
    for bit in sorted({lane[2] for lane in lanes}):
        members = [i for i, lane in enumerate(lanes) if lane[2] == bit]
        came = swap(jnp.concatenate([lanes[i][1] for i in members], axis=0), "rows", rows, 1 << bit)
        first = 0
        for i in members:
            last = first + lanes[i][1].shape[0]
            got[i] = came[first:last]
            first = last
    return got


def split(total):
    half = total.shape[0] // 2
    return total[:half], total[half:].astype(BF16)


def body(rows, cols, sketch, tiles, tile_user, tile_item, tile_count, item_owner):
    width = sketch.shape[1]
    row_bits = rows.bit_length() - 1
    first_order = tuple(range(row_bits))
    orders = (first_order, (1, 0) + first_order[2:])
    row = lax.axis_index("rows")
    col = lax.axis_index("cols")
    meta = jnp.stack([tile_count[0], row, col]).astype(jnp.int32)
    scalars = (tile_user, tile_item, item_owner[0], meta)
    kc = width // CHUNKS
    far_bit, *near_bits = bits_of(cols)

    def spread(piece):
        have = {0: piece}
        for bit in near_bits:
            for place in list(have):
                have[place | bit] = swap(have[place], "cols", cols, bit)
        return [have[i] for i in range(cols // 2)]

    fence = lax.optimization_barrier
    far = far_bit
    crossed = [swap(sketch[:, :kc], "cols", cols, far)]
    near = spread(sketch)
    crossed.append(swap(after(sketch, near[-1])[:, kc:], "cols", cols, far))
    sums = near_sums(scalars, near, tiles, rows)
    source = after(sketch, sums[0])
    gram = lax.dot_general(
        source, source, (((0,), (0,)), ((), ())), precision=HIGH, preferred_element_type=F32
    )
    packed = pack(gram)
    for bit in near_bits:
        packed = packed + swap(packed, "cols", cols, bit)
    came = swap(packed, "rows", rows, 1)
    crossed[0] = after(crossed[0], packed)
    outs = far_sums(scalars, spread(crossed[0]), sums[0], tiles, orders, EARLY_COST)
    packed, came, *outs = fence((packed, came, *outs))
    packed = packed + came
    packed = packed + swap(packed, "rows", rows, 2)
    came = swap(packed, "rows", rows, 4)
    lanes = [(outs[2 * o], outs[2 * o + 1], order[0]) for o, order in enumerate(orders)]
    got = exchange(lanes, rows)
    crossed[1] = after(crossed[1], packed)
    later = far_sums(scalars, spread(crossed[1]), sums[1], tiles, orders, LATE_COST)
    packed, came, *rest = fence((packed, came, *got, *later))
    got, later = rest[: len(got)], rest[len(got) :]
    packed = packed + came
    stages = [("cols", far)] + [("rows", 1 << b) for b in range(3, row_bits)]

    totals = [lane[0] + g.astype(F32) for lane, g in zip(lanes, got)]
    late = [(later[2 * o], later[2 * o + 1]) for o in range(len(orders))]
    done = []
    for step in range(1, row_bits + 1):
        lanes = []
        if step < row_bits:
            lanes += [(*split(t), order[step]) for t, order in zip(totals, orders)]
        lanes += [(*pair, order[step - 1]) for pair, order in zip(late, orders)]
        got = exchange(lanes, rows)
        if step <= len(stages):
            axis, bit = stages[step - 1]
            came = swap(packed, axis, rows if axis == "rows" else cols, bit)
            packed, came, *got = fence((packed, came, *got))
            packed = packed + came
        if step == len(stages) + 1:
            inverse, good = factor(after(packed, *[lane[1] for lane in lanes]))
            inverse, *got = fence((inverse, *got))
        new = [lane[0] + g.astype(F32) for lane, g in zip(lanes, got)]
        if step < row_bits:
            totals, new = new[: len(orders)], new[len(orders) :]
            late = [split(t) for t in new]
        if step >= row_bits - 1:
            done.append(jnp.concatenate([t[0] for t in (totals if step < row_bits else new)], axis=1))
    head = mm(inverse[:, :kc], done[0])
    out = lax.cond(
        good[0] > 0,
        lambda: jnp.concatenate([head[:kc], head[kc:] + mm(inverse[kc:, kc:], done[1])], axis=0),
        lambda: full_path(rows, cols, sketch, tiles, tile_user, tile_item, tile_count, item_owner, packed),
    )
    return out[None, None]


def solution(mesh):
    placed = (
        P(("rows", "cols"), None),
        P(("rows", "cols"), None, None),
        P(("rows", "cols")),
        P(("rows", "cols")),
        P(("rows", "cols")),
        P("cols", None),
    )
    return jax.shard_map(
        functools.partial(body, mesh.shape["rows"], mesh.shape["cols"]),
        mesh=mesh,
        in_specs=placed,
        out_specs=P("rows", "cols", None, None),
        check_vma=False,
    )
```

```python
import functools

import jax
import jax.numpy as jnp
from jax import lax
from jax.experimental import pallas as pl
from jax.experimental.pallas import tpu as pltpu
from jax.sharding import PartitionSpec as P

F32 = jnp.float32
BF16 = jnp.bfloat16
HIGH = lax.Precision.HIGHEST
SLOTS = 12
SPARE = 4 * 2**20
GROUP = 4
NEAR_COST = 200 * 2**20
EARLY_COST = 1024
LATE_COST = 1024
FACTOR_COST = 200 * 2**20
CHUNKS = (160, 96)
NEWTON = 2


def bits_of(count):
    return [1 << b for b in reversed(range(count.bit_length() - 1))]


def swap(x, axis, count, bit):
    return lax.ppermute(x, axis, [(i, i ^ bit) for i in range(count)])


def places(order, parity):
    found = [parity << order[0]]
    for bit in reversed(order[1:]):
        found = found + [p | (1 << bit) for p in found]
    return found


def run_tiles(base, span, per_piece, users, items, owner, meta, tiles, slab, add, buf, sems, order):
    count, row, col = meta[0], meta[1], meta[2]

    def relative(t):
        user = users[t]
        return lax.bitwise_xor(user // per_piece, col) - base, lax.rem(user, per_piece)

    def choose(t, n):
        piece, _ = relative(t)
        order[n] = t
        return n + jnp.where((piece >= 0) & (piece < span), 1, 0)

    live = lax.fori_loop(0, count, choose, 0)

    def fetch(i):
        slot = lax.rem(i, SLOTS)
        return pltpu.make_async_copy(tiles.at[order[i]], buf.at[slot], sems.at[slot])

    for i in range(SLOTS):
        @pl.when(i < live)
        def _():
            fetch(i).start()

    def group(first, size):
        for q in range(size):
            fetch(first + q).wait()
        found = []
        for q in range(size):
            piece, part = relative(order[first + q])
            both = jnp.dot(
                slab[piece * per_piece + part],
                buf[lax.rem(first + q, SLOTS)],
                preferred_element_type=F32,
            )
            found.append(both)
        for q in range(size):
            add(lax.bitwise_xor(owner[items[order[first + q]]], row), found[q])
        for q in range(size):
            @pl.when(first + q + SLOTS < live)
            def _():
                fetch(first + q + SLOTS).start()

    def finish():
        groups = live // GROUP

        def many(g, _):
            group(g * GROUP, GROUP)
            return 0

        def one(i, _):
            group(i, 1)
            return 0

        lax.fori_loop(0, groups, many, 0)
        lax.fori_loop(groups * GROUP, live, one, 0)

    return finish


def split_kernel(sketch, whole, *chunks):
    flat = sketch[...].T
    high = flat.astype(BF16)
    low = (flat - high.astype(F32)).astype(BF16)
    first = 0
    for chunk in chunks:
        kc = chunk.shape[0] // 2
        for i, part in enumerate((high, low)):
            rows = part[first : first + kc]
            chunk[i * kc : (i + 1) * kc, :] = rows
            whole[2 * first + i * kc : 2 * first + (i + 1) * kc, :] = rows
        first += kc


def split_sketch(sketch):
    users, width = sketch.shape
    vmem = pl.BlockSpec(memory_space=pltpu.VMEM)
    return pl.pallas_call(
        split_kernel,
        out_shape=[jax.ShapeDtypeStruct((2 * k, users), BF16) for k in (width, *CHUNKS)],
        in_specs=[vmem],
        out_specs=[vmem] * (1 + len(CHUNKS)),
        compiler_params=pltpu.CompilerParams(vmem_limit_bytes=16 * 2**20),
    )(sketch)


def fill(slab, pieces, per_piece):
    tile_size = slab.shape[2]
    for c, piece in enumerate(pieces):
        for h in range(per_piece):
            slab[c * per_piece + h] = piece[:, h * tile_size : (h + 1) * tile_size]


def near_kernel(span, users, items, owner, meta, *refs):
    pieces = refs[:span]
    tiles = refs[span]
    sums = refs[span + 1 : -4]
    slab, buf, sems, order = refs[-4:]
    per_piece = pieces[0].shape[1] // tiles.shape[1]

    def add(place, both):
        first = 0
        for part in sums:
            kc = part.shape[1]
            part[place] += both[first : first + kc] + both[first + kc : first + 2 * kc]
            first += 2 * kc

    finish = run_tiles(
        0, span, per_piece, users, items, owner, meta, tiles, slab, add, buf, sems, order
    )
    for part in sums:
        part[...] = jnp.zeros_like(part)
    fill(slab, pieces, per_piece)
    finish()


def far_kernel(span, orders, users, items, owner, meta, *refs):
    pieces = refs[:span]
    start, tiles = refs[span], refs[span + 1]
    outs = refs[span + 2 : -5]
    slab, buf, sems, order, acc = refs[-5:]
    tile_size = tiles.shape[1]
    per_piece = pieces[0].shape[1] // tile_size
    kc = pieces[0].shape[0] // 2

    def add(place, both):
        acc[place] += both[:kc] + both[kc:]

    finish = run_tiles(
        span, span, per_piece, users, items, owner, meta, tiles, slab, add, buf, sems, order
    )
    acc[...] = start[...]
    fill(slab, pieces, per_piece)
    finish()
    width = tile_size // len(orders)
    for o, bits in enumerate(orders):
        cut = slice(o * width, (o + 1) * width)
        for k, place in enumerate(places(bits, 0)):
            outs[2 * o][k] = acc[place, :, cut]
        for k, place in enumerate(places(bits, 1)):
            outs[2 * o + 1][k] = acc[place, :, cut].astype(BF16)


def tile_call(kernel, scalars, pieces, extra, tiles, shapes, scratch, cost):
    users = scalars[0].shape[0]
    tile_size = tiles.shape[1]
    blocks = len(pieces) * pieces[0].shape[1] // tile_size
    smem = pl.BlockSpec(memory_space=pltpu.SMEM)
    vmem = pl.BlockSpec(memory_space=pltpu.VMEM)
    slab = jax.ShapeDtypeStruct((blocks, pieces[0].shape[0], tile_size), BF16)
    buf = jax.ShapeDtypeStruct((SLOTS, tile_size, tile_size), BF16)
    held = sum(x.size * x.dtype.itemsize for x in (*pieces, *extra, *shapes, *scratch, slab, buf))
    return pl.pallas_call(
        kernel,
        out_shape=shapes,
        in_specs=[smem] * len(scalars)
        + [vmem] * (len(pieces) + len(extra))
        + [pl.BlockSpec(memory_space=pl.ANY)],
        out_specs=[vmem] * len(shapes),
        scratch_shapes=[
            pltpu.VMEM(slab.shape, BF16),
            pltpu.VMEM(buf.shape, BF16),
            pltpu.SemaphoreType.DMA((SLOTS,)),
            pltpu.SMEM((users,), jnp.int32),
        ]
        + [pltpu.VMEM(x.shape, x.dtype) for x in scratch],
        compiler_params=pltpu.CompilerParams(vmem_limit_bytes=held + SPARE),
        cost_estimate=pl.CostEstimate(flops=0, bytes_accessed=cost, transcendentals=0),
    )(*scalars, *pieces, *extra, tiles)


def near_sums(scalars, pieces, tiles, rows):
    tile_size = tiles.shape[1]
    shapes = [jax.ShapeDtypeStruct((rows, kc, tile_size), F32) for kc in CHUNKS]
    return tile_call(
        functools.partial(near_kernel, len(pieces)), scalars, pieces, [], tiles, shapes, [], NEAR_COST
    )


def far_sums(scalars, pieces, start, tiles, orders, cost):
    rows, kc, tile_size = start.shape
    width = tile_size // len(orders)
    shapes = []
    for _ in orders:
        shapes.append(jax.ShapeDtypeStruct((rows // 2, kc, width), F32))
        shapes.append(jax.ShapeDtypeStruct((rows // 2, kc, width), BF16))
    return tile_call(
        functools.partial(far_kernel, len(pieces), orders),
        scalars,
        pieces,
        [start],
        tiles,
        shapes,
        [jax.ShapeDtypeStruct(start.shape, F32)],
        cost,
    )


def mm(a, b):
    return lax.dot_general(a, b, (((1,), (0,)), ((), ())), precision=HIGH, preferred_element_type=F32)


def mmt(a, b):
    return lax.dot_general(a, b, (((1,), (1,)), ((), ())), precision=HIGH, preferred_element_type=F32)


def factor_kernel(packed, inverse, good):
    n = packed.shape[1]
    r = lax.broadcasted_iota(jnp.int32, (n, n), 0)
    c = lax.broadcasted_iota(jnp.int32, (n, n), 1)
    mixed = packed[:n]
    flipped = mixed.T
    side = packed[n : 2 * n]
    tail = jnp.broadcast_to(packed[2 * n : 2 * n + 1], (n, n))
    first = jnp.where(r >= c, mixed, flipped)
    second = jnp.where(r < c, mixed, jnp.where(r > c, flipped, tail))
    gram = jnp.concatenate(
        [jnp.concatenate([first, side.T], axis=1), jnp.concatenate([side, second], axis=1)], axis=0
    )
    m = 2 * n
    rr = lax.broadcasted_iota(jnp.int32, (m, m), 0)
    cc = lax.broadcasted_iota(jnp.int32, (m, m), 1)
    on = rr == cc
    eye = jnp.where(on, 1.0, 0.0).astype(F32)
    low = jnp.where(rr > cc, 1.0, jnp.where(on, 0.5, 0.0)).astype(F32)
    diag = jnp.where(on, gram, 0.0)
    scale_row = lax.rsqrt(jnp.sum(diag, axis=0, keepdims=True))
    scale_col = lax.rsqrt(jnp.sum(diag, axis=1, keepdims=True))
    unit = gram * scale_row * scale_col
    off = unit - eye
    square = jnp.dot(off, off, preferred_element_type=F32)
    spread = jnp.max(jnp.sum(jnp.abs(jnp.dot(square, square, preferred_element_type=F32)), axis=1))
    w = eye - low * off
    for _ in range(NEWTON):
        err = mmt(mm(w, unit), w) - eye
        w = w - mm(low * err, w)
    last = jnp.max(jnp.sum(jnp.abs(err), axis=1))
    inflation = jnp.max(jnp.sum(w * w, axis=0))
    inverse[...] = w * scale_row
    good[0] = jnp.where((spread < 0.025) & (last < 0.01) & (inflation < 1.1), 1, 0)


def factor(packed):
    n = packed.shape[1]
    return pl.pallas_call(
        factor_kernel,
        out_shape=[jax.ShapeDtypeStruct((2 * n, 2 * n), F32), jax.ShapeDtypeStruct((1,), jnp.int32)],
        in_specs=[pl.BlockSpec(memory_space=pltpu.VMEM)],
        out_specs=[pl.BlockSpec(memory_space=pltpu.VMEM), pl.BlockSpec(memory_space=pltpu.SMEM)],
        compiler_params=pltpu.CompilerParams(vmem_limit_bytes=24 * 2**20),
        cost_estimate=pl.CostEstimate(
            flops=0, bytes_accessed=FACTOR_COST, transcendentals=0
        ),
    )(packed)


def last_kernel(inverse, early, keep0, keep1, came, out):
    left = keep0[0] + came[0].astype(F32)
    right = keep1[0] + came[1].astype(F32)
    total = jnp.concatenate([early[...], jnp.concatenate([left, right], axis=1)], axis=0)
    w = inverse[...]
    wh, th = w.astype(BF16), total.astype(BF16)
    wl = (w - wh.astype(F32)).astype(BF16)
    tl = (total - th.astype(F32)).astype(BF16)
    small = jnp.dot(wh, tl, preferred_element_type=F32) + jnp.dot(wl, th, preferred_element_type=F32)
    out[...] = jnp.dot(wh, th, preferred_element_type=F32) + small


def last(inverse, early, keeps, came):
    vmem = pl.BlockSpec(memory_space=pltpu.VMEM)
    return pl.pallas_call(
        last_kernel,
        out_shape=jax.ShapeDtypeStruct((inverse.shape[0], early.shape[1]), F32),
        in_specs=[vmem] * 5,
        out_specs=vmem,
        compiler_params=pltpu.CompilerParams(vmem_limit_bytes=16 * 2**20),
    )(inverse, early, *keeps, came)


def pack(gram):
    n = gram.shape[0] // 2
    r = lax.broadcasted_iota(jnp.int32, (n, n), 0)
    c = lax.broadcasted_iota(jnp.int32, (n, n), 1)
    mixed = jnp.where(r >= c, gram[:n, :n], gram[n:, n:])
    tail = jnp.sum(jnp.where(r == c, gram[n:, n:], 0.0), axis=0, keepdims=True)
    return jnp.concatenate([mixed, gram[n:, :n], jnp.broadcast_to(tail, (8, n))], axis=0)


def full_path(rows, cols, sketch, tiles, tile_user, tile_item, tile_count, item_owner, packed):
    n = packed.shape[1]
    r = lax.broadcasted_iota(jnp.int32, (n, n), 0)
    c = lax.broadcasted_iota(jnp.int32, (n, n), 1)
    mixed, side, tail = packed[:n], packed[n : 2 * n], packed[2 * n : 2 * n + 1]
    first = jnp.where(r >= c, mixed, mixed.T)
    second = jnp.where(r < c, mixed, jnp.where(r > c, mixed.T, tail))
    gram = jnp.block([[first, side.T], [side, second]])
    lower = jnp.linalg.cholesky(gram)
    basis = lax.linalg.triangular_solve(lower, sketch, left_side=False, lower=True, transpose_a=True).astype(BF16)
    have = {0: basis}
    for bit in bits_of(cols):
        for place in list(have):
            have[place | bit] = swap(have[place], "cols", cols, bit)
    slab = jnp.concatenate([have[i] for i in range(cols)], axis=0)
    col = lax.axis_index("cols")
    row = lax.axis_index("rows")
    per_piece = sketch.shape[0] // tiles.shape[2]
    owner = item_owner[0]
    tile_size = tiles.shape[2]

    def step(index, sums):
        user = tile_user[index]
        block = lax.bitwise_xor(user // per_piece, col) * per_piece + user % per_piece
        part_rows = lax.dynamic_slice_in_dim(slab, block * tile_size, tile_size, 0)
        part = lax.dot_general(part_rows, tiles[index], (((0,), (0,)), ((), ())), preferred_element_type=F32)
        place = lax.bitwise_xor(owner[tile_item[index]], row)
        now = lax.dynamic_index_in_dim(sums, place, 0, keepdims=False)
        return lax.dynamic_update_index_in_dim(sums, now + part, place, 0)

    totals = jnp.zeros((owner.shape[0], sketch.shape[1], tile_size), F32)
    totals = lax.fori_loop(0, tile_count[0], step, totals)
    for bit in bits_of(rows):
        totals = totals[:bit] + swap(totals[bit:], "rows", rows, bit)
    return totals[0]


def after(value, *others):
    return lax.optimization_barrier((value, *others))[0]


def exchange(lanes, rows):
    groups = []
    for bit in sorted({lane[2] for lane in lanes}):
        members = [i for i, lane in enumerate(lanes) if lane[2] == bit]
        sent = [lanes[i][1].reshape(-1, lanes[i][1].shape[2]) for i in members]
        groups.append((members, swap(jnp.concatenate(sent, axis=0), "rows", rows, 1 << bit)))
    return groups


def received(lanes, groups):
    got = [None] * len(lanes)
    for members, came in groups:
        first = 0
        for i in members:
            shape = lanes[i][1].shape
            size = shape[0] * shape[1]
            got[i] = came[first : first + size].reshape(shape)
            first += size
    return [lane[0] + g.astype(F32) for lane, g in zip(lanes, got)]


def split(total):
    half = total.shape[0] // 2
    return total[:half], total[half:].astype(BF16)


def body(rows, cols, sketch, tiles, tile_user, tile_item, tile_count, item_owner):
    row_bits = rows.bit_length() - 1
    first_order = tuple(range(row_bits))
    orders = (first_order, (1, 0) + first_order[2:])
    row = lax.axis_index("rows")
    col = lax.axis_index("cols")
    meta = jnp.stack([tile_count[0], row, col]).astype(jnp.int32)
    scalars = (tile_user, tile_item, item_owner[0], meta)
    far_bit, *near_bits = bits_of(cols)

    def spread(piece):
        have = {0: piece}
        for bit in near_bits:
            for place in list(have):
                have[place | bit] = swap(have[place], "cols", cols, bit)
        return [have[i] for i in range(cols // 2)]

    fence = lax.optimization_barrier
    far = far_bit
    whole, *chunks = split_sketch(sketch)
    near = spread(whole)
    crossed = [swap(chunk, "cols", cols, far) for chunk in chunks]
    gram = lax.dot_general(
        sketch, sketch, (((0,), (0,)), ((), ())), precision=HIGH, preferred_element_type=F32
    )
    packed = pack(gram)
    for bit in near_bits:
        packed = packed + swap(packed, "cols", cols, bit)
    came = swap(packed, "rows", rows, 1)
    near[0] = after(near[0], packed)
    sums = near_sums(scalars, near, tiles, rows)
    packed, came, *sums = fence((packed, came, *sums))
    packed = packed + came
    came = swap(packed, "rows", rows, 2)
    crossed[0] = after(crossed[0], packed)
    outs = far_sums(scalars, spread(crossed[0]), sums[0], tiles, orders, EARLY_COST)
    packed, came, *outs = fence((packed, came, *outs))
    packed = packed + came
    came = swap(packed, "rows", rows, 4)
    lanes = [(outs[2 * o], outs[2 * o + 1], order[0]) for o, order in enumerate(orders)]
    groups = exchange(lanes, rows)
    crossed[1] = after(crossed[1], packed)
    later = far_sums(scalars, spread(crossed[1]), sums[1], tiles, orders, LATE_COST)
    flying = [g[1] for g in groups]
    packed, came, *rest = fence((packed, came, *flying, *later))
    groups = [(g[0], x) for g, x in zip(groups, rest)]
    later = rest[len(groups) :]
    packed = packed + came
    stages = [("cols", far)] + [("rows", 1 << b) for b in range(3, row_bits)]

    totals = received(lanes, groups)
    late = [(later[2 * o], later[2 * o + 1]) for o in range(len(orders))]
    for step in range(1, row_bits + 1):
        lanes = []
        if step < row_bits:
            lanes += [(*split(t), order[step]) for t, order in zip(totals, orders)]
        lanes += [(*pair, order[step - 1]) for pair, order in zip(late, orders)]
        groups = exchange(lanes, rows)
        flying = [g[1] for g in groups]
        if step <= len(stages):
            axis, bit = stages[step - 1]
            came = swap(packed, axis, rows if axis == "rows" else cols, bit)
            packed, came, *flying = fence((packed, came, *flying))
            packed = packed + came
        if step == len(stages) + 1:
            inverse, good = factor(after(packed, *[lane[1] for lane in lanes]))
            inverse, *flying = fence((inverse, *flying))
        groups = [(g[0], x) for g, x in zip(groups, flying)]
        if step < row_bits:
            new = received(lanes, groups)
            totals, new = new[: len(orders)], new[len(orders) :]
            late = [split(t) for t in new]
        if step == row_bits - 1:
            early = jnp.concatenate([t[0] for t in totals], axis=1)
    keeps = [lane[0] for lane in lanes]
    came = groups[0][1].reshape(len(lanes), *lanes[0][1].shape[1:])
    out = lax.cond(
        good[0] > 0,
        lambda: last(inverse, early, keeps, came),
        lambda: full_path(rows, cols, sketch, tiles, tile_user, tile_item, tile_count, item_owner, packed),
    )
    return out[None, None]


def solution(mesh):
    placed = (
        P(("rows", "cols"), None),
        P(("rows", "cols"), None, None),
        P(("rows", "cols")),
        P(("rows", "cols")),
        P(("rows", "cols")),
        P("cols", None),
    )
    return jax.shard_map(
        functools.partial(body, mesh.shape["rows"], mesh.shape["cols"]),
        mesh=mesh,
        in_specs=placed,
        out_specs=P("rows", "cols", None, None),
        check_vma=False,
    )
```

```python
import functools

import jax
import jax.numpy as jnp
from jax import lax
from jax.experimental import pallas as pl
from jax.experimental.pallas import tpu as pltpu
from jax.sharding import PartitionSpec as P

F32 = jnp.float32
BF16 = jnp.bfloat16
HIGH = lax.Precision.HIGHEST
SLOTS = 12
SPARE = 4 * 2**20
GROUP = 4
NEAR_COST = 200 * 2**20
FAR_COST = 200 * 2**20
FACTOR_COST = 200 * 2**20
LATE_ROWS = 128
NEWTON = 2


def bits_of(count):
    return [1 << b for b in reversed(range(count.bit_length() - 1))]


def swap(x, axis, count, bit):
    return lax.ppermute(x, axis, [(i, i ^ bit) for i in range(count)])


def places(order, parity):
    found = [parity << order[0]]
    for bit in reversed(order[1:]):
        found = found + [p | (1 << bit) for p in found]
    return found


def run_tiles(
    base, span, per_piece, first_col, users, items, owner, meta, tiles, slab, add, buf, sems, order
):
    count, row, col = meta[0], meta[1], meta[2]

    def relative(t):
        user = users[t]
        return lax.bitwise_xor(user // per_piece, col) - base, lax.rem(user, per_piece)

    def choose(t, n):
        piece, _ = relative(t)
        order[n] = t
        return n + jnp.where((piece >= 0) & (piece < span), 1, 0)

    live = lax.fori_loop(0, count, choose, 0)

    def fetch(i):
        slot = lax.rem(i, SLOTS)
        source = tiles.at[order[i], :, pl.ds(first_col, buf.shape[2])]
        return pltpu.make_async_copy(source, buf.at[slot], sems.at[slot])

    for i in range(SLOTS):
        @pl.when(i < live)
        def _():
            fetch(i).start()

    def group(first, size):
        for q in range(size):
            fetch(first + q).wait()
        found = []
        for q in range(size):
            piece, part = relative(order[first + q])
            both = jnp.dot(
                slab[piece * per_piece + part],
                buf[lax.rem(first + q, SLOTS)],
                preferred_element_type=F32,
            )
            half = both.shape[0] // 2
            found.append(both[:half] + both[half:])
        for q in range(size):
            add(lax.bitwise_xor(owner[items[order[first + q]]], row), found[q])
        for q in range(size):
            @pl.when(first + q + SLOTS < live)
            def _():
                fetch(first + q + SLOTS).start()

    def finish():
        groups = live // GROUP

        def many(g, _):
            group(g * GROUP, GROUP)
            return 0

        def one(i, _):
            group(i, 1)
            return 0

        lax.fori_loop(0, groups, many, 0)
        lax.fori_loop(groups * GROUP, live, one, 0)

    return finish


def split_kernel(sketch, flat, whole):
    width = flat.shape[0]
    flat[...] = sketch[...].T
    high = flat[...].astype(BF16)
    whole[:width, :] = high
    whole[width:, :] = (flat[...] - high.astype(F32)).astype(BF16)


def split_sketch(sketch):
    users, width = sketch.shape
    vmem = pl.BlockSpec(memory_space=pltpu.VMEM)
    return pl.pallas_call(
        split_kernel,
        out_shape=[
            jax.ShapeDtypeStruct((width, users), F32),
            jax.ShapeDtypeStruct((2 * width, users), BF16),
        ],
        in_specs=[vmem],
        out_specs=[vmem] * 2,
        compiler_params=pltpu.CompilerParams(vmem_limit_bytes=16 * 2**20),
    )(sketch)


def gram_kernel(flat, packed):
    n = packed.shape[1]
    top, low = flat[:n, :], flat[n:, :]
    second = mmt(low, low)
    r = lax.broadcasted_iota(jnp.int32, (n, n), 0)
    c = lax.broadcasted_iota(jnp.int32, (n, n), 1)
    packed[:n] = jnp.where(r >= c, mmt(top, top), second)
    packed[n : 2 * n] = mmt(low, top)
    tail = jnp.sum(jnp.where(r == c, second, 0.0), axis=0, keepdims=True)
    packed[2 * n :] = jnp.broadcast_to(tail, (8, n))


def packed_gram(flat):
    n = flat.shape[0] // 2
    vmem = pl.BlockSpec(memory_space=pltpu.VMEM)
    return pl.pallas_call(
        gram_kernel,
        out_shape=jax.ShapeDtypeStruct((2 * n + 8, n), F32),
        in_specs=[vmem],
        out_specs=vmem,
        compiler_params=pltpu.CompilerParams(vmem_limit_bytes=16 * 2**20),
    )(flat)


def fill(slab, pieces, per_piece):
    tile_size = slab.shape[2]
    for c, blocks in enumerate(pieces):
        first = 0
        for block in blocks:
            last = first + block.shape[0]
            for h in range(per_piece):
                slab[c * per_piece + h, first:last, :] = block[:, h * tile_size : (h + 1) * tile_size]
            first = last


def near_kernel(span, users, items, owner, meta, *refs):
    pieces = [refs[i : i + 1] for i in range(span)]
    tiles = refs[span]
    sums = refs[span + 1 : -4]
    slab, buf, sems, order = refs[-4:]
    per_piece = pieces[0][0].shape[1] // tiles.shape[1]
    width = sums[0].shape[2]

    def add(place, value):
        for o, part in enumerate(sums):
            part[place] += value[:, o * width : (o + 1) * width]

    finish = run_tiles(
        0, span, per_piece, 0, users, items, owner, meta, tiles, slab, add, buf, sems, order
    )
    for part in sums:
        part[...] = jnp.zeros_like(part)
    fill(slab, pieces, per_piece)
    finish()


def far_kernel(span, bits, first_col, users, items, owner, meta, *refs):
    blocks = (len(refs) - 9) // span
    pieces = [refs[i * blocks : (i + 1) * blocks] for i in range(span)]
    start, tiles, keep, send, slab, buf, sems, order, acc = refs[-9:]
    per_piece = pieces[0][0].shape[1] // tiles.shape[1]

    def add(place, value):
        acc[place] += value

    finish = run_tiles(
        span, span, per_piece, first_col, users, items, owner, meta, tiles, slab, add, buf, sems, order
    )
    acc[...] = start[...]
    fill(slab, pieces, per_piece)
    finish()
    for k, place in enumerate(places(bits, 0)):
        keep[k] = acc[place]
    for k, place in enumerate(places(bits, 1)):
        send[k] = acc[place].astype(BF16)


def tile_call(kernel, scalars, pieces, extra, tiles, shapes, scratch, cost):
    users = scalars[0].shape[0]
    tile_size = tiles.shape[1]
    flat = [block for blocks in pieces for block in blocks]
    count = len(pieces) * flat[0].shape[1] // tile_size
    rows = sum(block.shape[0] for block in pieces[0])
    cols = tile_size if len(shapes) == 2 and not extra else extra[0].shape[2]
    smem = pl.BlockSpec(memory_space=pltpu.SMEM)
    vmem = pl.BlockSpec(memory_space=pltpu.VMEM)
    slab = jax.ShapeDtypeStruct((count, rows, tile_size), BF16)
    buf = jax.ShapeDtypeStruct((SLOTS, tile_size, cols), BF16)
    held = sum(x.size * x.dtype.itemsize for x in (*flat, *extra, *shapes, *scratch, slab, buf))
    return pl.pallas_call(
        kernel,
        out_shape=shapes,
        in_specs=[smem] * len(scalars)
        + [vmem] * (len(flat) + len(extra))
        + [pl.BlockSpec(memory_space=pl.ANY)],
        out_specs=[vmem] * len(shapes),
        scratch_shapes=[
            pltpu.VMEM(slab.shape, BF16),
            pltpu.VMEM(buf.shape, BF16),
            pltpu.SemaphoreType.DMA((SLOTS,)),
            pltpu.SMEM((users,), jnp.int32),
        ]
        + [pltpu.VMEM(x.shape, x.dtype) for x in scratch],
        compiler_params=pltpu.CompilerParams(vmem_limit_bytes=held + SPARE),
        cost_estimate=pl.CostEstimate(flops=0, bytes_accessed=cost, transcendentals=0),
    )(*scalars, *flat, *extra, tiles)


def near_sums(scalars, pieces, tiles, rows, parts):
    tile_size = tiles.shape[1]
    width = pieces[0].shape[0] // 2
    shapes = [jax.ShapeDtypeStruct((rows, width, tile_size // parts), F32)] * parts
    return tile_call(
        functools.partial(near_kernel, len(pieces)),
        scalars,
        [[piece] for piece in pieces],
        [],
        tiles,
        shapes,
        [],
        NEAR_COST,
    )


def far_sums(scalars, pieces, start, tiles, bits, first_col):
    rows, width, cols = start.shape
    shapes = [
        jax.ShapeDtypeStruct((rows // 2, width, cols), F32),
        jax.ShapeDtypeStruct((rows // 2, width, cols), BF16),
    ]
    return tile_call(
        functools.partial(far_kernel, len(pieces), bits, first_col),
        scalars,
        pieces,
        [start],
        tiles,
        shapes,
        [jax.ShapeDtypeStruct(start.shape, F32)],
        FAR_COST,
    )


def mm(a, b):
    return lax.dot_general(a, b, (((1,), (0,)), ((), ())), precision=HIGH, preferred_element_type=F32)


def mmt(a, b):
    return lax.dot_general(a, b, (((1,), (1,)), ((), ())), precision=HIGH, preferred_element_type=F32)


def factor_kernel(packed, inverse, good):
    n = packed.shape[1]
    r = lax.broadcasted_iota(jnp.int32, (n, n), 0)
    c = lax.broadcasted_iota(jnp.int32, (n, n), 1)
    mixed = packed[:n]
    flipped = mixed.T
    side = packed[n : 2 * n]
    tail = jnp.broadcast_to(packed[2 * n : 2 * n + 1], (n, n))
    first = jnp.where(r >= c, mixed, flipped)
    second = jnp.where(r < c, mixed, jnp.where(r > c, flipped, tail))
    gram = jnp.concatenate(
        [jnp.concatenate([first, side.T], axis=1), jnp.concatenate([side, second], axis=1)], axis=0
    )
    m = 2 * n
    rr = lax.broadcasted_iota(jnp.int32, (m, m), 0)
    cc = lax.broadcasted_iota(jnp.int32, (m, m), 1)
    on = rr == cc
    eye = jnp.where(on, 1.0, 0.0).astype(F32)
    low = jnp.where(rr > cc, 1.0, jnp.where(on, 0.5, 0.0)).astype(F32)
    diag = jnp.where(on, gram, 0.0)
    scale_row = lax.rsqrt(jnp.sum(diag, axis=0, keepdims=True))
    scale_col = lax.rsqrt(jnp.sum(diag, axis=1, keepdims=True))
    unit = gram * scale_row * scale_col
    off = unit - eye
    square = jnp.dot(off, off, preferred_element_type=F32)
    spread = jnp.max(jnp.sum(jnp.abs(jnp.dot(square, square, preferred_element_type=F32)), axis=1))
    w = eye - low * off
    for _ in range(NEWTON):
        err = mmt(mm(w, unit), w) - eye
        w = w - mm(low * err, w)
    last = jnp.max(jnp.sum(jnp.abs(err), axis=1))
    inflation = jnp.max(jnp.sum(w * w, axis=0))
    inverse[...] = w * scale_row
    good[0] = jnp.where((spread < 0.025) & (last < 0.01) & (inflation < 1.1), 1, 0)


def factor(packed):
    n = packed.shape[1]
    return pl.pallas_call(
        factor_kernel,
        out_shape=[jax.ShapeDtypeStruct((2 * n, 2 * n), F32), jax.ShapeDtypeStruct((1,), jnp.int32)],
        in_specs=[pl.BlockSpec(memory_space=pltpu.VMEM)],
        out_specs=[pl.BlockSpec(memory_space=pltpu.VMEM), pl.BlockSpec(memory_space=pltpu.SMEM)],
        compiler_params=pltpu.CompilerParams(vmem_limit_bytes=24 * 2**20),
        cost_estimate=pl.CostEstimate(
            flops=0, bytes_accessed=FACTOR_COST, transcendentals=0
        ),
    )(packed)


def last_kernel(inverse, keep0, keep1, came, out):
    left = keep0[0] + came[0].astype(F32)
    right = keep1[0] + came[1].astype(F32)
    total = jnp.concatenate([left, right], axis=1)
    w = inverse[...]
    wh, th = w.astype(BF16), total.astype(BF16)
    wl = (w - wh.astype(F32)).astype(BF16)
    tl = (total - th.astype(F32)).astype(BF16)
    small = jnp.dot(wh, tl, preferred_element_type=F32) + jnp.dot(wl, th, preferred_element_type=F32)
    out[...] = jnp.dot(wh, th, preferred_element_type=F32) + small


def last(inverse, keeps, came):
    vmem = pl.BlockSpec(memory_space=pltpu.VMEM)
    return pl.pallas_call(
        last_kernel,
        out_shape=jax.ShapeDtypeStruct((inverse.shape[0], 2 * came.shape[2]), F32),
        in_specs=[vmem] * 4,
        out_specs=vmem,
        compiler_params=pltpu.CompilerParams(vmem_limit_bytes=16 * 2**20),
    )(inverse, *keeps, came)


def full_path(rows, cols, sketch, tiles, tile_user, tile_item, tile_count, item_owner, packed):
    n = packed.shape[1]
    r = lax.broadcasted_iota(jnp.int32, (n, n), 0)
    c = lax.broadcasted_iota(jnp.int32, (n, n), 1)
    mixed, side, tail = packed[:n], packed[n : 2 * n], packed[2 * n : 2 * n + 1]
    first = jnp.where(r >= c, mixed, mixed.T)
    second = jnp.where(r < c, mixed, jnp.where(r > c, mixed.T, tail))
    gram = jnp.block([[first, side.T], [side, second]])
    lower = jnp.linalg.cholesky(gram)
    basis = lax.linalg.triangular_solve(lower, sketch, left_side=False, lower=True, transpose_a=True).astype(BF16)
    have = {0: basis}
    for bit in bits_of(cols):
        for place in list(have):
            have[place | bit] = swap(have[place], "cols", cols, bit)
    slab = jnp.concatenate([have[i] for i in range(cols)], axis=0)
    col = lax.axis_index("cols")
    row = lax.axis_index("rows")
    per_piece = sketch.shape[0] // tiles.shape[2]
    owner = item_owner[0]
    tile_size = tiles.shape[2]

    def step(index, sums):
        user = tile_user[index]
        block = lax.bitwise_xor(user // per_piece, col) * per_piece + user % per_piece
        part_rows = lax.dynamic_slice_in_dim(slab, block * tile_size, tile_size, 0)
        part = lax.dot_general(part_rows, tiles[index], (((0,), (0,)), ((), ())), preferred_element_type=F32)
        place = lax.bitwise_xor(owner[tile_item[index]], row)
        now = lax.dynamic_index_in_dim(sums, place, 0, keepdims=False)
        return lax.dynamic_update_index_in_dim(sums, now + part, place, 0)

    totals = jnp.zeros((owner.shape[0], sketch.shape[1], tile_size), F32)
    totals = lax.fori_loop(0, tile_count[0], step, totals)
    for bit in bits_of(rows):
        totals = totals[:bit] + swap(totals[bit:], "rows", rows, bit)
    return totals[0]


def after(value, *others):
    return lax.optimization_barrier((value, *others))[0]


def exchange(lanes, rows):
    groups = []
    for bit in sorted({lane[2] for lane in lanes}):
        members = [i for i, lane in enumerate(lanes) if lane[2] == bit]
        sent = [lanes[i][1].reshape(-1, lanes[i][1].shape[2]) for i in members]
        groups.append((members, swap(jnp.concatenate(sent, axis=0), "rows", rows, 1 << bit)))
    return groups


def received(lanes, groups):
    got = [None] * len(lanes)
    for members, came in groups:
        first = 0
        for i in members:
            shape = lanes[i][1].shape
            size = shape[0] * shape[1]
            got[i] = came[first : first + size].reshape(shape)
            first += size
    return [lane[0] + g.astype(F32) for lane, g in zip(lanes, got)]


def split(total):
    half = total.shape[0] // 2
    return total[:half], total[half:].astype(BF16)


def body(rows, cols, sketch, tiles, tile_user, tile_item, tile_count, item_owner):
    row_bits = rows.bit_length() - 1
    first_order = tuple(range(row_bits))
    orders = (first_order, (1, 0) + first_order[2:])
    row = lax.axis_index("rows")
    col = lax.axis_index("cols")
    meta = jnp.stack([tile_count[0], row, col]).astype(jnp.int32)
    scalars = (tile_user, tile_item, item_owner[0], meta)
    far_bit, *near_bits = bits_of(cols)

    def spread(piece):
        have = {0: piece}
        for bit in near_bits:
            for place in list(have):
                have[place | bit] = swap(have[place], "cols", cols, bit)
        return [have[i] for i in range(cols // 2)]

    fence = lax.optimization_barrier
    far = far_bit
    flat, whole = split_sketch(sketch)
    near = spread(whole)
    crossed = [
        swap(part, "cols", cols, far) for part in (whole[:-LATE_ROWS], whole[-LATE_ROWS:])
    ]
    packed = packed_gram(flat)
    for bit in near_bits:
        packed = packed + swap(packed, "cols", cols, bit)
    came = swap(packed, "rows", rows, 1)
    near[0] = after(near[0], packed)
    sums = near_sums(scalars, near, tiles, rows, len(orders))
    packed, came, *sums = fence((packed, came, *sums))
    packed = packed + came
    for b in range(1, row_bits):
        packed = packed + swap(packed, "rows", rows, 1 << b)
        if b == row_bits - 1:
            _, *crossed = fence((packed, *crossed))
    parts = [spread(c) for c in crossed]
    parts[0][0] = after(parts[0][0], packed)
    pieces = list(zip(*parts))
    cut = tiles.shape[2] // len(orders)
    last_pair = far_sums(scalars, pieces, sums[1], tiles, orders[1], cut)
    came = swap(packed, "cols", cols, far)
    lanes = [(*last_pair, orders[1][0])]
    groups = exchange(lanes, rows)
    first_pair = far_sums(scalars, pieces, after(sums[0], last_pair[1]), tiles, orders[0], 0)
    packed = packed + after(came, first_pair[1])
    lanes.append((*first_pair, orders[0][0]))
    groups.append(([1], exchange(lanes[1:], rows)[0][1]))
    inverse, good = factor(after(packed, first_pair[1]))
    flying = fence((inverse, *[g[1] for g in groups]))
    inverse = flying[0]
    groups = [(g[0], x) for g, x in zip(groups, flying[1:])]
    totals = received(lanes, groups)
    for step in range(1, row_bits):
        lanes = [(*split(t), order[step]) for t, order in zip(totals, orders[::-1])]
        groups = exchange(lanes, rows)
        if step < row_bits - 1:
            totals = received(lanes, groups)
    keeps = [lane[0] for lane in lanes[::-1]]
    came = groups[0][1].reshape(len(lanes), *lanes[0][1].shape[1:])[::-1]
    out = lax.cond(
        good[0] > 0,
        lambda: last(inverse, keeps, came),
        lambda: full_path(rows, cols, sketch, tiles, tile_user, tile_item, tile_count, item_owner, packed),
    )
    return out[None, None]


def solution(mesh):
    placed = (
        P(("rows", "cols"), None),
        P(("rows", "cols"), None, None),
        P(("rows", "cols")),
        P(("rows", "cols")),
        P(("rows", "cols")),
        P("cols", None),
    )
    return jax.shard_map(
        functools.partial(body, mesh.shape["rows"], mesh.shape["cols"]),
        mesh=mesh,
        in_specs=placed,
        out_specs=P("rows", "cols", None, None),
        check_vma=False,
    )
```

```python
import functools

import jax
import jax.numpy as jnp
from jax import lax
from jax.experimental import pallas as pl
from jax.experimental.pallas import tpu as pltpu
from jax.sharding import PartitionSpec as P

F32 = jnp.float32
BF16 = jnp.bfloat16
HIGH = lax.Precision.HIGHEST
SLOTS = 12
SPARE = 4 * 2**20
GROUP = 4
NEAR_COST = 200 * 2**20
EARLY_COST = 1024
LATE_COST = 1024
FACTOR_COST = 200 * 2**20
CHUNKS = (160, 96)
NEWTON = 2


def bits_of(count):
    return [1 << b for b in reversed(range(count.bit_length() - 1))]


def swap(x, axis, count, bit):
    return lax.ppermute(x, axis, [(i, i ^ bit) for i in range(count)])


def places(order, parity):
    found = [parity << order[0]]
    for bit in reversed(order[1:]):
        found = found + [p | (1 << bit) for p in found]
    return found


def run_tiles(base, span, per_piece, users, items, owner, meta, tiles, slab, add, buf, sems, order):
    count, row, col = meta[0], meta[1], meta[2]

    def relative(t):
        user = users[t]
        return lax.bitwise_xor(user // per_piece, col) - base, lax.rem(user, per_piece)

    def choose(t, n):
        piece, _ = relative(t)
        order[n] = t
        return n + jnp.where((piece >= 0) & (piece < span), 1, 0)

    live = lax.fori_loop(0, count, choose, 0)

    def fetch(i):
        slot = lax.rem(i, SLOTS)
        return pltpu.make_async_copy(tiles.at[order[i]], buf.at[slot], sems.at[slot])

    for i in range(SLOTS):
        @pl.when(i < live)
        def _():
            fetch(i).start()

    def group(first, size):
        for q in range(size):
            fetch(first + q).wait()
        found = []
        for q in range(size):
            piece, part = relative(order[first + q])
            both = jnp.dot(
                slab[piece * per_piece + part],
                buf[lax.rem(first + q, SLOTS)],
                preferred_element_type=F32,
            )
            found.append(both)
        for q in range(size):
            add(lax.bitwise_xor(owner[items[order[first + q]]], row), found[q])
        for q in range(size):
            @pl.when(first + q + SLOTS < live)
            def _():
                fetch(first + q + SLOTS).start()

    def finish():
        groups = live // GROUP

        def many(g, _):
            group(g * GROUP, GROUP)
            return 0

        def one(i, _):
            group(i, 1)
            return 0

        lax.fori_loop(0, groups, many, 0)
        lax.fori_loop(groups * GROUP, live, one, 0)

    return finish


def split_kernel(sketch, flat, whole, chunk):
    flat[...] = sketch[...].T
    first = 0
    for kc in CHUNKS:
        rows = flat[first : first + kc, :]
        high = rows.astype(BF16)
        low = (rows - high.astype(F32)).astype(BF16)
        for i, part in enumerate((high, low)):
            start = 2 * first + i * kc
            whole[start : start + kc, :] = part
            if first == 0:
                chunk[start : start + kc, :] = part
        first += kc


def split_sketch(sketch):
    users, width = sketch.shape
    vmem = pl.BlockSpec(memory_space=pltpu.VMEM)
    return pl.pallas_call(
        split_kernel,
        out_shape=[jax.ShapeDtypeStruct((width, users), F32)]
        + [jax.ShapeDtypeStruct((2 * k, users), BF16) for k in (width, CHUNKS[0])],
        in_specs=[vmem],
        out_specs=[vmem] * 3,
        compiler_params=pltpu.CompilerParams(vmem_limit_bytes=16 * 2**20),
    )(sketch)


def gram_kernel(flat, packed):
    n = packed.shape[1]
    top, low = flat[:n, :], flat[n:, :]
    second = mmt(low, low)
    r = lax.broadcasted_iota(jnp.int32, (n, n), 0)
    c = lax.broadcasted_iota(jnp.int32, (n, n), 1)
    packed[:n] = jnp.where(r >= c, mmt(top, top), second)
    packed[n : 2 * n] = mmt(low, top)
    tail = jnp.sum(jnp.where(r == c, second, 0.0), axis=0, keepdims=True)
    packed[2 * n :] = jnp.broadcast_to(tail, (8, n))


def packed_gram(flat):
    n = flat.shape[0] // 2
    vmem = pl.BlockSpec(memory_space=pltpu.VMEM)
    return pl.pallas_call(
        gram_kernel,
        out_shape=jax.ShapeDtypeStruct((2 * n + 8, n), F32),
        in_specs=[vmem],
        out_specs=vmem,
        compiler_params=pltpu.CompilerParams(vmem_limit_bytes=16 * 2**20),
    )(flat)


def fill(slab, pieces, per_piece):
    tile_size = slab.shape[2]
    for c, piece in enumerate(pieces):
        for h in range(per_piece):
            slab[c * per_piece + h] = piece[:, h * tile_size : (h + 1) * tile_size]


def near_kernel(span, users, items, owner, meta, *refs):
    pieces = refs[:span]
    tiles = refs[span]
    sums = refs[span + 1 : -4]
    slab, buf, sems, order = refs[-4:]
    per_piece = pieces[0].shape[1] // tiles.shape[1]

    def add(place, both):
        first = 0
        for part in sums:
            kc = part.shape[1]
            part[place] += both[first : first + kc] + both[first + kc : first + 2 * kc]
            first += 2 * kc

    finish = run_tiles(
        0, span, per_piece, users, items, owner, meta, tiles, slab, add, buf, sems, order
    )
    for part in sums:
        part[...] = jnp.zeros_like(part)
    fill(slab, pieces, per_piece)
    finish()


def far_kernel(span, orders, users, items, owner, meta, *refs):
    pieces = refs[:span]
    start, tiles = refs[span], refs[span + 1]
    outs = refs[span + 2 : -5]
    slab, buf, sems, order, acc = refs[-5:]
    tile_size = tiles.shape[1]
    per_piece = pieces[0].shape[1] // tile_size
    kc = pieces[0].shape[0] // 2

    def add(place, both):
        acc[place] += both[:kc] + both[kc:]

    finish = run_tiles(
        span, span, per_piece, users, items, owner, meta, tiles, slab, add, buf, sems, order
    )
    acc[...] = start[...]
    fill(slab, pieces, per_piece)
    finish()
    width = tile_size // len(orders)
    for o, bits in enumerate(orders):
        cut = slice(o * width, (o + 1) * width)
        for k, place in enumerate(places(bits, 0)):
            outs[2 * o][k] = acc[place, :, cut]
        for k, place in enumerate(places(bits, 1)):
            outs[2 * o + 1][k] = acc[place, :, cut].astype(BF16)


def tile_call(kernel, scalars, pieces, extra, tiles, shapes, scratch, cost):
    users = scalars[0].shape[0]
    tile_size = tiles.shape[1]
    blocks = len(pieces) * pieces[0].shape[1] // tile_size
    smem = pl.BlockSpec(memory_space=pltpu.SMEM)
    vmem = pl.BlockSpec(memory_space=pltpu.VMEM)
    slab = jax.ShapeDtypeStruct((blocks, pieces[0].shape[0], tile_size), BF16)
    buf = jax.ShapeDtypeStruct((SLOTS, tile_size, tile_size), BF16)
    held = sum(x.size * x.dtype.itemsize for x in (*pieces, *extra, *shapes, *scratch, slab, buf))
    return pl.pallas_call(
        kernel,
        out_shape=shapes,
        in_specs=[smem] * len(scalars)
        + [vmem] * (len(pieces) + len(extra))
        + [pl.BlockSpec(memory_space=pl.ANY)],
        out_specs=[vmem] * len(shapes),
        scratch_shapes=[
            pltpu.VMEM(slab.shape, BF16),
            pltpu.VMEM(buf.shape, BF16),
            pltpu.SemaphoreType.DMA((SLOTS,)),
            pltpu.SMEM((users,), jnp.int32),
        ]
        + [pltpu.VMEM(x.shape, x.dtype) for x in scratch],
        compiler_params=pltpu.CompilerParams(vmem_limit_bytes=held + SPARE),
        cost_estimate=pl.CostEstimate(flops=0, bytes_accessed=cost, transcendentals=0),
    )(*scalars, *pieces, *extra, tiles)


def near_sums(scalars, pieces, tiles, rows):
    tile_size = tiles.shape[1]
    shapes = [jax.ShapeDtypeStruct((rows, kc, tile_size), F32) for kc in CHUNKS]
    return tile_call(
        functools.partial(near_kernel, len(pieces)), scalars, pieces, [], tiles, shapes, [], NEAR_COST
    )


def far_sums(scalars, pieces, start, tiles, orders, cost):
    rows, kc, tile_size = start.shape
    width = tile_size // len(orders)
    shapes = []
    for _ in orders:
        shapes.append(jax.ShapeDtypeStruct((rows // 2, kc, width), F32))
        shapes.append(jax.ShapeDtypeStruct((rows // 2, kc, width), BF16))
    return tile_call(
        functools.partial(far_kernel, len(pieces), orders),
        scalars,
        pieces,
        [start],
        tiles,
        shapes,
        [jax.ShapeDtypeStruct(start.shape, F32)],
        cost,
    )


def mm(a, b):
    return lax.dot_general(a, b, (((1,), (0,)), ((), ())), precision=HIGH, preferred_element_type=F32)


def mmt(a, b):
    return lax.dot_general(a, b, (((1,), (1,)), ((), ())), precision=HIGH, preferred_element_type=F32)


def factor_kernel(packed, inverse, good):
    n = packed.shape[1]
    r = lax.broadcasted_iota(jnp.int32, (n, n), 0)
    c = lax.broadcasted_iota(jnp.int32, (n, n), 1)
    mixed = packed[:n]
    flipped = mixed.T
    side = packed[n : 2 * n]
    tail = jnp.broadcast_to(packed[2 * n : 2 * n + 1], (n, n))
    first = jnp.where(r >= c, mixed, flipped)
    second = jnp.where(r < c, mixed, jnp.where(r > c, flipped, tail))
    gram = jnp.concatenate(
        [jnp.concatenate([first, side.T], axis=1), jnp.concatenate([side, second], axis=1)], axis=0
    )
    m = 2 * n
    rr = lax.broadcasted_iota(jnp.int32, (m, m), 0)
    cc = lax.broadcasted_iota(jnp.int32, (m, m), 1)
    on = rr == cc
    eye = jnp.where(on, 1.0, 0.0).astype(F32)
    low = jnp.where(rr > cc, 1.0, jnp.where(on, 0.5, 0.0)).astype(F32)
    diag = jnp.where(on, gram, 0.0)
    scale_row = lax.rsqrt(jnp.sum(diag, axis=0, keepdims=True))
    scale_col = lax.rsqrt(jnp.sum(diag, axis=1, keepdims=True))
    unit = gram * scale_row * scale_col
    off = unit - eye
    square = jnp.dot(off, off, preferred_element_type=F32)
    spread = jnp.max(jnp.sum(jnp.abs(jnp.dot(square, square, preferred_element_type=F32)), axis=1))
    w = eye - low * off
    for _ in range(NEWTON):
        err = mmt(mm(w, unit), w) - eye
        w = w - mm(low * err, w)
    last = jnp.max(jnp.sum(jnp.abs(err), axis=1))
    inflation = jnp.max(jnp.sum(w * w, axis=0))
    inverse[...] = w * scale_row
    good[0] = jnp.where((spread < 0.025) & (last < 0.01) & (inflation < 1.1), 1, 0)


def factor(packed):
    n = packed.shape[1]
    return pl.pallas_call(
        factor_kernel,
        out_shape=[jax.ShapeDtypeStruct((2 * n, 2 * n), F32), jax.ShapeDtypeStruct((1,), jnp.int32)],
        in_specs=[pl.BlockSpec(memory_space=pltpu.VMEM)],
        out_specs=[pl.BlockSpec(memory_space=pltpu.VMEM), pl.BlockSpec(memory_space=pltpu.SMEM)],
        compiler_params=pltpu.CompilerParams(vmem_limit_bytes=24 * 2**20),
        cost_estimate=pl.CostEstimate(
            flops=0, bytes_accessed=FACTOR_COST, transcendentals=0
        ),
    )(packed)


def last_kernel(inverse, early, keep0, keep1, came, out):
    left = keep0[0] + came[0].astype(F32)
    right = keep1[0] + came[1].astype(F32)
    total = jnp.concatenate([early[...], jnp.concatenate([left, right], axis=1)], axis=0)
    w = inverse[...]
    wh, th = w.astype(BF16), total.astype(BF16)
    wl = (w - wh.astype(F32)).astype(BF16)
    tl = (total - th.astype(F32)).astype(BF16)
    small = jnp.dot(wh, tl, preferred_element_type=F32) + jnp.dot(wl, th, preferred_element_type=F32)
    out[...] = jnp.dot(wh, th, preferred_element_type=F32) + small


def last(inverse, early, keeps, came):
    vmem = pl.BlockSpec(memory_space=pltpu.VMEM)
    return pl.pallas_call(
        last_kernel,
        out_shape=jax.ShapeDtypeStruct((inverse.shape[0], early.shape[1]), F32),
        in_specs=[vmem] * 5,
        out_specs=vmem,
        compiler_params=pltpu.CompilerParams(vmem_limit_bytes=16 * 2**20),
    )(inverse, early, *keeps, came)


def full_path(rows, cols, sketch, tiles, tile_user, tile_item, tile_count, item_owner, packed):
    n = packed.shape[1]
    r = lax.broadcasted_iota(jnp.int32, (n, n), 0)
    c = lax.broadcasted_iota(jnp.int32, (n, n), 1)
    mixed, side, tail = packed[:n], packed[n : 2 * n], packed[2 * n : 2 * n + 1]
    first = jnp.where(r >= c, mixed, mixed.T)
    second = jnp.where(r < c, mixed, jnp.where(r > c, mixed.T, tail))
    gram = jnp.block([[first, side.T], [side, second]])
    lower = jnp.linalg.cholesky(gram)
    basis = lax.linalg.triangular_solve(lower, sketch, left_side=False, lower=True, transpose_a=True).astype(BF16)
    have = {0: basis}
    for bit in bits_of(cols):
        for place in list(have):
            have[place | bit] = swap(have[place], "cols", cols, bit)
    slab = jnp.concatenate([have[i] for i in range(cols)], axis=0)
    col = lax.axis_index("cols")
    row = lax.axis_index("rows")
    per_piece = sketch.shape[0] // tiles.shape[2]
    owner = item_owner[0]
    tile_size = tiles.shape[2]

    def step(index, sums):
        user = tile_user[index]
        block = lax.bitwise_xor(user // per_piece, col) * per_piece + user % per_piece
        part_rows = lax.dynamic_slice_in_dim(slab, block * tile_size, tile_size, 0)
        part = lax.dot_general(part_rows, tiles[index], (((0,), (0,)), ((), ())), preferred_element_type=F32)
        place = lax.bitwise_xor(owner[tile_item[index]], row)
        now = lax.dynamic_index_in_dim(sums, place, 0, keepdims=False)
        return lax.dynamic_update_index_in_dim(sums, now + part, place, 0)

    totals = jnp.zeros((owner.shape[0], sketch.shape[1], tile_size), F32)
    totals = lax.fori_loop(0, tile_count[0], step, totals)
    for bit in bits_of(rows):
        totals = totals[:bit] + swap(totals[bit:], "rows", rows, bit)
    return totals[0]


def after(value, *others):
    return lax.optimization_barrier((value, *others))[0]


def exchange(lanes, rows):
    groups = []
    for bit in sorted({lane[2] for lane in lanes}):
        members = [i for i, lane in enumerate(lanes) if lane[2] == bit]
        sent = [lanes[i][1].reshape(-1, lanes[i][1].shape[2]) for i in members]
        groups.append((members, swap(jnp.concatenate(sent, axis=0), "rows", rows, 1 << bit)))
    return groups


def received(lanes, groups):
    got = [None] * len(lanes)
    for members, came in groups:
        first = 0
        for i in members:
            shape = lanes[i][1].shape
            size = shape[0] * shape[1]
            got[i] = came[first : first + size].reshape(shape)
            first += size
    return [lane[0] + g.astype(F32) for lane, g in zip(lanes, got)]


def split(total):
    half = total.shape[0] // 2
    return total[:half], total[half:].astype(BF16)


def body(rows, cols, sketch, tiles, tile_user, tile_item, tile_count, item_owner):
    row_bits = rows.bit_length() - 1
    first_order = tuple(range(row_bits))
    orders = (first_order, (1, 0) + first_order[2:])
    row = lax.axis_index("rows")
    col = lax.axis_index("cols")
    meta = jnp.stack([tile_count[0], row, col]).astype(jnp.int32)
    scalars = (tile_user, tile_item, item_owner[0], meta)
    far_bit, *near_bits = bits_of(cols)

    def spread(piece):
        have = {0: piece}
        for bit in near_bits:
            for place in list(have):
                have[place | bit] = swap(have[place], "cols", cols, bit)
        return [have[i] for i in range(cols // 2)]

    fence = lax.optimization_barrier
    far = far_bit
    flat, whole, chunk = split_sketch(sketch)
    near = spread(whole)
    crossed = [swap(chunk, "cols", cols, far), swap(whole[2 * CHUNKS[0] :], "cols", cols, far)]
    packed = packed_gram(flat)
    for bit in near_bits:
        packed = packed + swap(packed, "cols", cols, bit)
    came = swap(packed, "rows", rows, 1)
    near[0] = after(near[0], packed)
    sums = near_sums(scalars, near, tiles, rows)
    packed, came, *sums = fence((packed, came, *sums))
    packed = packed + came
    came = swap(packed, "rows", rows, 2)
    crossed[0] = after(crossed[0], packed)
    outs = far_sums(scalars, spread(crossed[0]), sums[0], tiles, orders, EARLY_COST)
    packed, came, *outs = fence((packed, came, *outs))
    packed = packed + came
    came = swap(packed, "rows", rows, 4)
    lanes = [(outs[2 * o], outs[2 * o + 1], order[0]) for o, order in enumerate(orders)]
    groups = exchange(lanes, rows)
    crossed[1] = after(crossed[1], packed)
    later = far_sums(scalars, spread(crossed[1]), sums[1], tiles, orders, LATE_COST)
    flying = [g[1] for g in groups]
    packed, came, *rest = fence((packed, came, *flying, *later))
    groups = [(g[0], x) for g, x in zip(groups, rest)]
    later = rest[len(groups) :]
    packed = packed + came
    stages = [("cols", far)] + [("rows", 1 << b) for b in range(3, row_bits)]

    totals = received(lanes, groups)
    late = [(later[2 * o], later[2 * o + 1]) for o in range(len(orders))]
    for step in range(1, row_bits + 1):
        lanes = []
        if step < row_bits:
            lanes += [(*split(t), order[step]) for t, order in zip(totals, orders)]
        lanes += [(*pair, order[step - 1]) for pair, order in zip(late, orders)]
        groups = exchange(lanes, rows)
        flying = [g[1] for g in groups]
        if step <= len(stages):
            axis, bit = stages[step - 1]
            came = swap(packed, axis, rows if axis == "rows" else cols, bit)
            packed, came, *flying = fence((packed, came, *flying))
            packed = packed + came
        if step == len(stages) + 1:
            inverse, good = factor(after(packed, *[lane[1] for lane in lanes]))
            inverse, *flying = fence((inverse, *flying))
        groups = [(g[0], x) for g, x in zip(groups, flying)]
        if step < row_bits:
            new = received(lanes, groups)
            totals, new = new[: len(orders)], new[len(orders) :]
            late = [split(t) for t in new]
        if step == row_bits - 1:
            early = jnp.concatenate([t[0] for t in totals], axis=1)
    keeps = [lane[0] for lane in lanes]
    came = groups[0][1].reshape(len(lanes), *lanes[0][1].shape[1:])
    out = lax.cond(
        good[0] > 0,
        lambda: last(inverse, early, keeps, came),
        lambda: full_path(rows, cols, sketch, tiles, tile_user, tile_item, tile_count, item_owner, packed),
    )
    return out[None, None]


def solution(mesh):
    placed = (
        P(("rows", "cols"), None),
        P(("rows", "cols"), None, None),
        P(("rows", "cols")),
        P(("rows", "cols")),
        P(("rows", "cols")),
        P("cols", None),
    )
    return jax.shard_map(
        functools.partial(body, mesh.shape["rows"], mesh.shape["cols"]),
        mesh=mesh,
        in_specs=placed,
        out_specs=P("rows", "cols", None, None),
        check_vma=False,
    )
```

```python
import functools

import jax
import jax.numpy as jnp
from jax import lax
from jax.experimental import pallas as pl
from jax.experimental.pallas import tpu as pltpu
from jax.sharding import PartitionSpec as P

F32 = jnp.float32
BF16 = jnp.bfloat16
HIGH = lax.Precision.HIGHEST
SLOTS = 12
SPARE = 4 * 2**20
GROUP = 4
NEAR_COST = 200 * 2**20
EARLY_COST = 1024
LATE_COST = 1024
FACTOR_COST = 200 * 2**20
CHUNKS = (160, 96)
NEWTON = 2


def bits_of(count):
    return [1 << b for b in reversed(range(count.bit_length() - 1))]


def swap(x, axis, count, bit):
    return lax.ppermute(x, axis, [(i, i ^ bit) for i in range(count)])


def places(order, parity):
    found = [parity << order[0]]
    for bit in reversed(order[1:]):
        found = found + [p | (1 << bit) for p in found]
    return found


def run_tiles(base, span, per_piece, users, items, owner, meta, tiles, slab, add, buf, sems, order):
    count, row, col = meta[0], meta[1], meta[2]

    def relative(t):
        user = users[t]
        return lax.bitwise_xor(user // per_piece, col) - base, lax.rem(user, per_piece)

    def choose(t, n):
        piece, _ = relative(t)
        order[n] = t
        return n + jnp.where((piece >= 0) & (piece < span), 1, 0)

    live = lax.fori_loop(0, count, choose, 0)

    def fetch(i):
        slot = lax.rem(i, SLOTS)
        return pltpu.make_async_copy(tiles.at[order[i]], buf.at[slot], sems.at[slot])

    for i in range(SLOTS):
        @pl.when(i < live)
        def _():
            fetch(i).start()

    def group(first, size):
        for q in range(size):
            fetch(first + q).wait()
        found = []
        for q in range(size):
            piece, part = relative(order[first + q])
            both = jnp.dot(
                slab[piece * per_piece + part],
                buf[lax.rem(first + q, SLOTS)],
                preferred_element_type=F32,
            )
            found.append(both)
        for q in range(size):
            add(lax.bitwise_xor(owner[items[order[first + q]]], row), found[q])
        for q in range(size):
            @pl.when(first + q + SLOTS < live)
            def _():
                fetch(first + q + SLOTS).start()

    def finish():
        groups = live // GROUP

        def many(g, _):
            group(g * GROUP, GROUP)
            return 0

        def one(i, _):
            group(i, 1)
            return 0

        lax.fori_loop(0, groups, many, 0)
        lax.fori_loop(groups * GROUP, live, one, 0)

    return finish


def split_kernel(sketch, flat, whole, chunk):
    flat[...] = sketch[...].T
    first = 0
    for kc in CHUNKS:
        rows = flat[first : first + kc, :]
        high = rows.astype(BF16)
        low = (rows - high.astype(F32)).astype(BF16)
        for i, part in enumerate((high, low)):
            start = 2 * first + i * kc
            whole[start : start + kc, :] = part
            if first == 0:
                chunk[start : start + kc, :] = part
        first += kc


def split_sketch(sketch):
    users, width = sketch.shape
    vmem = pl.BlockSpec(memory_space=pltpu.VMEM)
    return pl.pallas_call(
        split_kernel,
        out_shape=[jax.ShapeDtypeStruct((width, users), F32)]
        + [jax.ShapeDtypeStruct((2 * k, users), BF16) for k in (width, CHUNKS[0])],
        in_specs=[vmem],
        out_specs=[vmem] * 3,
        compiler_params=pltpu.CompilerParams(vmem_limit_bytes=16 * 2**20),
    )(sketch)


def gram_kernel(flat, packed):
    n = packed.shape[1]
    top, low = flat[:n, :], flat[n:, :]
    second = mmt(low, low)
    r = lax.broadcasted_iota(jnp.int32, (n, n), 0)
    c = lax.broadcasted_iota(jnp.int32, (n, n), 1)
    packed[:n] = jnp.where(r >= c, mmt(top, top), second)
    packed[n : 2 * n] = mmt(low, top)
    tail = jnp.sum(jnp.where(r == c, second, 0.0), axis=0, keepdims=True)
    packed[2 * n :] = jnp.broadcast_to(tail, (8, n))


def packed_gram(flat):
    n = flat.shape[0] // 2
    vmem = pl.BlockSpec(memory_space=pltpu.VMEM)
    return pl.pallas_call(
        gram_kernel,
        out_shape=jax.ShapeDtypeStruct((2 * n + 8, n), F32),
        in_specs=[vmem],
        out_specs=vmem,
        compiler_params=pltpu.CompilerParams(vmem_limit_bytes=16 * 2**20),
    )(flat)


def fill(slab, pieces, per_piece):
    tile_size = slab.shape[2]
    for c, piece in enumerate(pieces):
        for h in range(per_piece):
            slab[c * per_piece + h] = piece[:, h * tile_size : (h + 1) * tile_size]


def near_kernel(span, users, items, owner, meta, *refs):
    pieces = refs[:span]
    tiles = refs[span]
    sums = refs[span + 1 : -4]
    slab, buf, sems, order = refs[-4:]
    per_piece = pieces[0].shape[1] // tiles.shape[1]

    def add(place, both):
        first = 0
        for part in sums:
            kc = part.shape[1]
            part[place] += both[first : first + kc] + both[first + kc : first + 2 * kc]
            first += 2 * kc

    finish = run_tiles(
        0, span, per_piece, users, items, owner, meta, tiles, slab, add, buf, sems, order
    )
    for part in sums:
        part[...] = jnp.zeros_like(part)
    fill(slab, pieces, per_piece)
    finish()


def far_kernel(span, orders, users, items, owner, meta, *refs):
    pieces = refs[:span]
    start, tiles = refs[span], refs[span + 1]
    outs = refs[span + 2 : -5]
    slab, buf, sems, order, acc = refs[-5:]
    tile_size = tiles.shape[1]
    per_piece = pieces[0].shape[1] // tile_size
    kc = pieces[0].shape[0] // 2

    def add(place, both):
        acc[place] += both[:kc] + both[kc:]

    finish = run_tiles(
        span, span, per_piece, users, items, owner, meta, tiles, slab, add, buf, sems, order
    )
    acc[...] = start[...]
    fill(slab, pieces, per_piece)
    finish()
    width = tile_size // len(orders)
    for o, bits in enumerate(orders):
        cut = slice(o * width, (o + 1) * width)
        for k, place in enumerate(places(bits, 0)):
            outs[2 * o][k] = acc[place, :, cut]
        for k, place in enumerate(places(bits, 1)):
            outs[2 * o + 1][k] = acc[place, :, cut].astype(BF16)


def tile_call(kernel, scalars, pieces, extra, tiles, shapes, scratch, cost):
    users = scalars[0].shape[0]
    tile_size = tiles.shape[1]
    blocks = len(pieces) * pieces[0].shape[1] // tile_size
    smem = pl.BlockSpec(memory_space=pltpu.SMEM)
    vmem = pl.BlockSpec(memory_space=pltpu.VMEM)
    slab = jax.ShapeDtypeStruct((blocks, pieces[0].shape[0], tile_size), BF16)
    buf = jax.ShapeDtypeStruct((SLOTS, tile_size, tile_size), BF16)
    held = sum(x.size * x.dtype.itemsize for x in (*pieces, *extra, *shapes, *scratch, slab, buf))
    return pl.pallas_call(
        kernel,
        out_shape=shapes,
        in_specs=[smem] * len(scalars)
        + [vmem] * (len(pieces) + len(extra))
        + [pl.BlockSpec(memory_space=pl.ANY)],
        out_specs=[vmem] * len(shapes),
        scratch_shapes=[
            pltpu.VMEM(slab.shape, BF16),
            pltpu.VMEM(buf.shape, BF16),
            pltpu.SemaphoreType.DMA((SLOTS,)),
            pltpu.SMEM((users,), jnp.int32),
        ]
        + [pltpu.VMEM(x.shape, x.dtype) for x in scratch],
        compiler_params=pltpu.CompilerParams(vmem_limit_bytes=held + SPARE),
        cost_estimate=pl.CostEstimate(flops=0, bytes_accessed=cost, transcendentals=0),
    )(*scalars, *pieces, *extra, tiles)


def near_sums(scalars, pieces, tiles, rows):
    tile_size = tiles.shape[1]
    shapes = [jax.ShapeDtypeStruct((rows, kc, tile_size), F32) for kc in CHUNKS]
    return tile_call(
        functools.partial(near_kernel, len(pieces)), scalars, pieces, [], tiles, shapes, [], NEAR_COST
    )


def far_sums(scalars, pieces, start, tiles, orders, cost):
    rows, kc, tile_size = start.shape
    width = tile_size // len(orders)
    shapes = []
    for _ in orders:
        shapes.append(jax.ShapeDtypeStruct((rows // 2, kc, width), F32))
        shapes.append(jax.ShapeDtypeStruct((rows // 2, kc, width), BF16))
    return tile_call(
        functools.partial(far_kernel, len(pieces), orders),
        scalars,
        pieces,
        [start],
        tiles,
        shapes,
        [jax.ShapeDtypeStruct(start.shape, F32)],
        cost,
    )


def mm(a, b):
    return lax.dot_general(a, b, (((1,), (0,)), ((), ())), precision=HIGH, preferred_element_type=F32)


def mmt(a, b):
    return lax.dot_general(a, b, (((1,), (1,)), ((), ())), precision=HIGH, preferred_element_type=F32)


def factor_kernel(packed, inverse, good):
    n = packed.shape[1]
    r = lax.broadcasted_iota(jnp.int32, (n, n), 0)
    c = lax.broadcasted_iota(jnp.int32, (n, n), 1)
    mixed = packed[:n]
    flipped = mixed.T
    side = packed[n : 2 * n]
    tail = jnp.broadcast_to(packed[2 * n : 2 * n + 1], (n, n))
    first = jnp.where(r >= c, mixed, flipped)
    second = jnp.where(r < c, mixed, jnp.where(r > c, flipped, tail))
    gram = jnp.concatenate(
        [jnp.concatenate([first, side.T], axis=1), jnp.concatenate([side, second], axis=1)], axis=0
    )
    m = 2 * n
    rr = lax.broadcasted_iota(jnp.int32, (m, m), 0)
    cc = lax.broadcasted_iota(jnp.int32, (m, m), 1)
    on = rr == cc
    eye = jnp.where(on, 1.0, 0.0).astype(F32)
    low = jnp.where(rr > cc, 1.0, jnp.where(on, 0.5, 0.0)).astype(F32)
    diag = jnp.where(on, gram, 0.0)
    scale_row = lax.rsqrt(jnp.sum(diag, axis=0, keepdims=True))
    scale_col = lax.rsqrt(jnp.sum(diag, axis=1, keepdims=True))
    unit = gram * scale_row * scale_col
    off = unit - eye
    square = jnp.dot(off, off, preferred_element_type=F32)
    spread = jnp.max(jnp.sum(jnp.abs(jnp.dot(square, square, preferred_element_type=F32)), axis=1))
    w = eye - low * off
    for _ in range(NEWTON):
        err = mmt(mm(w, unit), w) - eye
        w = w - mm(low * err, w)
    last = jnp.max(jnp.sum(jnp.abs(err), axis=1))
    inflation = jnp.max(jnp.sum(w * w, axis=0))
    inverse[...] = w * scale_row
    good[0] = jnp.where((spread < 0.025) & (last < 0.01) & (inflation < 1.1), 1, 0)


def factor(packed):
    n = packed.shape[1]
    return pl.pallas_call(
        factor_kernel,
        out_shape=[jax.ShapeDtypeStruct((2 * n, 2 * n), F32), jax.ShapeDtypeStruct((1,), jnp.int32)],
        in_specs=[pl.BlockSpec(memory_space=pltpu.VMEM)],
        out_specs=[pl.BlockSpec(memory_space=pltpu.VMEM), pl.BlockSpec(memory_space=pltpu.SMEM)],
        compiler_params=pltpu.CompilerParams(vmem_limit_bytes=24 * 2**20),
        cost_estimate=pl.CostEstimate(
            flops=0, bytes_accessed=FACTOR_COST, transcendentals=0
        ),
    )(packed)


def last_kernel(inverse, early, keep0, keep1, came, out):
    left = keep0[0] + came[0].astype(F32)
    right = keep1[0] + came[1].astype(F32)
    total = jnp.concatenate([early[...], jnp.concatenate([left, right], axis=1)], axis=0)
    w = inverse[...]
    wh, th = w.astype(BF16), total.astype(BF16)
    wl = (w - wh.astype(F32)).astype(BF16)
    tl = (total - th.astype(F32)).astype(BF16)
    small = jnp.dot(wh, tl, preferred_element_type=F32) + jnp.dot(wl, th, preferred_element_type=F32)
    out[...] = jnp.dot(wh, th, preferred_element_type=F32) + small


def last(inverse, early, keeps, came):
    vmem = pl.BlockSpec(memory_space=pltpu.VMEM)
    return pl.pallas_call(
        last_kernel,
        out_shape=jax.ShapeDtypeStruct((inverse.shape[0], early.shape[1]), F32),
        in_specs=[vmem] * 5,
        out_specs=vmem,
        compiler_params=pltpu.CompilerParams(vmem_limit_bytes=16 * 2**20),
    )(inverse, early, *keeps, came)


def full_path(rows, cols, sketch, tiles, tile_user, tile_item, tile_count, item_owner, packed):
    n = packed.shape[1]
    r = lax.broadcasted_iota(jnp.int32, (n, n), 0)
    c = lax.broadcasted_iota(jnp.int32, (n, n), 1)
    mixed, side, tail = packed[:n], packed[n : 2 * n], packed[2 * n : 2 * n + 1]
    first = jnp.where(r >= c, mixed, mixed.T)
    second = jnp.where(r < c, mixed, jnp.where(r > c, mixed.T, tail))
    gram = jnp.block([[first, side.T], [side, second]])
    lower = jnp.linalg.cholesky(gram)
    basis = lax.linalg.triangular_solve(lower, sketch, left_side=False, lower=True, transpose_a=True).astype(BF16)
    have = {0: basis}
    for bit in bits_of(cols):
        for place in list(have):
            have[place | bit] = swap(have[place], "cols", cols, bit)
    slab = jnp.concatenate([have[i] for i in range(cols)], axis=0)
    col = lax.axis_index("cols")
    row = lax.axis_index("rows")
    per_piece = sketch.shape[0] // tiles.shape[2]
    owner = item_owner[0]
    tile_size = tiles.shape[2]

    def step(index, sums):
        user = tile_user[index]
        block = lax.bitwise_xor(user // per_piece, col) * per_piece + user % per_piece
        part_rows = lax.dynamic_slice_in_dim(slab, block * tile_size, tile_size, 0)
        part = lax.dot_general(part_rows, tiles[index], (((0,), (0,)), ((), ())), preferred_element_type=F32)
        place = lax.bitwise_xor(owner[tile_item[index]], row)
        now = lax.dynamic_index_in_dim(sums, place, 0, keepdims=False)
        return lax.dynamic_update_index_in_dim(sums, now + part, place, 0)

    totals = jnp.zeros((owner.shape[0], sketch.shape[1], tile_size), F32)
    totals = lax.fori_loop(0, tile_count[0], step, totals)
    for bit in bits_of(rows):
        totals = totals[:bit] + swap(totals[bit:], "rows", rows, bit)
    return totals[0]


def after(value, *others):
    return lax.optimization_barrier((value, *others))[0]


def exchange(lanes, rows):
    groups = []
    for bit in sorted({lane[2] for lane in lanes}):
        members = [i for i, lane in enumerate(lanes) if lane[2] == bit]
        sent = [lanes[i][1].reshape(-1, lanes[i][1].shape[2]) for i in members]
        groups.append((members, swap(jnp.concatenate(sent, axis=0), "rows", rows, 1 << bit)))
    return groups


def received(lanes, groups):
    got = [None] * len(lanes)
    for members, came in groups:
        first = 0
        for i in members:
            shape = lanes[i][1].shape
            size = shape[0] * shape[1]
            got[i] = came[first : first + size].reshape(shape)
            first += size
    return [lane[0] + g.astype(F32) for lane, g in zip(lanes, got)]


def split(total):
    half = total.shape[0] // 2
    return total[:half], total[half:].astype(BF16)


def body(rows, cols, sketch, tiles, tile_user, tile_item, tile_count, item_owner):
    row_bits = rows.bit_length() - 1
    first_order = tuple(range(row_bits))
    orders = (first_order, (1, 0) + first_order[2:])
    row = lax.axis_index("rows")
    col = lax.axis_index("cols")
    meta = jnp.stack([tile_count[0], row, col]).astype(jnp.int32)
    scalars = (tile_user, tile_item, item_owner[0], meta)
    far_bit, *near_bits = bits_of(cols)

    def spread(piece):
        have = {0: piece}
        for bit in near_bits:
            for place in list(have):
                have[place | bit] = swap(have[place], "cols", cols, bit)
        return [have[i] for i in range(cols // 2)]

    fence = lax.optimization_barrier
    far = far_bit
    flat, whole, chunk = split_sketch(sketch)
    near = spread(whole)
    crossed = [swap(chunk, "cols", cols, far), swap(whole[2 * CHUNKS[0] :], "cols", cols, far)]
    packed = packed_gram(flat)
    for bit in near_bits:
        packed = packed + swap(packed, "cols", cols, bit)
    came = swap(packed, "rows", rows, 1)
    near[0] = after(near[0], packed)
    sums = near_sums(scalars, near, tiles, rows)
    packed, came, *sums = fence((packed, came, *sums))
    packed = packed + came
    packed = packed + swap(packed, "rows", rows, 2)
    came = swap(packed, "rows", rows, 4)
    crossed[0] = after(crossed[0], packed)
    outs = far_sums(scalars, spread(crossed[0]), sums[0], tiles, orders, EARLY_COST)
    packed, came, *outs = fence((packed, came, *outs))
    packed = packed + came
    lanes = [(outs[2 * o], outs[2 * o + 1], order[0]) for o, order in enumerate(orders)]
    groups = exchange(lanes, rows)
    crossed[1] = after(crossed[1], packed)
    later = far_sums(scalars, spread(crossed[1]), sums[1], tiles, orders, LATE_COST)
    flying = [g[1] for g in groups]
    rest = fence((*flying, *later))
    groups = [(g[0], x) for g, x in zip(groups, rest)]
    later = rest[len(groups) :]
    stages = [("cols", far)] + [("rows", 1 << b) for b in range(3, row_bits)]

    totals = received(lanes, groups)
    late = [(later[2 * o], later[2 * o + 1]) for o in range(len(orders))]
    for step in range(1, row_bits + 1):
        lanes = []
        if step < row_bits:
            lanes += [(*split(t), order[step]) for t, order in zip(totals, orders)]
        lanes += [(*pair, order[step - 1]) for pair, order in zip(late, orders)]
        groups = exchange(lanes, rows)
        flying = [g[1] for g in groups]
        if step <= len(stages):
            axis, bit = stages[step - 1]
            came = swap(packed, axis, rows if axis == "rows" else cols, bit)
            if step < len(stages):
                packed, came, *flying = fence((packed, came, *flying))
                packed = packed + came
            else:
                packed = packed + came
                inverse, good = factor(after(packed, *[lane[1] for lane in lanes]))
                inverse, *flying = fence((inverse, *flying))
        groups = [(g[0], x) for g, x in zip(groups, flying)]
        if step < row_bits:
            new = received(lanes, groups)
            totals, new = new[: len(orders)], new[len(orders) :]
            late = [split(t) for t in new]
        if step == row_bits - 1:
            early = jnp.concatenate([t[0] for t in totals], axis=1)
    keeps = [lane[0] for lane in lanes]
    came = groups[0][1].reshape(len(lanes), *lanes[0][1].shape[1:])
    out = lax.cond(
        good[0] > 0,
        lambda: last(inverse, early, keeps, came),
        lambda: full_path(rows, cols, sketch, tiles, tile_user, tile_item, tile_count, item_owner, packed),
    )
    return out[None, None]


def solution(mesh):
    placed = (
        P(("rows", "cols"), None),
        P(("rows", "cols"), None, None),
        P(("rows", "cols")),
        P(("rows", "cols")),
        P(("rows", "cols")),
        P("cols", None),
    )
    return jax.shard_map(
        functools.partial(body, mesh.shape["rows"], mesh.shape["cols"]),
        mesh=mesh,
        in_specs=placed,
        out_specs=P("rows", "cols", None, None),
        check_vma=False,
    )
```

```python
import functools

import jax
import jax.numpy as jnp
from jax import lax
from jax.experimental import pallas as pl
from jax.experimental.pallas import tpu as pltpu
from jax.sharding import PartitionSpec as P

F32 = jnp.float32
BF16 = jnp.bfloat16
HIGH = lax.Precision.HIGHEST
SLOTS = 12
SPARE = 4 * 2**20
GROUP = 4
NEAR_COST = 200 * 2**20
EARLY_COST = 1024
LATE_COST = 1024
FACTOR_COST = 200 * 2**20
CHUNKS = (160, 96)
NEWTON = 2


def bits_of(count):
    return [1 << b for b in reversed(range(count.bit_length() - 1))]


def swap(x, axis, count, bit):
    return lax.ppermute(x, axis, [(i, i ^ bit) for i in range(count)])


def places(order, parity):
    found = [parity << order[0]]
    for bit in reversed(order[1:]):
        found = found + [p | (1 << bit) for p in found]
    return found


def run_tiles(base, span, per_piece, users, items, owner, meta, tiles, slab, add, buf, sems, order):
    count, row, col = meta[0], meta[1], meta[2]

    def relative(t):
        user = users[t]
        return lax.bitwise_xor(user // per_piece, col) - base, lax.rem(user, per_piece)

    def choose(t, n):
        piece, _ = relative(t)
        order[n] = t
        return n + jnp.where((piece >= 0) & (piece < span), 1, 0)

    live = lax.fori_loop(0, count, choose, 0)

    def fetch(i):
        slot = lax.rem(i, SLOTS)
        return pltpu.make_async_copy(tiles.at[order[i]], buf.at[slot], sems.at[slot])

    for i in range(SLOTS):
        @pl.when(i < live)
        def _():
            fetch(i).start()

    def group(first, size):
        for q in range(size):
            fetch(first + q).wait()
        found = []
        for q in range(size):
            piece, part = relative(order[first + q])
            both = jnp.dot(
                slab[piece * per_piece + part],
                buf[lax.rem(first + q, SLOTS)],
                preferred_element_type=F32,
            )
            found.append(both)
        for q in range(size):
            add(lax.bitwise_xor(owner[items[order[first + q]]], row), found[q])
        for q in range(size):
            @pl.when(first + q + SLOTS < live)
            def _():
                fetch(first + q + SLOTS).start()

    def finish():
        groups = live // GROUP

        def many(g, _):
            group(g * GROUP, GROUP)
            return 0

        def one(i, _):
            group(i, 1)
            return 0

        lax.fori_loop(0, groups, many, 0)
        lax.fori_loop(groups * GROUP, live, one, 0)

    return finish


def split_kernel(sketch, flat, whole, chunk):
    flat[...] = sketch[...].T
    first = 0
    for kc in CHUNKS:
        rows = flat[first : first + kc, :]
        high = rows.astype(BF16)
        low = (rows - high.astype(F32)).astype(BF16)
        for i, part in enumerate((high, low)):
            start = 2 * first + i * kc
            whole[start : start + kc, :] = part
            if first == 0:
                chunk[start : start + kc, :] = part
        first += kc


def split_sketch(sketch):
    users, width = sketch.shape
    vmem = pl.BlockSpec(memory_space=pltpu.VMEM)
    return pl.pallas_call(
        split_kernel,
        out_shape=[jax.ShapeDtypeStruct((width, users), F32)]
        + [jax.ShapeDtypeStruct((k, users), BF16) for k in (2 * width, 2 * CHUNKS[0])],
        in_specs=[vmem],
        out_specs=[vmem] * 3,
        compiler_params=pltpu.CompilerParams(vmem_limit_bytes=16 * 2**20),
    )(sketch)


def gram_kernel(flat, packed):
    n = packed.shape[1]
    top, low = flat[:n, :], flat[n:, :]
    second = mmt(low, low)
    r = lax.broadcasted_iota(jnp.int32, (n, n), 0)
    c = lax.broadcasted_iota(jnp.int32, (n, n), 1)
    packed[:n] = jnp.where(r >= c, mmt(top, top), second)
    packed[n : 2 * n] = mmt(low, top)
    tail = jnp.sum(jnp.where(r == c, second, 0.0), axis=0, keepdims=True)
    packed[2 * n :] = jnp.broadcast_to(tail, (8, n))


def packed_gram(flat):
    n = flat.shape[0] // 2
    vmem = pl.BlockSpec(memory_space=pltpu.VMEM)
    return pl.pallas_call(
        gram_kernel,
        out_shape=jax.ShapeDtypeStruct((2 * n + 8, n), F32),
        in_specs=[vmem],
        out_specs=vmem,
        compiler_params=pltpu.CompilerParams(vmem_limit_bytes=16 * 2**20),
    )(flat)


def fill(slab, pieces, per_piece):
    tile_size = slab.shape[2]
    for c, blocks in enumerate(pieces):
        first = 0
        for block in blocks:
            stop = first + block.shape[0]
            for h in range(per_piece):
                slab[c * per_piece + h, first:stop, :] = block[:, h * tile_size : (h + 1) * tile_size]
            first = stop


def near_kernel(span, users, items, owner, meta, *refs):
    pieces = [refs[i : i + 1] for i in range(span)]
    tiles = refs[span]
    sums = refs[span + 1 : -4]
    slab, buf, sems, order = refs[-4:]
    per_piece = refs[0].shape[1] // tiles.shape[1]

    def add(place, both):
        first = 0
        for part in sums:
            kc = part.shape[1]
            part[place] += both[first : first + kc] + both[first + kc : first + 2 * kc]
            first += 2 * kc

    finish = run_tiles(
        0, span, per_piece, users, items, owner, meta, tiles, slab, add, buf, sems, order
    )
    for part in sums:
        part[...] = jnp.zeros_like(part)
    fill(slab, pieces, per_piece)
    finish()


def far_kernel(span, blocks, orders, users, items, owner, meta, *refs):
    pieces = [refs[i * blocks : (i + 1) * blocks] for i in range(span)]
    start, tiles = refs[span * blocks], refs[span * blocks + 1]
    outs = refs[span * blocks + 2 : -5]
    slab, buf, sems, order, acc = refs[-5:]
    tile_size = tiles.shape[1]
    per_piece = refs[0].shape[1] // tile_size
    kc = start.shape[1]

    def add(place, both):
        acc[place] += both[:kc] + both[kc:]

    finish = run_tiles(
        span, span, per_piece, users, items, owner, meta, tiles, slab, add, buf, sems, order
    )
    acc[...] = start[...]
    fill(slab, pieces, per_piece)
    finish()
    width = tile_size // len(orders)
    for o, bits in enumerate(orders):
        cut = slice(o * width, (o + 1) * width)
        for k, place in enumerate(places(bits, 0)):
            outs[2 * o][k] = acc[place, :, cut]
        for k, place in enumerate(places(bits, 1)):
            outs[2 * o + 1][k] = acc[place, :, cut].astype(BF16)


def tile_call(kernel, scalars, pieces, extra, tiles, shapes, scratch, cost):
    users = scalars[0].shape[0]
    tile_size = tiles.shape[1]
    count = len(pieces) * pieces[0][0].shape[1] // tile_size
    depth = sum(block.shape[0] for block in pieces[0])
    pieces = [block for blocks in pieces for block in blocks]
    smem = pl.BlockSpec(memory_space=pltpu.SMEM)
    vmem = pl.BlockSpec(memory_space=pltpu.VMEM)
    slab = jax.ShapeDtypeStruct((count, depth, tile_size), BF16)
    buf = jax.ShapeDtypeStruct((SLOTS, tile_size, tile_size), BF16)
    held = sum(x.size * x.dtype.itemsize for x in (*pieces, *extra, *shapes, *scratch, slab, buf))
    return pl.pallas_call(
        kernel,
        out_shape=shapes,
        in_specs=[smem] * len(scalars)
        + [vmem] * (len(pieces) + len(extra))
        + [pl.BlockSpec(memory_space=pl.ANY)],
        out_specs=[vmem] * len(shapes),
        scratch_shapes=[
            pltpu.VMEM(slab.shape, BF16),
            pltpu.VMEM(buf.shape, BF16),
            pltpu.SemaphoreType.DMA((SLOTS,)),
            pltpu.SMEM((users,), jnp.int32),
        ]
        + [pltpu.VMEM(x.shape, x.dtype) for x in scratch],
        compiler_params=pltpu.CompilerParams(vmem_limit_bytes=held + SPARE),
        cost_estimate=pl.CostEstimate(flops=0, bytes_accessed=cost, transcendentals=0),
    )(*scalars, *pieces, *extra, tiles)


def near_sums(scalars, pieces, tiles, rows):
    tile_size = tiles.shape[1]
    shapes = [jax.ShapeDtypeStruct((rows, kc, tile_size), F32) for kc in CHUNKS]
    return tile_call(
        functools.partial(near_kernel, len(pieces)), scalars, [[p] for p in pieces], [], tiles, shapes, [], NEAR_COST
    )


def far_sums(scalars, pieces, start, tiles, orders, cost):
    rows, kc, tile_size = start.shape
    width = tile_size // len(orders)
    shapes = []
    for _ in orders:
        shapes.append(jax.ShapeDtypeStruct((rows // 2, kc, width), F32))
        shapes.append(jax.ShapeDtypeStruct((rows // 2, kc, width), BF16))
    return tile_call(
        functools.partial(far_kernel, len(pieces), len(pieces[0]), orders),
        scalars,
        pieces,
        [start],
        tiles,
        shapes,
        [jax.ShapeDtypeStruct(start.shape, F32)],
        cost,
    )


def mm(a, b):
    return lax.dot_general(a, b, (((1,), (0,)), ((), ())), precision=HIGH, preferred_element_type=F32)


def mmt(a, b):
    return lax.dot_general(a, b, (((1,), (1,)), ((), ())), precision=HIGH, preferred_element_type=F32)


def factor_kernel(packed, inverse, good):
    n = packed.shape[1]
    r = lax.broadcasted_iota(jnp.int32, (n, n), 0)
    c = lax.broadcasted_iota(jnp.int32, (n, n), 1)
    mixed = packed[:n]
    flipped = mixed.T
    side = packed[n : 2 * n]
    tail = jnp.broadcast_to(packed[2 * n : 2 * n + 1], (n, n))
    first = jnp.where(r >= c, mixed, flipped)
    second = jnp.where(r < c, mixed, jnp.where(r > c, flipped, tail))
    gram = jnp.concatenate(
        [jnp.concatenate([first, side.T], axis=1), jnp.concatenate([side, second], axis=1)], axis=0
    )
    m = 2 * n
    rr = lax.broadcasted_iota(jnp.int32, (m, m), 0)
    cc = lax.broadcasted_iota(jnp.int32, (m, m), 1)
    on = rr == cc
    eye = jnp.where(on, 1.0, 0.0).astype(F32)
    low = jnp.where(rr > cc, 1.0, jnp.where(on, 0.5, 0.0)).astype(F32)
    diag = jnp.where(on, gram, 0.0)
    scale_row = lax.rsqrt(jnp.sum(diag, axis=0, keepdims=True))
    scale_col = lax.rsqrt(jnp.sum(diag, axis=1, keepdims=True))
    unit = gram * scale_row * scale_col
    off = unit - eye
    square = jnp.dot(off, off, preferred_element_type=F32)
    spread = jnp.max(jnp.sum(jnp.abs(jnp.dot(square, square, preferred_element_type=F32)), axis=1))
    w = eye - low * off
    for _ in range(NEWTON):
        err = mmt(mm(w, unit), w) - eye
        w = w - mm(low * err, w)
    last = jnp.max(jnp.sum(jnp.abs(err), axis=1))
    inflation = jnp.max(jnp.sum(w * w, axis=0))
    inverse[...] = w * scale_row
    good[0] = jnp.where((spread < 0.025) & (last < 0.01) & (inflation < 1.1), 1, 0)


def factor(packed):
    n = packed.shape[1]
    return pl.pallas_call(
        factor_kernel,
        out_shape=[jax.ShapeDtypeStruct((2 * n, 2 * n), F32), jax.ShapeDtypeStruct((1,), jnp.int32)],
        in_specs=[pl.BlockSpec(memory_space=pltpu.VMEM)],
        out_specs=[pl.BlockSpec(memory_space=pltpu.VMEM), pl.BlockSpec(memory_space=pltpu.SMEM)],
        compiler_params=pltpu.CompilerParams(vmem_limit_bytes=24 * 2**20),
        cost_estimate=pl.CostEstimate(
            flops=0, bytes_accessed=FACTOR_COST, transcendentals=0
        ),
    )(packed)


def last_kernel(inverse, early, keep0, keep1, came, out):
    left = keep0[0] + came[0].astype(F32)
    right = keep1[0] + came[1].astype(F32)
    total = jnp.concatenate([early[...], jnp.concatenate([left, right], axis=1)], axis=0)
    w = inverse[...]
    wh, th = w.astype(BF16), total.astype(BF16)
    wl = (w - wh.astype(F32)).astype(BF16)
    tl = (total - th.astype(F32)).astype(BF16)
    small = jnp.dot(wh, tl, preferred_element_type=F32) + jnp.dot(wl, th, preferred_element_type=F32)
    out[...] = jnp.dot(wh, th, preferred_element_type=F32) + small


def last(inverse, early, keeps, came):
    vmem = pl.BlockSpec(memory_space=pltpu.VMEM)
    return pl.pallas_call(
        last_kernel,
        out_shape=jax.ShapeDtypeStruct((inverse.shape[0], early.shape[1]), F32),
        in_specs=[vmem] * 5,
        out_specs=vmem,
        compiler_params=pltpu.CompilerParams(vmem_limit_bytes=16 * 2**20),
    )(inverse, early, *keeps, came)


def full_path(rows, cols, sketch, tiles, tile_user, tile_item, tile_count, item_owner, packed):
    n = packed.shape[1]
    r = lax.broadcasted_iota(jnp.int32, (n, n), 0)
    c = lax.broadcasted_iota(jnp.int32, (n, n), 1)
    mixed, side, tail = packed[:n], packed[n : 2 * n], packed[2 * n : 2 * n + 1]
    first = jnp.where(r >= c, mixed, mixed.T)
    second = jnp.where(r < c, mixed, jnp.where(r > c, mixed.T, tail))
    gram = jnp.block([[first, side.T], [side, second]])
    lower = jnp.linalg.cholesky(gram)
    basis = lax.linalg.triangular_solve(lower, sketch, left_side=False, lower=True, transpose_a=True).astype(BF16)
    have = {0: basis}
    for bit in bits_of(cols):
        for place in list(have):
            have[place | bit] = swap(have[place], "cols", cols, bit)
    slab = jnp.concatenate([have[i] for i in range(cols)], axis=0)
    col = lax.axis_index("cols")
    row = lax.axis_index("rows")
    per_piece = sketch.shape[0] // tiles.shape[2]
    owner = item_owner[0]
    tile_size = tiles.shape[2]

    def step(index, sums):
        user = tile_user[index]
        block = lax.bitwise_xor(user // per_piece, col) * per_piece + user % per_piece
        part_rows = lax.dynamic_slice_in_dim(slab, block * tile_size, tile_size, 0)
        part = lax.dot_general(part_rows, tiles[index], (((0,), (0,)), ((), ())), preferred_element_type=F32)
        place = lax.bitwise_xor(owner[tile_item[index]], row)
        now = lax.dynamic_index_in_dim(sums, place, 0, keepdims=False)
        return lax.dynamic_update_index_in_dim(sums, now + part, place, 0)

    totals = jnp.zeros((owner.shape[0], sketch.shape[1], tile_size), F32)
    totals = lax.fori_loop(0, tile_count[0], step, totals)
    for bit in bits_of(rows):
        totals = totals[:bit] + swap(totals[bit:], "rows", rows, bit)
    return totals[0]


def after(value, *others):
    return lax.optimization_barrier((value, *others))[0]


def exchange(lanes, rows):
    groups = []
    for bit in sorted({lane[2] for lane in lanes}):
        members = [i for i, lane in enumerate(lanes) if lane[2] == bit]
        sent = [lanes[i][1].reshape(-1, lanes[i][1].shape[2]) for i in members]
        groups.append((members, swap(jnp.concatenate(sent, axis=0), "rows", rows, 1 << bit)))
    return groups


def received(lanes, groups):
    got = [None] * len(lanes)
    for members, came in groups:
        first = 0
        for i in members:
            shape = lanes[i][1].shape
            size = shape[0] * shape[1]
            got[i] = came[first : first + size].reshape(shape)
            first += size
    return [lane[0] + g.astype(F32) for lane, g in zip(lanes, got)]


def split(total):
    half = total.shape[0] // 2
    return total[:half], total[half:].astype(BF16)


def body(rows, cols, sketch, tiles, tile_user, tile_item, tile_count, item_owner):
    row_bits = rows.bit_length() - 1
    first_order = tuple(range(row_bits))
    orders = (first_order, (1, 0) + first_order[2:])
    row = lax.axis_index("rows")
    col = lax.axis_index("cols")
    meta = jnp.stack([tile_count[0], row, col]).astype(jnp.int32)
    scalars = (tile_user, tile_item, item_owner[0], meta)
    far_bit, *near_bits = bits_of(cols)

    def spread(piece):
        have = {0: piece}
        for bit in near_bits:
            for place in list(have):
                have[place | bit] = swap(have[place], "cols", cols, bit)
        return [have[i] for i in range(cols // 2)]

    fence = lax.optimization_barrier
    far = far_bit
    flat, whole, chunk = split_sketch(sketch)
    near = spread(whole)
    crossed = [swap(c, "cols", cols, far) for c in (chunk, whole[2 * CHUNKS[0] :])]
    packed = packed_gram(flat)
    for bit in near_bits:
        packed = packed + swap(packed, "cols", cols, bit)
    came = swap(packed, "rows", rows, 1)
    near[0] = after(near[0], packed)
    sums = near_sums(scalars, near, tiles, rows)
    packed, came, *sums = fence((packed, came, *sums))
    packed = packed + came
    packed = packed + swap(packed, "rows", rows, 2)
    came = swap(packed, "rows", rows, 4)
    crossed[0] = after(crossed[0], packed)
    pieces = list(zip(*[spread(c) for c in jnp.split(crossed[0], 2, axis=0)]))
    outs = far_sums(scalars, pieces, sums[0], tiles, orders, EARLY_COST)
    packed, came, *outs = fence((packed, came, *outs))
    packed = packed + came
    lanes = [(outs[2 * o], outs[2 * o + 1], order[0]) for o, order in enumerate(orders)]
    groups = exchange(lanes, rows)
    crossed[1] = after(crossed[1], packed)
    later = far_sums(scalars, [[p] for p in spread(crossed[1])], sums[1], tiles, orders, LATE_COST)
    flying = [g[1] for g in groups]
    rest = fence((*flying, *later))
    groups = [(g[0], x) for g, x in zip(groups, rest)]
    later = rest[len(groups) :]
    stages = [("cols", far)] + [("rows", 1 << b) for b in range(3, row_bits)]

    totals = received(lanes, groups)
    late = [(later[2 * o], later[2 * o + 1]) for o in range(len(orders))]
    for step in range(1, row_bits + 1):
        lanes = []
        if step < row_bits:
            lanes += [(*split(t), order[step]) for t, order in zip(totals, orders)]
        lanes += [(*pair, order[step - 1]) for pair, order in zip(late, orders)]
        groups = exchange(lanes, rows)
        flying = [g[1] for g in groups]
        if step <= len(stages):
            axis, bit = stages[step - 1]
            came = swap(packed, axis, rows if axis == "rows" else cols, bit)
            if step < len(stages):
                packed, came, *flying = fence((packed, came, *flying))
                packed = packed + came
            else:
                packed = packed + came
                inverse, good = factor(after(packed, *[lane[1] for lane in lanes]))
                inverse, *flying = fence((inverse, *flying))
        groups = [(g[0], x) for g, x in zip(groups, flying)]
        if step < row_bits:
            new = received(lanes, groups)
            totals, new = new[: len(orders)], new[len(orders) :]
            late = [split(t) for t in new]
        if step == row_bits - 1:
            early = jnp.concatenate([t[0] for t in totals], axis=1)
    keeps = [lane[0] for lane in lanes]
    came = groups[0][1].reshape(len(lanes), *lanes[0][1].shape[1:])
    out = lax.cond(
        good[0] > 0,
        lambda: last(inverse, early, keeps, came),
        lambda: full_path(rows, cols, sketch, tiles, tile_user, tile_item, tile_count, item_owner, packed),
    )
    return out[None, None]


def solution(mesh):
    placed = (
        P(("rows", "cols"), None),
        P(("rows", "cols"), None, None),
        P(("rows", "cols")),
        P(("rows", "cols")),
        P(("rows", "cols")),
        P("cols", None),
    )
    return jax.shard_map(
        functools.partial(body, mesh.shape["rows"], mesh.shape["cols"]),
        mesh=mesh,
        in_specs=placed,
        out_specs=P("rows", "cols", None, None),
        check_vma=False,
    )
```

```python
import functools

import jax
import jax.numpy as jnp
from jax import lax
from jax.experimental import pallas as pl
from jax.experimental.pallas import tpu as pltpu
from jax.sharding import PartitionSpec as P

F32 = jnp.float32
BF16 = jnp.bfloat16
HIGH = lax.Precision.HIGHEST
SLOTS = 12
SPARE = 4 * 2**20
GROUP = 4
NEAR_COST = 200 * 2**20
EARLY_COST = 1024
LATE_COST = 1024
FACTOR_COST = 200 * 2**20
CHUNKS = (160, 96)
NEWTON = 2


def bits_of(count):
    return [1 << b for b in reversed(range(count.bit_length() - 1))]


def swap(x, axis, count, bit):
    return lax.ppermute(x, axis, [(i, i ^ bit) for i in range(count)])


def places(order, parity):
    found = [parity << order[0]]
    for bit in reversed(order[1:]):
        found = found + [p | (1 << bit) for p in found]
    return found


def run_tiles(base, span, per_piece, users, items, owner, meta, tiles, slab, add, buf, sems, order):
    count, row, col = meta[0], meta[1], meta[2]

    def relative(t):
        user = users[t]
        return lax.bitwise_xor(user // per_piece, col) - base, lax.rem(user, per_piece)

    def choose(t, n):
        piece, _ = relative(t)
        order[n] = t
        return n + jnp.where((piece >= 0) & (piece < span), 1, 0)

    live = lax.fori_loop(0, count, choose, 0)

    def fetch(i):
        slot = lax.rem(i, SLOTS)
        return pltpu.make_async_copy(tiles.at[order[i]], buf.at[slot], sems.at[slot])

    for i in range(SLOTS):
        @pl.when(i < live)
        def _():
            fetch(i).start()

    def group(first, size):
        for q in range(size):
            fetch(first + q).wait()
        found = []
        for q in range(size):
            piece, part = relative(order[first + q])
            both = jnp.dot(
                slab[piece * per_piece + part],
                buf[lax.rem(first + q, SLOTS)],
                preferred_element_type=F32,
            )
            found.append(both)
        for q in range(size):
            add(lax.bitwise_xor(owner[items[order[first + q]]], row), found[q])
        for q in range(size):
            @pl.when(first + q + SLOTS < live)
            def _():
                fetch(first + q + SLOTS).start()

    def finish():
        groups = live // GROUP

        def many(g, _):
            group(g * GROUP, GROUP)
            return 0

        def one(i, _):
            group(i, 1)
            return 0

        lax.fori_loop(0, groups, many, 0)
        lax.fori_loop(groups * GROUP, live, one, 0)

    return finish


def split_kernel(sketch, flat, whole, chunk):
    flat[...] = sketch[...].T
    first = 0
    for kc in CHUNKS:
        rows = flat[first : first + kc, :]
        high = rows.astype(BF16)
        low = (rows - high.astype(F32)).astype(BF16)
        for i, part in enumerate((high, low)):
            start = 2 * first + i * kc
            whole[start : start + kc, :] = part
            if first == 0:
                chunk[start : start + kc, :] = part
        first += kc


def split_sketch(sketch):
    users, width = sketch.shape
    vmem = pl.BlockSpec(memory_space=pltpu.VMEM)
    return pl.pallas_call(
        split_kernel,
        out_shape=[jax.ShapeDtypeStruct((width, users), F32)]
        + [jax.ShapeDtypeStruct((k, users), BF16) for k in (2 * width, 2 * CHUNKS[0])],
        in_specs=[vmem],
        out_specs=[vmem] * 3,
        compiler_params=pltpu.CompilerParams(vmem_limit_bytes=16 * 2**20),
    )(sketch)


def gram_kernel(flat, packed):
    n = packed.shape[1]
    top, low = flat[:n, :], flat[n:, :]
    second = mmt(low, low)
    r = lax.broadcasted_iota(jnp.int32, (n, n), 0)
    c = lax.broadcasted_iota(jnp.int32, (n, n), 1)
    packed[:n] = jnp.where(r >= c, mmt(top, top), second)
    packed[n : 2 * n] = mmt(low, top)
    tail = jnp.sum(jnp.where(r == c, second, 0.0), axis=0, keepdims=True)
    packed[2 * n :] = jnp.broadcast_to(tail, (8, n))


def packed_gram(flat):
    n = flat.shape[0] // 2
    vmem = pl.BlockSpec(memory_space=pltpu.VMEM)
    return pl.pallas_call(
        gram_kernel,
        out_shape=jax.ShapeDtypeStruct((2 * n + 8, n), F32),
        in_specs=[vmem],
        out_specs=vmem,
        compiler_params=pltpu.CompilerParams(vmem_limit_bytes=16 * 2**20),
    )(flat)


def fill(slab, pieces, per_piece):
    tile_size = slab.shape[2]
    for c, blocks in enumerate(pieces):
        first = 0
        for block in blocks:
            stop = first + block.shape[0]
            for h in range(per_piece):
                slab[c * per_piece + h, first:stop, :] = block[:, h * tile_size : (h + 1) * tile_size]
            first = stop


def near_kernel(span, users, items, owner, meta, *refs):
    pieces = [refs[i : i + 1] for i in range(span)]
    tiles = refs[span]
    sums = refs[span + 1 : -4]
    slab, buf, sems, order = refs[-4:]
    per_piece = refs[0].shape[1] // tiles.shape[1]

    def add(place, both):
        first = 0
        for part in sums:
            kc = part.shape[1]
            part[place] += both[first : first + kc] + both[first + kc : first + 2 * kc]
            first += 2 * kc

    finish = run_tiles(
        0, span, per_piece, users, items, owner, meta, tiles, slab, add, buf, sems, order
    )
    for part in sums:
        part[...] = jnp.zeros_like(part)
    fill(slab, pieces, per_piece)
    finish()


def far_kernel(span, blocks, orders, users, items, owner, meta, *refs):
    pieces = [refs[i * blocks : (i + 1) * blocks] for i in range(span)]
    start, tiles = refs[span * blocks], refs[span * blocks + 1]
    outs = refs[span * blocks + 2 : -5]
    slab, buf, sems, order, acc = refs[-5:]
    tile_size = tiles.shape[1]
    per_piece = refs[0].shape[1] // tile_size
    kc = start.shape[1]

    def add(place, both):
        acc[place] += both[:kc] + both[kc:]

    finish = run_tiles(
        span, span, per_piece, users, items, owner, meta, tiles, slab, add, buf, sems, order
    )
    acc[...] = start[...]
    fill(slab, pieces, per_piece)
    finish()
    width = tile_size // len(orders)
    for o, bits in enumerate(orders):
        cut = slice(o * width, (o + 1) * width)
        for k, place in enumerate(places(bits, 0)):
            outs[2 * o][k] = acc[place, :, cut]
        for k, place in enumerate(places(bits, 1)):
            outs[2 * o + 1][k] = acc[place, :, cut].astype(BF16)


def tile_call(kernel, scalars, pieces, extra, tiles, shapes, scratch, cost):
    users = scalars[0].shape[0]
    tile_size = tiles.shape[1]
    count = len(pieces) * pieces[0][0].shape[1] // tile_size
    depth = sum(block.shape[0] for block in pieces[0])
    pieces = [block for blocks in pieces for block in blocks]
    smem = pl.BlockSpec(memory_space=pltpu.SMEM)
    vmem = pl.BlockSpec(memory_space=pltpu.VMEM)
    slab = jax.ShapeDtypeStruct((count, depth, tile_size), BF16)
    buf = jax.ShapeDtypeStruct((SLOTS, tile_size, tile_size), BF16)
    held = sum(x.size * x.dtype.itemsize for x in (*pieces, *extra, *shapes, *scratch, slab, buf))
    return pl.pallas_call(
        kernel,
        out_shape=shapes,
        in_specs=[smem] * len(scalars)
        + [vmem] * (len(pieces) + len(extra))
        + [pl.BlockSpec(memory_space=pl.ANY)],
        out_specs=[vmem] * len(shapes),
        scratch_shapes=[
            pltpu.VMEM(slab.shape, BF16),
            pltpu.VMEM(buf.shape, BF16),
            pltpu.SemaphoreType.DMA((SLOTS,)),
            pltpu.SMEM((users,), jnp.int32),
        ]
        + [pltpu.VMEM(x.shape, x.dtype) for x in scratch],
        compiler_params=pltpu.CompilerParams(vmem_limit_bytes=held + SPARE),
        cost_estimate=pl.CostEstimate(flops=0, bytes_accessed=cost, transcendentals=0),
    )(*scalars, *pieces, *extra, tiles)


def near_sums(scalars, pieces, tiles, rows):
    tile_size = tiles.shape[1]
    shapes = [jax.ShapeDtypeStruct((rows, kc, tile_size), F32) for kc in CHUNKS]
    return tile_call(
        functools.partial(near_kernel, len(pieces)), scalars, [[p] for p in pieces], [], tiles, shapes, [], NEAR_COST
    )


def far_sums(scalars, pieces, start, tiles, orders, cost):
    rows, kc, tile_size = start.shape
    width = tile_size // len(orders)
    shapes = []
    for _ in orders:
        shapes.append(jax.ShapeDtypeStruct((rows // 2, kc, width), F32))
        shapes.append(jax.ShapeDtypeStruct((rows // 2, kc, width), BF16))
    return tile_call(
        functools.partial(far_kernel, len(pieces), len(pieces[0]), orders),
        scalars,
        pieces,
        [start],
        tiles,
        shapes,
        [jax.ShapeDtypeStruct(start.shape, F32)],
        cost,
    )


def mm(a, b):
    return lax.dot_general(a, b, (((1,), (0,)), ((), ())), precision=HIGH, preferred_element_type=F32)


def mmt(a, b):
    return lax.dot_general(a, b, (((1,), (1,)), ((), ())), precision=HIGH, preferred_element_type=F32)


def factor_kernel(packed, inverse, good):
    n = packed.shape[1]
    r = lax.broadcasted_iota(jnp.int32, (n, n), 0)
    c = lax.broadcasted_iota(jnp.int32, (n, n), 1)
    mixed = packed[:n]
    flipped = mixed.T
    side = packed[n : 2 * n]
    tail = jnp.broadcast_to(packed[2 * n : 2 * n + 1], (n, n))
    first = jnp.where(r >= c, mixed, flipped)
    second = jnp.where(r < c, mixed, jnp.where(r > c, flipped, tail))
    gram = jnp.concatenate(
        [jnp.concatenate([first, side.T], axis=1), jnp.concatenate([side, second], axis=1)], axis=0
    )
    m = 2 * n
    rr = lax.broadcasted_iota(jnp.int32, (m, m), 0)
    cc = lax.broadcasted_iota(jnp.int32, (m, m), 1)
    on = rr == cc
    eye = jnp.where(on, 1.0, 0.0).astype(F32)
    low = jnp.where(rr > cc, 1.0, jnp.where(on, 0.5, 0.0)).astype(F32)
    diag = jnp.where(on, gram, 0.0)
    scale_row = lax.rsqrt(jnp.sum(diag, axis=0, keepdims=True))
    scale_col = lax.rsqrt(jnp.sum(diag, axis=1, keepdims=True))
    unit = gram * scale_row * scale_col
    off = unit - eye
    square = jnp.dot(off, off, preferred_element_type=F32)
    spread = jnp.max(jnp.sum(jnp.abs(jnp.dot(square, square, preferred_element_type=F32)), axis=1))
    w = eye - low * off
    for _ in range(NEWTON):
        err = mmt(mm(w, unit), w) - eye
        w = w - mm(low * err, w)
    last = jnp.max(jnp.sum(jnp.abs(err), axis=1))
    inflation = jnp.max(jnp.sum(w * w, axis=0))
    inverse[...] = w * scale_row
    good[0] = jnp.where((spread < 0.025) & (last < 0.01) & (inflation < 1.1), 1, 0)


def factor(packed):
    n = packed.shape[1]
    return pl.pallas_call(
        factor_kernel,
        out_shape=[jax.ShapeDtypeStruct((2 * n, 2 * n), F32), jax.ShapeDtypeStruct((1,), jnp.int32)],
        in_specs=[pl.BlockSpec(memory_space=pltpu.VMEM)],
        out_specs=[pl.BlockSpec(memory_space=pltpu.VMEM), pl.BlockSpec(memory_space=pltpu.SMEM)],
        compiler_params=pltpu.CompilerParams(vmem_limit_bytes=24 * 2**20),
        cost_estimate=pl.CostEstimate(
            flops=0, bytes_accessed=FACTOR_COST, transcendentals=0
        ),
    )(packed)


def last_kernel(inverse, early, keep0, keep1, came, out):
    left = keep0[0] + came[0].astype(F32)
    right = keep1[0] + came[1].astype(F32)
    total = jnp.concatenate([early[...], jnp.concatenate([left, right], axis=1)], axis=0)
    w = inverse[...]
    wh, th = w.astype(BF16), total.astype(BF16)
    wl = (w - wh.astype(F32)).astype(BF16)
    tl = (total - th.astype(F32)).astype(BF16)
    small = jnp.dot(wh, tl, preferred_element_type=F32) + jnp.dot(wl, th, preferred_element_type=F32)
    out[...] = jnp.dot(wh, th, preferred_element_type=F32) + small


def last(inverse, early, keeps, came):
    vmem = pl.BlockSpec(memory_space=pltpu.VMEM)
    return pl.pallas_call(
        last_kernel,
        out_shape=jax.ShapeDtypeStruct((inverse.shape[0], early.shape[1]), F32),
        in_specs=[vmem] * 5,
        out_specs=vmem,
        compiler_params=pltpu.CompilerParams(vmem_limit_bytes=16 * 2**20),
    )(inverse, early, *keeps, came)


def full_path(rows, cols, sketch, tiles, tile_user, tile_item, tile_count, item_owner, packed):
    n = packed.shape[1]
    r = lax.broadcasted_iota(jnp.int32, (n, n), 0)
    c = lax.broadcasted_iota(jnp.int32, (n, n), 1)
    mixed, side, tail = packed[:n], packed[n : 2 * n], packed[2 * n : 2 * n + 1]
    first = jnp.where(r >= c, mixed, mixed.T)
    second = jnp.where(r < c, mixed, jnp.where(r > c, mixed.T, tail))
    gram = jnp.block([[first, side.T], [side, second]])
    lower = jnp.linalg.cholesky(gram)
    basis = lax.linalg.triangular_solve(lower, sketch, left_side=False, lower=True, transpose_a=True).astype(BF16)
    have = {0: basis}
    for bit in bits_of(cols):
        for place in list(have):
            have[place | bit] = swap(have[place], "cols", cols, bit)
    slab = jnp.concatenate([have[i] for i in range(cols)], axis=0)
    col = lax.axis_index("cols")
    row = lax.axis_index("rows")
    per_piece = sketch.shape[0] // tiles.shape[2]
    owner = item_owner[0]
    tile_size = tiles.shape[2]

    def step(index, sums):
        user = tile_user[index]
        block = lax.bitwise_xor(user // per_piece, col) * per_piece + user % per_piece
        part_rows = lax.dynamic_slice_in_dim(slab, block * tile_size, tile_size, 0)
        part = lax.dot_general(part_rows, tiles[index], (((0,), (0,)), ((), ())), preferred_element_type=F32)
        place = lax.bitwise_xor(owner[tile_item[index]], row)
        now = lax.dynamic_index_in_dim(sums, place, 0, keepdims=False)
        return lax.dynamic_update_index_in_dim(sums, now + part, place, 0)

    totals = jnp.zeros((owner.shape[0], sketch.shape[1], tile_size), F32)
    totals = lax.fori_loop(0, tile_count[0], step, totals)
    for bit in bits_of(rows):
        totals = totals[:bit] + swap(totals[bit:], "rows", rows, bit)
    return totals[0]


def after(value, *others):
    return lax.optimization_barrier((value, *others))[0]


def exchange(lanes, rows):
    groups = []
    for bit in sorted({lane[2] for lane in lanes}):
        members = [i for i, lane in enumerate(lanes) if lane[2] == bit]
        sent = [lanes[i][1].reshape(-1, lanes[i][1].shape[2]) for i in members]
        groups.append((members, swap(jnp.concatenate(sent, axis=0), "rows", rows, 1 << bit)))
    return groups


def received(lanes, groups):
    got = [None] * len(lanes)
    for members, came in groups:
        first = 0
        for i in members:
            shape = lanes[i][1].shape
            size = shape[0] * shape[1]
            got[i] = came[first : first + size].reshape(shape)
            first += size
    return [lane[0] + g.astype(F32) for lane, g in zip(lanes, got)]


def split(total):
    half = total.shape[0] // 2
    return total[:half], total[half:].astype(BF16)


def body(rows, cols, sketch, tiles, tile_user, tile_item, tile_count, item_owner):
    row_bits = rows.bit_length() - 1
    first_order = tuple(range(row_bits))
    orders = (first_order, (1, 0) + first_order[2:])
    row = lax.axis_index("rows")
    col = lax.axis_index("cols")
    meta = jnp.stack([tile_count[0], row, col]).astype(jnp.int32)
    scalars = (tile_user, tile_item, item_owner[0], meta)
    far_bit, *near_bits = bits_of(cols)

    def spread(piece):
        have = {0: piece}
        for bit in near_bits:
            for place in list(have):
                have[place | bit] = swap(have[place], "cols", cols, bit)
        return [have[i] for i in range(cols // 2)]

    fence = lax.optimization_barrier
    far = far_bit
    flat, whole, chunk = split_sketch(sketch)
    near = spread(whole)
    crossed = [swap(c, "cols", cols, far) for c in (chunk, whole[2 * CHUNKS[0] :])]
    packed = packed_gram(flat)
    for bit in near_bits:
        packed = packed + swap(packed, "cols", cols, bit)
    came = swap(packed, "rows", rows, 1)
    near[0] = after(near[0], packed)
    sums = near_sums(scalars, near, tiles, rows)
    packed, came, *sums = fence((packed, came, *sums))
    packed = packed + came
    came = swap(packed, "rows", rows, 2)
    crossed[0] = after(crossed[0], packed)
    pieces = list(zip(*[spread(c) for c in jnp.split(crossed[0], 2, axis=0)]))
    outs = far_sums(scalars, pieces, sums[0], tiles, orders, EARLY_COST)
    packed, came, *outs = fence((packed, came, *outs))
    packed = packed + came
    came = swap(packed, "rows", rows, 4)
    lanes = [(outs[2 * o], outs[2 * o + 1], order[0]) for o, order in enumerate(orders)]
    groups = exchange(lanes, rows)
    crossed[1] = after(crossed[1], packed)
    later = far_sums(scalars, [[p] for p in spread(crossed[1])], sums[1], tiles, orders, LATE_COST)
    flying = [g[1] for g in groups]
    packed, came, *rest = fence((packed, came, *flying, *later))
    groups = [(g[0], x) for g, x in zip(groups, rest)]
    later = rest[len(groups) :]
    packed = packed + came
    stages = [("cols", far)] + [("rows", 1 << b) for b in range(3, row_bits)]

    totals = received(lanes, groups)
    late = [(later[2 * o], later[2 * o + 1]) for o in range(len(orders))]
    for step in range(1, row_bits + 1):
        lanes = []
        if step < row_bits:
            lanes += [(*split(t), order[step]) for t, order in zip(totals, orders)]
        lanes += [(*pair, order[step - 1]) for pair, order in zip(late, orders)]
        groups = exchange(lanes, rows)
        flying = [g[1] for g in groups]
        if step <= len(stages):
            axis, bit = stages[step - 1]
            came = swap(packed, axis, rows if axis == "rows" else cols, bit)
            if step < len(stages):
                packed, came, *flying = fence((packed, came, *flying))
                packed = packed + came
            else:
                packed = packed + came
                inverse, good = factor(after(packed, *[lane[1] for lane in lanes]))
                inverse, *flying = fence((inverse, *flying))
        groups = [(g[0], x) for g, x in zip(groups, flying)]
        if step < row_bits:
            new = received(lanes, groups)
            totals, new = new[: len(orders)], new[len(orders) :]
            late = [split(t) for t in new]
        if step == row_bits - 1:
            early = jnp.concatenate([t[0] for t in totals], axis=1)
    keeps = [lane[0] for lane in lanes]
    came = groups[0][1].reshape(len(lanes), *lanes[0][1].shape[1:])
    out = lax.cond(
        good[0] > 0,
        lambda: last(inverse, early, keeps, came),
        lambda: full_path(rows, cols, sketch, tiles, tile_user, tile_item, tile_count, item_owner, packed),
    )
    return out[None, None]


def solution(mesh):
    placed = (
        P(("rows", "cols"), None),
        P(("rows", "cols"), None, None),
        P(("rows", "cols")),
        P(("rows", "cols")),
        P(("rows", "cols")),
        P("cols", None),
    )
    return jax.shard_map(
        functools.partial(body, mesh.shape["rows"], mesh.shape["cols"]),
        mesh=mesh,
        in_specs=placed,
        out_specs=P("rows", "cols", None, None),
        check_vma=False,
    )
```

```python
import functools

import jax
import jax.numpy as jnp
from jax import lax
from jax.experimental import pallas as pl
from jax.experimental.pallas import tpu as pltpu
from jax.sharding import PartitionSpec as P

F32 = jnp.float32
BF16 = jnp.bfloat16
HIGH = lax.Precision.HIGHEST
SLOTS = 12
SPARE = 4 * 2**20
GROUP = 4
NEAR_COST = 200 * 2**20
EARLY_COST = 1024
LATE_COST = 1024
FACTOR_COST = 200 * 2**20
CHUNKS = (160, 96)
NEWTON = 2


def bits_of(count):
    return [1 << b for b in reversed(range(count.bit_length() - 1))]


def swap(x, axis, count, bit):
    return lax.ppermute(x, axis, [(i, i ^ bit) for i in range(count)])


def places(order, parity):
    found = [parity << order[0]]
    for bit in reversed(order[1:]):
        found = found + [p | (1 << bit) for p in found]
    return found


def run_tiles(base, span, per_piece, users, items, owner, meta, tiles, slab, add, buf, sems, order):
    count, row, col = meta[0], meta[1], meta[2]

    def relative(t):
        user = users[t]
        return lax.bitwise_xor(user // per_piece, col) - base, lax.rem(user, per_piece)

    def choose(t, n):
        piece, _ = relative(t)
        order[n] = t
        return n + jnp.where((piece >= 0) & (piece < span), 1, 0)

    live = lax.fori_loop(0, count, choose, 0)

    def fetch(i):
        slot = lax.rem(i, SLOTS)
        return pltpu.make_async_copy(tiles.at[order[i]], buf.at[slot], sems.at[slot])

    for i in range(SLOTS):
        @pl.when(i < live)
        def _():
            fetch(i).start()

    def group(first, size):
        for q in range(size):
            fetch(first + q).wait()
        found = []
        for q in range(size):
            piece, part = relative(order[first + q])
            both = jnp.dot(
                slab[piece * per_piece + part],
                buf[lax.rem(first + q, SLOTS)],
                preferred_element_type=F32,
            )
            found.append(both)
        for q in range(size):
            add(lax.bitwise_xor(owner[items[order[first + q]]], row), found[q])
        for q in range(size):
            @pl.when(first + q + SLOTS < live)
            def _():
                fetch(first + q + SLOTS).start()

    def finish():
        groups = live // GROUP

        def many(g, _):
            group(g * GROUP, GROUP)
            return 0

        def one(i, _):
            group(i, 1)
            return 0

        lax.fori_loop(0, groups, many, 0)
        lax.fori_loop(groups * GROUP, live, one, 0)

    return finish


def split_kernel(sketch, flat, *chunks):
    flat[...] = sketch[...].T
    first = 0
    for chunk in chunks:
        kc = chunk.shape[0] // 2
        rows = flat[first : first + kc, :]
        high = rows.astype(BF16)
        chunk[:kc, :] = high
        chunk[kc:, :] = (rows - high.astype(F32)).astype(BF16)
        first += kc


def split_sketch(sketch):
    users, width = sketch.shape
    vmem = pl.BlockSpec(memory_space=pltpu.VMEM)
    return pl.pallas_call(
        split_kernel,
        out_shape=[jax.ShapeDtypeStruct((width, users), F32)]
        + [jax.ShapeDtypeStruct((2 * k, users), BF16) for k in CHUNKS],
        in_specs=[vmem],
        out_specs=[vmem] * (1 + len(CHUNKS)),
        compiler_params=pltpu.CompilerParams(vmem_limit_bytes=16 * 2**20),
    )(sketch)


def gram_kernel(flat, packed):
    n = packed.shape[1]
    top, low = flat[:n, :], flat[n:, :]
    second = mmt(low, low)
    r = lax.broadcasted_iota(jnp.int32, (n, n), 0)
    c = lax.broadcasted_iota(jnp.int32, (n, n), 1)
    packed[:n] = jnp.where(r >= c, mmt(top, top), second)
    packed[n : 2 * n] = mmt(low, top)
    tail = jnp.sum(jnp.where(r == c, second, 0.0), axis=0, keepdims=True)
    packed[2 * n :] = jnp.broadcast_to(tail, (8, n))


def packed_gram(flat):
    n = flat.shape[0] // 2
    vmem = pl.BlockSpec(memory_space=pltpu.VMEM)
    return pl.pallas_call(
        gram_kernel,
        out_shape=jax.ShapeDtypeStruct((2 * n + 8, n), F32),
        in_specs=[vmem],
        out_specs=vmem,
        compiler_params=pltpu.CompilerParams(vmem_limit_bytes=16 * 2**20),
    )(flat)


def fill(slab, pieces, per_piece):
    tile_size = slab.shape[2]
    for c, blocks in enumerate(pieces):
        first = 0
        for block in blocks:
            stop = first + block.shape[0]
            for h in range(per_piece):
                slab[c * per_piece + h, first:stop, :] = block[:, h * tile_size : (h + 1) * tile_size]
            first = stop


def near_kernel(span, blocks, users, items, owner, meta, *refs):
    pieces = [refs[i * blocks : (i + 1) * blocks] for i in range(span)]
    tiles = refs[span * blocks]
    sums = refs[span * blocks + 1 : -4]
    slab, buf, sems, order = refs[-4:]
    per_piece = refs[0].shape[1] // tiles.shape[1]

    def add(place, both):
        first = 0
        for part in sums:
            kc = part.shape[1]
            part[place] += both[first : first + kc] + both[first + kc : first + 2 * kc]
            first += 2 * kc

    finish = run_tiles(
        0, span, per_piece, users, items, owner, meta, tiles, slab, add, buf, sems, order
    )
    for part in sums:
        part[...] = jnp.zeros_like(part)
    fill(slab, pieces, per_piece)
    finish()


def far_kernel(span, blocks, orders, users, items, owner, meta, *refs):
    pieces = [refs[i * blocks : (i + 1) * blocks] for i in range(span)]
    start, tiles = refs[span * blocks], refs[span * blocks + 1]
    outs = refs[span * blocks + 2 : -5]
    slab, buf, sems, order, acc = refs[-5:]
    tile_size = tiles.shape[1]
    per_piece = refs[0].shape[1] // tile_size
    kc = start.shape[1]

    def add(place, both):
        acc[place] += both[:kc] + both[kc:]

    finish = run_tiles(
        span, span, per_piece, users, items, owner, meta, tiles, slab, add, buf, sems, order
    )
    acc[...] = start[...]
    fill(slab, pieces, per_piece)
    finish()
    width = tile_size // len(orders)
    for o, bits in enumerate(orders):
        cut = slice(o * width, (o + 1) * width)
        for k, place in enumerate(places(bits, 0)):
            outs[2 * o][k] = acc[place, :, cut]
        for k, place in enumerate(places(bits, 1)):
            outs[2 * o + 1][k] = acc[place, :, cut].astype(BF16)


def tile_call(kernel, scalars, pieces, extra, tiles, shapes, scratch, cost):
    users = scalars[0].shape[0]
    tile_size = tiles.shape[1]
    count = len(pieces) * pieces[0][0].shape[1] // tile_size
    depth = sum(block.shape[0] for block in pieces[0])
    pieces = [block for blocks in pieces for block in blocks]
    smem = pl.BlockSpec(memory_space=pltpu.SMEM)
    vmem = pl.BlockSpec(memory_space=pltpu.VMEM)
    slab = jax.ShapeDtypeStruct((count, depth, tile_size), BF16)
    buf = jax.ShapeDtypeStruct((SLOTS, tile_size, tile_size), BF16)
    held = sum(x.size * x.dtype.itemsize for x in (*pieces, *extra, *shapes, *scratch, slab, buf))
    return pl.pallas_call(
        kernel,
        out_shape=shapes,
        in_specs=[smem] * len(scalars)
        + [vmem] * (len(pieces) + len(extra))
        + [pl.BlockSpec(memory_space=pl.ANY)],
        out_specs=[vmem] * len(shapes),
        scratch_shapes=[
            pltpu.VMEM(slab.shape, BF16),
            pltpu.VMEM(buf.shape, BF16),
            pltpu.SemaphoreType.DMA((SLOTS,)),
            pltpu.SMEM((users,), jnp.int32),
        ]
        + [pltpu.VMEM(x.shape, x.dtype) for x in scratch],
        compiler_params=pltpu.CompilerParams(vmem_limit_bytes=held + SPARE),
        cost_estimate=pl.CostEstimate(flops=0, bytes_accessed=cost, transcendentals=0),
    )(*scalars, *pieces, *extra, tiles)


def near_sums(scalars, pieces, tiles, rows):
    tile_size = tiles.shape[1]
    shapes = [jax.ShapeDtypeStruct((rows, kc, tile_size), F32) for kc in CHUNKS]
    return tile_call(
        functools.partial(near_kernel, len(pieces), len(pieces[0])), scalars, pieces, [], tiles, shapes, [], NEAR_COST
    )


def far_sums(scalars, pieces, start, tiles, orders, cost):
    rows, kc, tile_size = start.shape
    width = tile_size // len(orders)
    shapes = []
    for _ in orders:
        shapes.append(jax.ShapeDtypeStruct((rows // 2, kc, width), F32))
        shapes.append(jax.ShapeDtypeStruct((rows // 2, kc, width), BF16))
    return tile_call(
        functools.partial(far_kernel, len(pieces), len(pieces[0]), orders),
        scalars,
        pieces,
        [start],
        tiles,
        shapes,
        [jax.ShapeDtypeStruct(start.shape, F32)],
        cost,
    )


def mm(a, b):
    return lax.dot_general(a, b, (((1,), (0,)), ((), ())), precision=HIGH, preferred_element_type=F32)


def mmt(a, b):
    return lax.dot_general(a, b, (((1,), (1,)), ((), ())), precision=HIGH, preferred_element_type=F32)


def factor_kernel(packed, inverse, good):
    n = packed.shape[1]
    r = lax.broadcasted_iota(jnp.int32, (n, n), 0)
    c = lax.broadcasted_iota(jnp.int32, (n, n), 1)
    mixed = packed[:n]
    flipped = mixed.T
    side = packed[n : 2 * n]
    tail = jnp.broadcast_to(packed[2 * n : 2 * n + 1], (n, n))
    first = jnp.where(r >= c, mixed, flipped)
    second = jnp.where(r < c, mixed, jnp.where(r > c, flipped, tail))
    gram = jnp.concatenate(
        [jnp.concatenate([first, side.T], axis=1), jnp.concatenate([side, second], axis=1)], axis=0
    )
    m = 2 * n
    rr = lax.broadcasted_iota(jnp.int32, (m, m), 0)
    cc = lax.broadcasted_iota(jnp.int32, (m, m), 1)
    on = rr == cc
    eye = jnp.where(on, 1.0, 0.0).astype(F32)
    low = jnp.where(rr > cc, 1.0, jnp.where(on, 0.5, 0.0)).astype(F32)
    diag = jnp.where(on, gram, 0.0)
    scale_row = lax.rsqrt(jnp.sum(diag, axis=0, keepdims=True))
    scale_col = lax.rsqrt(jnp.sum(diag, axis=1, keepdims=True))
    unit = gram * scale_row * scale_col
    off = unit - eye
    square = jnp.dot(off, off, preferred_element_type=F32)
    spread = jnp.max(jnp.sum(jnp.abs(jnp.dot(square, square, preferred_element_type=F32)), axis=1))
    w = eye - low * off
    for _ in range(NEWTON):
        err = mmt(mm(w, unit), w) - eye
        w = w - mm(low * err, w)
    last = jnp.max(jnp.sum(jnp.abs(err), axis=1))
    inflation = jnp.max(jnp.sum(w * w, axis=0))
    inverse[...] = w * scale_row
    good[0] = jnp.where((spread < 0.025) & (last < 0.01) & (inflation < 1.1), 1, 0)


def factor(packed):
    n = packed.shape[1]
    return pl.pallas_call(
        factor_kernel,
        out_shape=[jax.ShapeDtypeStruct((2 * n, 2 * n), F32), jax.ShapeDtypeStruct((1,), jnp.int32)],
        in_specs=[pl.BlockSpec(memory_space=pltpu.VMEM)],
        out_specs=[pl.BlockSpec(memory_space=pltpu.VMEM), pl.BlockSpec(memory_space=pltpu.SMEM)],
        compiler_params=pltpu.CompilerParams(vmem_limit_bytes=24 * 2**20),
        cost_estimate=pl.CostEstimate(
            flops=0, bytes_accessed=FACTOR_COST, transcendentals=0
        ),
    )(packed)


def last_kernel(inverse, early, keep0, keep1, came, out):
    left = keep0[0] + came[0].astype(F32)
    right = keep1[0] + came[1].astype(F32)
    total = jnp.concatenate([early[...], jnp.concatenate([left, right], axis=1)], axis=0)
    w = inverse[...]
    wh, th = w.astype(BF16), total.astype(BF16)
    wl = (w - wh.astype(F32)).astype(BF16)
    tl = (total - th.astype(F32)).astype(BF16)
    small = jnp.dot(wh, tl, preferred_element_type=F32) + jnp.dot(wl, th, preferred_element_type=F32)
    out[...] = jnp.dot(wh, th, preferred_element_type=F32) + small


def last(inverse, early, keeps, came):
    vmem = pl.BlockSpec(memory_space=pltpu.VMEM)
    return pl.pallas_call(
        last_kernel,
        out_shape=jax.ShapeDtypeStruct((inverse.shape[0], early.shape[1]), F32),
        in_specs=[vmem] * 5,
        out_specs=vmem,
        compiler_params=pltpu.CompilerParams(vmem_limit_bytes=16 * 2**20),
    )(inverse, early, *keeps, came)


def full_path(rows, cols, sketch, tiles, tile_user, tile_item, tile_count, item_owner, packed):
    n = packed.shape[1]
    r = lax.broadcasted_iota(jnp.int32, (n, n), 0)
    c = lax.broadcasted_iota(jnp.int32, (n, n), 1)
    mixed, side, tail = packed[:n], packed[n : 2 * n], packed[2 * n : 2 * n + 1]
    first = jnp.where(r >= c, mixed, mixed.T)
    second = jnp.where(r < c, mixed, jnp.where(r > c, mixed.T, tail))
    gram = jnp.block([[first, side.T], [side, second]])
    lower = jnp.linalg.cholesky(gram)
    basis = lax.linalg.triangular_solve(lower, sketch, left_side=False, lower=True, transpose_a=True).astype(BF16)
    have = {0: basis}
    for bit in bits_of(cols):
        for place in list(have):
            have[place | bit] = swap(have[place], "cols", cols, bit)
    slab = jnp.concatenate([have[i] for i in range(cols)], axis=0)
    col = lax.axis_index("cols")
    row = lax.axis_index("rows")
    per_piece = sketch.shape[0] // tiles.shape[2]
    owner = item_owner[0]
    tile_size = tiles.shape[2]

    def step(index, sums):
        user = tile_user[index]
        block = lax.bitwise_xor(user // per_piece, col) * per_piece + user % per_piece
        part_rows = lax.dynamic_slice_in_dim(slab, block * tile_size, tile_size, 0)
        part = lax.dot_general(part_rows, tiles[index], (((0,), (0,)), ((), ())), preferred_element_type=F32)
        place = lax.bitwise_xor(owner[tile_item[index]], row)
        now = lax.dynamic_index_in_dim(sums, place, 0, keepdims=False)
        return lax.dynamic_update_index_in_dim(sums, now + part, place, 0)

    totals = jnp.zeros((owner.shape[0], sketch.shape[1], tile_size), F32)
    totals = lax.fori_loop(0, tile_count[0], step, totals)
    for bit in bits_of(rows):
        totals = totals[:bit] + swap(totals[bit:], "rows", rows, bit)
    return totals[0]


def after(value, *others):
    return lax.optimization_barrier((value, *others))[0]


def exchange(lanes, rows):
    groups = []
    for bit in sorted({lane[2] for lane in lanes}):
        members = [i for i, lane in enumerate(lanes) if lane[2] == bit]
        sent = [lanes[i][1].reshape(-1, lanes[i][1].shape[2]) for i in members]
        groups.append((members, swap(jnp.concatenate(sent, axis=0), "rows", rows, 1 << bit)))
    return groups


def received(lanes, groups):
    got = [None] * len(lanes)
    for members, came in groups:
        first = 0
        for i in members:
            shape = lanes[i][1].shape
            size = shape[0] * shape[1]
            got[i] = came[first : first + size].reshape(shape)
            first += size
    return [lane[0] + g.astype(F32) for lane, g in zip(lanes, got)]


def split(total):
    half = total.shape[0] // 2
    return total[:half], total[half:].astype(BF16)


def body(rows, cols, sketch, tiles, tile_user, tile_item, tile_count, item_owner):
    row_bits = rows.bit_length() - 1
    first_order = tuple(range(row_bits))
    orders = (first_order, (1, 0) + first_order[2:])
    row = lax.axis_index("rows")
    col = lax.axis_index("cols")
    meta = jnp.stack([tile_count[0], row, col]).astype(jnp.int32)
    scalars = (tile_user, tile_item, item_owner[0], meta)
    far_bit, *near_bits = bits_of(cols)

    def spread(piece):
        have = {0: piece}
        for bit in near_bits:
            for place in list(have):
                have[place | bit] = swap(have[place], "cols", cols, bit)
        return [have[i] for i in range(cols // 2)]

    fence = lax.optimization_barrier
    far = far_bit
    flat, *chunks = split_sketch(sketch)
    near = list(zip(*[spread(c) for c in chunks]))
    crossed = [swap(c, "cols", cols, far) for c in chunks]
    packed = packed_gram(flat)
    for bit in near_bits:
        packed = packed + swap(packed, "cols", cols, bit)
    came = swap(packed, "rows", rows, 2)
    near[0] = (after(near[0][0], packed), *near[0][1:])
    sums = near_sums(scalars, near, tiles, rows)
    packed, came, *sums = fence((packed, came, *sums))
    packed = packed + came
    came = swap(packed, "rows", rows, 4)
    crossed[0] = after(crossed[0], packed)
    outs = far_sums(scalars, [[p] for p in spread(crossed[0])], sums[0], tiles, orders, EARLY_COST)
    packed, came, *outs = fence((packed, came, *outs))
    packed = packed + came
    came = swap(packed, "cols", cols, far)
    lanes = [(outs[2 * o], outs[2 * o + 1], order[0]) for o, order in enumerate(orders)]
    groups = exchange(lanes, rows)
    crossed[1] = after(crossed[1], packed)
    later = far_sums(scalars, [[p] for p in spread(crossed[1])], sums[1], tiles, orders, LATE_COST)
    flying = [g[1] for g in groups]
    packed, came, *rest = fence((packed, came, *flying, *later))
    groups = [(g[0], x) for g, x in zip(groups, rest)]
    later = rest[len(groups) :]
    packed = packed + came
    stages = [1] + [1 << b for b in range(3, row_bits)]

    totals = received(lanes, groups)
    late = [(later[2 * o], later[2 * o + 1]) for o in range(len(orders))]
    for step in range(1, row_bits + 1):
        lanes = []
        if step < row_bits:
            lanes += [(*split(t), order[step]) for t, order in zip(totals, orders)]
        lanes += [(*pair, order[step - 1]) for pair, order in zip(late, orders)]
        groups = exchange(lanes, rows)
        flying = [g[1] for g in groups]
        if step <= len(stages):
            came = swap(packed, "rows", rows, stages[step - 1])
            packed, came, *flying = fence((packed, came, *flying))
            packed = packed + came
        if step == len(stages) + 1:
            inverse, good = factor(after(packed, *[lane[1] for lane in lanes]))
            inverse, *flying = fence((inverse, *flying))
        groups = [(g[0], x) for g, x in zip(groups, flying)]
        if step < row_bits:
            new = received(lanes, groups)
            totals, new = new[: len(orders)], new[len(orders) :]
            late = [split(t) for t in new]
        if step == row_bits - 1:
            early = jnp.concatenate([t[0] for t in totals], axis=1)
    keeps = [lane[0] for lane in lanes]
    came = groups[0][1].reshape(len(lanes), *lanes[0][1].shape[1:])
    out = lax.cond(
        good[0] > 0,
        lambda: last(inverse, early, keeps, came),
        lambda: full_path(rows, cols, sketch, tiles, tile_user, tile_item, tile_count, item_owner, packed),
    )
    return out[None, None]


def solution(mesh):
    placed = (
        P(("rows", "cols"), None),
        P(("rows", "cols"), None, None),
        P(("rows", "cols")),
        P(("rows", "cols")),
        P(("rows", "cols")),
        P("cols", None),
    )
    return jax.shard_map(
        functools.partial(body, mesh.shape["rows"], mesh.shape["cols"]),
        mesh=mesh,
        in_specs=placed,
        out_specs=P("rows", "cols", None, None),
        check_vma=False,
    )
```

```python
import functools

import jax
import jax.numpy as jnp
from jax import lax
from jax.experimental import pallas as pl
from jax.experimental.pallas import tpu as pltpu
from jax.sharding import PartitionSpec as P

F32 = jnp.float32
BF16 = jnp.bfloat16
HIGH = lax.Precision.HIGHEST
SLOTS = 12
SPARE = 4 * 2**20
GROUP = 4
NEAR_COST = 200 * 2**20
EARLY_COST = 1024
LATE_COST = 1024
FACTOR_COST = 200 * 2**20
CHUNKS = (160, 96)
NEWTON = 2


def bits_of(count):
    return [1 << b for b in reversed(range(count.bit_length() - 1))]


def swap(x, axis, count, bit):
    return lax.ppermute(x, axis, [(i, i ^ bit) for i in range(count)])


def places(order, parity):
    found = [parity << order[0]]
    for bit in reversed(order[1:]):
        found = found + [p | (1 << bit) for p in found]
    return found


def run_tiles(base, span, per_piece, users, items, owner, meta, tiles, slab, add, buf, sems, order):
    count, row, col = meta[0], meta[1], meta[2]

    def relative(t):
        user = users[t]
        return lax.bitwise_xor(user // per_piece, col) - base, lax.rem(user, per_piece)

    def choose(t, n):
        piece, _ = relative(t)
        order[n] = t
        return n + jnp.where((piece >= 0) & (piece < span), 1, 0)

    live = lax.fori_loop(0, count, choose, 0)

    def fetch(i):
        slot = lax.rem(i, SLOTS)
        return pltpu.make_async_copy(tiles.at[order[i]], buf.at[slot], sems.at[slot])

    for i in range(SLOTS):
        @pl.when(i < live)
        def _():
            fetch(i).start()

    def group(first, size):
        for q in range(size):
            fetch(first + q).wait()
        found = []
        for q in range(size):
            piece, part = relative(order[first + q])
            both = jnp.dot(
                slab[piece * per_piece + part],
                buf[lax.rem(first + q, SLOTS)],
                preferred_element_type=F32,
            )
            found.append(both)
        for q in range(size):
            add(lax.bitwise_xor(owner[items[order[first + q]]], row), found[q])
        for q in range(size):
            @pl.when(first + q + SLOTS < live)
            def _():
                fetch(first + q + SLOTS).start()

    def finish():
        groups = live // GROUP

        def many(g, _):
            group(g * GROUP, GROUP)
            return 0

        def one(i, _):
            group(i, 1)
            return 0

        lax.fori_loop(0, groups, many, 0)
        lax.fori_loop(groups * GROUP, live, one, 0)

    return finish


def split_kernel(sketch, flat, *chunks):
    flat[...] = sketch[...].T
    first = 0
    for chunk in chunks:
        kc = chunk.shape[0] // 2
        rows = flat[first : first + kc, :]
        high = rows.astype(BF16)
        chunk[:kc, :] = high
        chunk[kc:, :] = (rows - high.astype(F32)).astype(BF16)
        first += kc


def split_sketch(sketch):
    users, width = sketch.shape
    vmem = pl.BlockSpec(memory_space=pltpu.VMEM)
    return pl.pallas_call(
        split_kernel,
        out_shape=[jax.ShapeDtypeStruct((width, users), F32)]
        + [jax.ShapeDtypeStruct((2 * k, users), BF16) for k in CHUNKS],
        in_specs=[vmem],
        out_specs=[vmem] * (1 + len(CHUNKS)),
        compiler_params=pltpu.CompilerParams(vmem_limit_bytes=16 * 2**20),
    )(sketch)


def gram_kernel(flat, packed):
    n = packed.shape[1]
    top, low = flat[:n, :], flat[n:, :]
    second = mmt(low, low)
    r = lax.broadcasted_iota(jnp.int32, (n, n), 0)
    c = lax.broadcasted_iota(jnp.int32, (n, n), 1)
    packed[:n] = jnp.where(r >= c, mmt(top, top), second)
    packed[n : 2 * n] = mmt(low, top)
    tail = jnp.sum(jnp.where(r == c, second, 0.0), axis=0, keepdims=True)
    packed[2 * n :] = jnp.broadcast_to(tail, (8, n))


def packed_gram(flat):
    n = flat.shape[0] // 2
    vmem = pl.BlockSpec(memory_space=pltpu.VMEM)
    return pl.pallas_call(
        gram_kernel,
        out_shape=jax.ShapeDtypeStruct((2 * n + 8, n), F32),
        in_specs=[vmem],
        out_specs=vmem,
        compiler_params=pltpu.CompilerParams(vmem_limit_bytes=16 * 2**20),
    )(flat)


def fill(slab, pieces, per_piece):
    tile_size = slab.shape[2]
    for c, blocks in enumerate(pieces):
        first = 0
        for block in blocks:
            stop = first + block.shape[0]
            for h in range(per_piece):
                slab[c * per_piece + h, first:stop, :] = block[:, h * tile_size : (h + 1) * tile_size]
            first = stop


def near_kernel(span, blocks, users, items, owner, meta, *refs):
    pieces = [refs[i * blocks : (i + 1) * blocks] for i in range(span)]
    tiles = refs[span * blocks]
    sums = refs[span * blocks + 1 : -4]
    slab, buf, sems, order = refs[-4:]
    per_piece = refs[0].shape[1] // tiles.shape[1]

    def add(place, both):
        first = 0
        for part in sums:
            kc = part.shape[1]
            part[place] += both[first : first + kc] + both[first + kc : first + 2 * kc]
            first += 2 * kc

    finish = run_tiles(
        0, span, per_piece, users, items, owner, meta, tiles, slab, add, buf, sems, order
    )
    for part in sums:
        part[...] = jnp.zeros_like(part)
    fill(slab, pieces, per_piece)
    finish()


def far_kernel(span, blocks, orders, users, items, owner, meta, *refs):
    pieces = [refs[i * blocks : (i + 1) * blocks] for i in range(span)]
    start, tiles = refs[span * blocks], refs[span * blocks + 1]
    outs = refs[span * blocks + 2 : -5]
    slab, buf, sems, order, acc = refs[-5:]
    tile_size = tiles.shape[1]
    per_piece = refs[0].shape[1] // tile_size
    kc = start.shape[1]

    def add(place, both):
        acc[place] += both[:kc] + both[kc:]

    finish = run_tiles(
        span, span, per_piece, users, items, owner, meta, tiles, slab, add, buf, sems, order
    )
    acc[...] = start[...]
    fill(slab, pieces, per_piece)
    finish()
    width = tile_size // len(orders)
    for o, bits in enumerate(orders):
        cut = slice(o * width, (o + 1) * width)
        for k, place in enumerate(places(bits, 0)):
            outs[2 * o][k] = acc[place, :, cut]
        for k, place in enumerate(places(bits, 1)):
            outs[2 * o + 1][k] = acc[place, :, cut].astype(BF16)


def tile_call(kernel, scalars, pieces, extra, tiles, shapes, scratch, cost):
    users = scalars[0].shape[0]
    tile_size = tiles.shape[1]
    count = len(pieces) * pieces[0][0].shape[1] // tile_size
    depth = sum(block.shape[0] for block in pieces[0])
    pieces = [block for blocks in pieces for block in blocks]
    smem = pl.BlockSpec(memory_space=pltpu.SMEM)
    vmem = pl.BlockSpec(memory_space=pltpu.VMEM)
    slab = jax.ShapeDtypeStruct((count, depth, tile_size), BF16)
    buf = jax.ShapeDtypeStruct((SLOTS, tile_size, tile_size), BF16)
    held = sum(x.size * x.dtype.itemsize for x in (*pieces, *extra, *shapes, *scratch, slab, buf))
    return pl.pallas_call(
        kernel,
        out_shape=shapes,
        in_specs=[smem] * len(scalars)
        + [vmem] * (len(pieces) + len(extra))
        + [pl.BlockSpec(memory_space=pl.ANY)],
        out_specs=[vmem] * len(shapes),
        scratch_shapes=[
            pltpu.VMEM(slab.shape, BF16),
            pltpu.VMEM(buf.shape, BF16),
            pltpu.SemaphoreType.DMA((SLOTS,)),
            pltpu.SMEM((users,), jnp.int32),
        ]
        + [pltpu.VMEM(x.shape, x.dtype) for x in scratch],
        compiler_params=pltpu.CompilerParams(vmem_limit_bytes=held + SPARE),
        cost_estimate=pl.CostEstimate(flops=0, bytes_accessed=cost, transcendentals=0),
    )(*scalars, *pieces, *extra, tiles)


def near_sums(scalars, pieces, tiles, rows):
    tile_size = tiles.shape[1]
    shapes = [jax.ShapeDtypeStruct((rows, kc, tile_size), F32) for kc in CHUNKS]
    return tile_call(
        functools.partial(near_kernel, len(pieces), len(pieces[0])), scalars, pieces, [], tiles, shapes, [], NEAR_COST
    )


def far_sums(scalars, pieces, start, tiles, orders, cost):
    rows, kc, tile_size = start.shape
    width = tile_size // len(orders)
    shapes = []
    for _ in orders:
        shapes.append(jax.ShapeDtypeStruct((rows // 2, kc, width), F32))
        shapes.append(jax.ShapeDtypeStruct((rows // 2, kc, width), BF16))
    return tile_call(
        functools.partial(far_kernel, len(pieces), len(pieces[0]), orders),
        scalars,
        pieces,
        [start],
        tiles,
        shapes,
        [jax.ShapeDtypeStruct(start.shape, F32)],
        cost,
    )


def mm(a, b):
    return lax.dot_general(a, b, (((1,), (0,)), ((), ())), precision=HIGH, preferred_element_type=F32)


def mmt(a, b):
    return lax.dot_general(a, b, (((1,), (1,)), ((), ())), precision=HIGH, preferred_element_type=F32)


def factor_kernel(packed, inverse, good):
    n = packed.shape[1]
    r = lax.broadcasted_iota(jnp.int32, (n, n), 0)
    c = lax.broadcasted_iota(jnp.int32, (n, n), 1)
    mixed = packed[:n]
    flipped = mixed.T
    side = packed[n : 2 * n]
    tail = jnp.broadcast_to(packed[2 * n : 2 * n + 1], (n, n))
    first = jnp.where(r >= c, mixed, flipped)
    second = jnp.where(r < c, mixed, jnp.where(r > c, flipped, tail))
    gram = jnp.concatenate(
        [jnp.concatenate([first, side.T], axis=1), jnp.concatenate([side, second], axis=1)], axis=0
    )
    m = 2 * n
    rr = lax.broadcasted_iota(jnp.int32, (m, m), 0)
    cc = lax.broadcasted_iota(jnp.int32, (m, m), 1)
    on = rr == cc
    eye = jnp.where(on, 1.0, 0.0).astype(F32)
    low = jnp.where(rr > cc, 1.0, jnp.where(on, 0.5, 0.0)).astype(F32)
    diag = jnp.where(on, gram, 0.0)
    scale_row = lax.rsqrt(jnp.sum(diag, axis=0, keepdims=True))
    scale_col = lax.rsqrt(jnp.sum(diag, axis=1, keepdims=True))
    unit = gram * scale_row * scale_col
    off = unit - eye
    square = jnp.dot(off, off, preferred_element_type=F32)
    spread = jnp.max(jnp.sum(jnp.abs(jnp.dot(square, square, preferred_element_type=F32)), axis=1))
    w = eye - low * off
    for _ in range(NEWTON):
        err = mmt(mm(w, unit), w) - eye
        w = w - mm(low * err, w)
    last = jnp.max(jnp.sum(jnp.abs(err), axis=1))
    inflation = jnp.max(jnp.sum(w * w, axis=0))
    inverse[...] = w * scale_row
    good[0] = jnp.where((spread < 0.025) & (last < 0.01) & (inflation < 1.1), 1, 0)


def factor(packed):
    n = packed.shape[1]
    return pl.pallas_call(
        factor_kernel,
        out_shape=[jax.ShapeDtypeStruct((2 * n, 2 * n), F32), jax.ShapeDtypeStruct((1,), jnp.int32)],
        in_specs=[pl.BlockSpec(memory_space=pltpu.VMEM)],
        out_specs=[pl.BlockSpec(memory_space=pltpu.VMEM), pl.BlockSpec(memory_space=pltpu.SMEM)],
        compiler_params=pltpu.CompilerParams(vmem_limit_bytes=24 * 2**20),
        cost_estimate=pl.CostEstimate(
            flops=0, bytes_accessed=FACTOR_COST, transcendentals=0
        ),
    )(packed)


def last_kernel(inverse, early, keep0, keep1, came, out):
    left = keep0[0] + came[0].astype(F32)
    right = keep1[0] + came[1].astype(F32)
    total = jnp.concatenate([early[...], jnp.concatenate([left, right], axis=1)], axis=0)
    w = inverse[...]
    wh, th = w.astype(BF16), total.astype(BF16)
    wl = (w - wh.astype(F32)).astype(BF16)
    tl = (total - th.astype(F32)).astype(BF16)
    small = jnp.dot(wh, tl, preferred_element_type=F32) + jnp.dot(wl, th, preferred_element_type=F32)
    out[...] = jnp.dot(wh, th, preferred_element_type=F32) + small


def last(inverse, early, keeps, came):
    vmem = pl.BlockSpec(memory_space=pltpu.VMEM)
    return pl.pallas_call(
        last_kernel,
        out_shape=jax.ShapeDtypeStruct((inverse.shape[0], early.shape[1]), F32),
        in_specs=[vmem] * 5,
        out_specs=vmem,
        compiler_params=pltpu.CompilerParams(vmem_limit_bytes=16 * 2**20),
    )(inverse, early, *keeps, came)


def full_path(rows, cols, sketch, tiles, tile_user, tile_item, tile_count, item_owner, packed):
    n = packed.shape[1]
    r = lax.broadcasted_iota(jnp.int32, (n, n), 0)
    c = lax.broadcasted_iota(jnp.int32, (n, n), 1)
    mixed, side, tail = packed[:n], packed[n : 2 * n], packed[2 * n : 2 * n + 1]
    first = jnp.where(r >= c, mixed, mixed.T)
    second = jnp.where(r < c, mixed, jnp.where(r > c, mixed.T, tail))
    gram = jnp.block([[first, side.T], [side, second]])
    lower = jnp.linalg.cholesky(gram)
    basis = lax.linalg.triangular_solve(lower, sketch, left_side=False, lower=True, transpose_a=True).astype(BF16)
    have = {0: basis}
    for bit in bits_of(cols):
        for place in list(have):
            have[place | bit] = swap(have[place], "cols", cols, bit)
    slab = jnp.concatenate([have[i] for i in range(cols)], axis=0)
    col = lax.axis_index("cols")
    row = lax.axis_index("rows")
    per_piece = sketch.shape[0] // tiles.shape[2]
    owner = item_owner[0]
    tile_size = tiles.shape[2]

    def step(index, sums):
        user = tile_user[index]
        block = lax.bitwise_xor(user // per_piece, col) * per_piece + user % per_piece
        part_rows = lax.dynamic_slice_in_dim(slab, block * tile_size, tile_size, 0)
        part = lax.dot_general(part_rows, tiles[index], (((0,), (0,)), ((), ())), preferred_element_type=F32)
        place = lax.bitwise_xor(owner[tile_item[index]], row)
        now = lax.dynamic_index_in_dim(sums, place, 0, keepdims=False)
        return lax.dynamic_update_index_in_dim(sums, now + part, place, 0)

    totals = jnp.zeros((owner.shape[0], sketch.shape[1], tile_size), F32)
    totals = lax.fori_loop(0, tile_count[0], step, totals)
    for bit in bits_of(rows):
        totals = totals[:bit] + swap(totals[bit:], "rows", rows, bit)
    return totals[0]


def after(value, *others):
    return lax.optimization_barrier((value, *others))[0]


def exchange(lanes, rows):
    groups = []
    for bit in sorted({lane[2] for lane in lanes}):
        members = [i for i, lane in enumerate(lanes) if lane[2] == bit]
        sent = [lanes[i][1].reshape(-1, lanes[i][1].shape[2]) for i in members]
        groups.append((members, swap(jnp.concatenate(sent, axis=0), "rows", rows, 1 << bit)))
    return groups


def received(lanes, groups):
    got = [None] * len(lanes)
    for members, came in groups:
        first = 0
        for i in members:
            shape = lanes[i][1].shape
            size = shape[0] * shape[1]
            got[i] = came[first : first + size].reshape(shape)
            first += size
    return [lane[0] + g.astype(F32) for lane, g in zip(lanes, got)]


def split(total):
    half = total.shape[0] // 2
    return total[:half], total[half:].astype(BF16)


def body(rows, cols, sketch, tiles, tile_user, tile_item, tile_count, item_owner):
    row_bits = rows.bit_length() - 1
    first_order = tuple(range(row_bits))
    orders = (first_order, (1, 0) + first_order[2:])
    row = lax.axis_index("rows")
    col = lax.axis_index("cols")
    meta = jnp.stack([tile_count[0], row, col]).astype(jnp.int32)
    scalars = (tile_user, tile_item, item_owner[0], meta)
    far_bit, *near_bits = bits_of(cols)

    def spread(piece):
        have = {0: piece}
        for bit in near_bits:
            for place in list(have):
                have[place | bit] = swap(have[place], "cols", cols, bit)
        return [have[i] for i in range(cols // 2)]

    fence = lax.optimization_barrier
    far = far_bit
    flat, *chunks = split_sketch(sketch)
    near = list(zip(*[spread(c) for c in chunks]))
    crossed = [swap(c, "cols", cols, far) for c in chunks]
    packed = packed_gram(flat)
    for bit in near_bits:
        packed = packed + swap(packed, "cols", cols, bit)
    came = swap(packed, "rows", rows, 2)
    near[0] = (after(near[0][0], packed), *near[0][1:])
    sums = near_sums(scalars, near, tiles, rows)
    packed, came, *sums = fence((packed, came, *sums))
    packed = packed + came
    came = swap(packed, "rows", rows, 4)
    crossed[0] = after(crossed[0], packed)
    outs = far_sums(scalars, [[p] for p in spread(crossed[0])], sums[0], tiles, orders, EARLY_COST)
    packed, came, *outs = fence((packed, came, *outs))
    packed = packed + came
    came = swap(packed, "cols", cols, far)
    lanes = [(outs[2 * o], outs[2 * o + 1], order[0]) for o, order in enumerate(orders)]
    groups = exchange(lanes, rows)
    crossed[1] = after(crossed[1], packed)
    later = far_sums(scalars, [[p] for p in spread(crossed[1])], sums[1], tiles, orders, LATE_COST)
    flying = [g[1] for g in groups]
    packed, came, *rest = fence((packed, came, *flying, *later))
    groups = [(g[0], x) for g, x in zip(groups, rest)]
    later = rest[len(groups) :]
    packed = packed + came
    stages = [1] + [1 << b for b in range(3, row_bits)]

    totals = received(lanes, groups)
    late = [(later[2 * o], later[2 * o + 1]) for o in range(len(orders))]
    for step in range(1, row_bits + 1):
        lanes = []
        if step < row_bits:
            lanes += [(*split(t), order[step]) for t, order in zip(totals, orders)]
        lanes += [(*pair, order[step - 1]) for pair, order in zip(late, orders)]
        groups = exchange(lanes, rows)
        flying = [g[1] for g in groups]
        sends = [lane[1] for lane in lanes]
        if step > 1 and step <= len(stages) + 1:
            packed = packed + after(came, *sends)
        if step <= len(stages):
            came = swap(packed, "rows", rows, stages[step - 1])
        if step == len(stages) + 1:
            inverse, good = factor(after(packed, *sends))
            free = [i for i, g in enumerate(groups) if max(g[0]) < len(lanes) - len(orders)]
            inverse, *tied = fence((inverse, *[flying[i] for i in free]))
            for i, x in zip(free, tied):
                flying[i] = x
        groups = [(g[0], x) for g, x in zip(groups, flying)]
        if step < row_bits:
            new = received(lanes, groups)
            totals, new = new[: len(orders)], new[len(orders) :]
            late = [split(t) for t in new]
        if step == row_bits - 1:
            early = jnp.concatenate([t[0] for t in totals], axis=1)
    keeps = [lane[0] for lane in lanes]
    came = groups[0][1].reshape(len(lanes), *lanes[0][1].shape[1:])
    out = lax.cond(
        good[0] > 0,
        lambda: last(inverse, early, keeps, came),
        lambda: full_path(rows, cols, sketch, tiles, tile_user, tile_item, tile_count, item_owner, packed),
    )
    return out[None, None]


def solution(mesh):
    placed = (
        P(("rows", "cols"), None),
        P(("rows", "cols"), None, None),
        P(("rows", "cols")),
        P(("rows", "cols")),
        P(("rows", "cols")),
        P("cols", None),
    )
    return jax.shard_map(
        functools.partial(body, mesh.shape["rows"], mesh.shape["cols"]),
        mesh=mesh,
        in_specs=placed,
        out_specs=P("rows", "cols", None, None),
        check_vma=False,
    )
```

```python
import functools

import jax
import jax.numpy as jnp
from jax import lax
from jax.experimental import pallas as pl
from jax.experimental.pallas import tpu as pltpu
from jax.sharding import PartitionSpec as P

F32 = jnp.float32
BF16 = jnp.bfloat16
HIGH = lax.Precision.HIGHEST
SLOTS = 12
SPARE = 4 * 2**20
GROUP = 4
NEAR_COST = 200 * 2**20
EARLY_COST = 1024
LATE_COST = 1024
FACTOR_COST = 200 * 2**20
CHUNKS = (160, 96)
NEWTON = 2


def bits_of(count):
    return [1 << b for b in reversed(range(count.bit_length() - 1))]


def swap(x, axis, count, bit):
    return lax.ppermute(x, axis, [(i, i ^ bit) for i in range(count)])


def places(order, parity):
    found = [parity << order[0]]
    for bit in reversed(order[1:]):
        found = found + [p | (1 << bit) for p in found]
    return found


def run_tiles(base, span, per_piece, users, items, owner, meta, tiles, slab, add, buf, sems, order):
    count, row, col = meta[0], meta[1], meta[2]

    def relative(t):
        user = users[t]
        return lax.bitwise_xor(user // per_piece, col) - base, lax.rem(user, per_piece)

    def choose(t, n):
        piece, _ = relative(t)
        order[n] = t
        return n + jnp.where((piece >= 0) & (piece < span), 1, 0)

    live = lax.fori_loop(0, count, choose, 0)

    def fetch(i):
        slot = lax.rem(i, SLOTS)
        return pltpu.make_async_copy(tiles.at[order[i]], buf.at[slot], sems.at[slot])

    for i in range(SLOTS):
        @pl.when(i < live)
        def _():
            fetch(i).start()

    def group(first, size):
        for q in range(size):
            fetch(first + q).wait()
        found = []
        for q in range(size):
            piece, part = relative(order[first + q])
            both = jnp.dot(
                slab[piece * per_piece + part],
                buf[lax.rem(first + q, SLOTS)],
                preferred_element_type=F32,
            )
            found.append(both)
        for q in range(size):
            add(lax.bitwise_xor(owner[items[order[first + q]]], row), found[q])
        for q in range(size):
            @pl.when(first + q + SLOTS < live)
            def _():
                fetch(first + q + SLOTS).start()

    def finish():
        groups = live // GROUP

        def many(g, _):
            group(g * GROUP, GROUP)
            return 0

        def one(i, _):
            group(i, 1)
            return 0

        lax.fori_loop(0, groups, many, 0)
        lax.fori_loop(groups * GROUP, live, one, 0)

    return finish


def split_kernel(sketch, flat, *chunks):
    flat[...] = sketch[...].T
    first = 0
    for chunk in chunks:
        kc = chunk.shape[0] // 2
        rows = flat[first : first + kc, :]
        high = rows.astype(BF16)
        chunk[:kc, :] = high
        chunk[kc:, :] = (rows - high.astype(F32)).astype(BF16)
        first += kc


def split_sketch(sketch):
    users, width = sketch.shape
    vmem = pl.BlockSpec(memory_space=pltpu.VMEM)
    return pl.pallas_call(
        split_kernel,
        out_shape=[jax.ShapeDtypeStruct((width, users), F32)]
        + [jax.ShapeDtypeStruct((2 * k, users), BF16) for k in CHUNKS],
        in_specs=[vmem],
        out_specs=[vmem] * (1 + len(CHUNKS)),
        compiler_params=pltpu.CompilerParams(vmem_limit_bytes=16 * 2**20),
    )(sketch)


def gram_kernel(flat, packed):
    n = packed.shape[1]
    top, low = flat[:n, :], flat[n:, :]
    second = mmt(low, low)
    r = lax.broadcasted_iota(jnp.int32, (n, n), 0)
    c = lax.broadcasted_iota(jnp.int32, (n, n), 1)
    packed[:n] = jnp.where(r >= c, mmt(top, top), second)
    packed[n : 2 * n] = mmt(low, top)
    tail = jnp.sum(jnp.where(r == c, second, 0.0), axis=0, keepdims=True)
    packed[2 * n :] = jnp.broadcast_to(tail, (8, n))


def packed_gram(flat):
    n = flat.shape[0] // 2
    vmem = pl.BlockSpec(memory_space=pltpu.VMEM)
    return pl.pallas_call(
        gram_kernel,
        out_shape=jax.ShapeDtypeStruct((2 * n + 8, n), F32),
        in_specs=[vmem],
        out_specs=vmem,
        compiler_params=pltpu.CompilerParams(vmem_limit_bytes=16 * 2**20),
    )(flat)


def fill(slab, pieces, per_piece):
    tile_size = slab.shape[2]
    for c, blocks in enumerate(pieces):
        first = 0
        for block in blocks:
            stop = first + block.shape[0]
            for h in range(per_piece):
                slab[c * per_piece + h, first:stop, :] = block[:, h * tile_size : (h + 1) * tile_size]
            first = stop


def near_kernel(span, blocks, users, items, owner, meta, *refs):
    pieces = [refs[i * blocks : (i + 1) * blocks] for i in range(span)]
    tiles = refs[span * blocks]
    sums = refs[span * blocks + 1 : -4]
    slab, buf, sems, order = refs[-4:]
    per_piece = refs[0].shape[1] // tiles.shape[1]

    def add(place, both):
        first = 0
        for part in sums:
            kc = part.shape[1]
            part[place] += both[first : first + kc] + both[first + kc : first + 2 * kc]
            first += 2 * kc

    finish = run_tiles(
        0, span, per_piece, users, items, owner, meta, tiles, slab, add, buf, sems, order
    )
    for part in sums:
        part[...] = jnp.zeros_like(part)
    fill(slab, pieces, per_piece)
    finish()


def far_kernel(span, blocks, orders, users, items, owner, meta, *refs):
    pieces = [refs[i * blocks : (i + 1) * blocks] for i in range(span)]
    start, tiles = refs[span * blocks], refs[span * blocks + 1]
    outs = refs[span * blocks + 2 : -5]
    slab, buf, sems, order, acc = refs[-5:]
    tile_size = tiles.shape[1]
    per_piece = refs[0].shape[1] // tile_size
    kc = start.shape[1]

    def add(place, both):
        acc[place] += both[:kc] + both[kc:]

    finish = run_tiles(
        span, span, per_piece, users, items, owner, meta, tiles, slab, add, buf, sems, order
    )
    acc[...] = start[...]
    fill(slab, pieces, per_piece)
    finish()
    width = tile_size // len(orders)
    for o, bits in enumerate(orders):
        cut = slice(o * width, (o + 1) * width)
        for k, place in enumerate(places(bits, 0)):
            outs[2 * o][k] = acc[place, :, cut]
        for k, place in enumerate(places(bits, 1)):
            outs[2 * o + 1][k] = acc[place, :, cut].astype(BF16)


def tile_call(kernel, scalars, pieces, extra, tiles, shapes, scratch, cost):
    users = scalars[0].shape[0]
    tile_size = tiles.shape[1]
    count = len(pieces) * pieces[0][0].shape[1] // tile_size
    depth = sum(block.shape[0] for block in pieces[0])
    pieces = [block for blocks in pieces for block in blocks]
    smem = pl.BlockSpec(memory_space=pltpu.SMEM)
    vmem = pl.BlockSpec(memory_space=pltpu.VMEM)
    slab = jax.ShapeDtypeStruct((count, depth, tile_size), BF16)
    buf = jax.ShapeDtypeStruct((SLOTS, tile_size, tile_size), BF16)
    held = sum(x.size * x.dtype.itemsize for x in (*pieces, *extra, *shapes, *scratch, slab, buf))
    return pl.pallas_call(
        kernel,
        out_shape=shapes,
        in_specs=[smem] * len(scalars)
        + [vmem] * (len(pieces) + len(extra))
        + [pl.BlockSpec(memory_space=pl.ANY)],
        out_specs=[vmem] * len(shapes),
        scratch_shapes=[
            pltpu.VMEM(slab.shape, BF16),
            pltpu.VMEM(buf.shape, BF16),
            pltpu.SemaphoreType.DMA((SLOTS,)),
            pltpu.SMEM((users,), jnp.int32),
        ]
        + [pltpu.VMEM(x.shape, x.dtype) for x in scratch],
        compiler_params=pltpu.CompilerParams(vmem_limit_bytes=held + SPARE),
        cost_estimate=pl.CostEstimate(flops=0, bytes_accessed=cost, transcendentals=0),
    )(*scalars, *pieces, *extra, tiles)


def near_sums(scalars, pieces, tiles, rows):
    tile_size = tiles.shape[1]
    shapes = [jax.ShapeDtypeStruct((rows, kc, tile_size), F32) for kc in CHUNKS]
    return tile_call(
        functools.partial(near_kernel, len(pieces), len(pieces[0])), scalars, pieces, [], tiles, shapes, [], NEAR_COST
    )


def far_sums(scalars, pieces, start, tiles, orders, cost):
    rows, kc, tile_size = start.shape
    width = tile_size // len(orders)
    shapes = []
    for _ in orders:
        shapes.append(jax.ShapeDtypeStruct((rows // 2, kc, width), F32))
        shapes.append(jax.ShapeDtypeStruct((rows // 2, kc, width), BF16))
    return tile_call(
        functools.partial(far_kernel, len(pieces), len(pieces[0]), orders),
        scalars,
        pieces,
        [start],
        tiles,
        shapes,
        [jax.ShapeDtypeStruct(start.shape, F32)],
        cost,
    )


def mm(a, b):
    return lax.dot_general(a, b, (((1,), (0,)), ((), ())), precision=HIGH, preferred_element_type=F32)


def mmt(a, b):
    return lax.dot_general(a, b, (((1,), (1,)), ((), ())), precision=HIGH, preferred_element_type=F32)


def factor_kernel(packed, inverse, good):
    n = packed.shape[1]
    r = lax.broadcasted_iota(jnp.int32, (n, n), 0)
    c = lax.broadcasted_iota(jnp.int32, (n, n), 1)
    mixed = packed[:n]
    flipped = mixed.T
    side = packed[n : 2 * n]
    tail = jnp.broadcast_to(packed[2 * n : 2 * n + 1], (n, n))
    first = jnp.where(r >= c, mixed, flipped)
    second = jnp.where(r < c, mixed, jnp.where(r > c, flipped, tail))
    gram = jnp.concatenate(
        [jnp.concatenate([first, side.T], axis=1), jnp.concatenate([side, second], axis=1)], axis=0
    )
    m = 2 * n
    rr = lax.broadcasted_iota(jnp.int32, (m, m), 0)
    cc = lax.broadcasted_iota(jnp.int32, (m, m), 1)
    on = rr == cc
    eye = jnp.where(on, 1.0, 0.0).astype(F32)
    low = jnp.where(rr > cc, 1.0, jnp.where(on, 0.5, 0.0)).astype(F32)
    diag = jnp.where(on, gram, 0.0)
    scale_row = lax.rsqrt(jnp.sum(diag, axis=0, keepdims=True))
    scale_col = lax.rsqrt(jnp.sum(diag, axis=1, keepdims=True))
    unit = gram * scale_row * scale_col
    off = unit - eye
    square = jnp.dot(off, off, preferred_element_type=F32)
    spread = jnp.max(jnp.sum(jnp.abs(jnp.dot(square, square, preferred_element_type=F32)), axis=1))
    w = eye - low * off
    for _ in range(NEWTON):
        err = mmt(mm(w, unit), w) - eye
        w = w - mm(low * err, w)
    last = jnp.max(jnp.sum(jnp.abs(err), axis=1))
    inflation = jnp.max(jnp.sum(w * w, axis=0))
    inverse[...] = w * scale_row
    good[0] = jnp.where((spread < 0.025) & (last < 0.01) & (inflation < 1.1), 1, 0)


def factor(packed):
    n = packed.shape[1]
    return pl.pallas_call(
        factor_kernel,
        out_shape=[jax.ShapeDtypeStruct((2 * n, 2 * n), F32), jax.ShapeDtypeStruct((1,), jnp.int32)],
        in_specs=[pl.BlockSpec(memory_space=pltpu.VMEM)],
        out_specs=[pl.BlockSpec(memory_space=pltpu.VMEM), pl.BlockSpec(memory_space=pltpu.SMEM)],
        compiler_params=pltpu.CompilerParams(vmem_limit_bytes=24 * 2**20),
        cost_estimate=pl.CostEstimate(
            flops=0, bytes_accessed=FACTOR_COST, transcendentals=0
        ),
    )(packed)


def last_kernel(inverse, early, keep0, keep1, came, out):
    left = keep0[0] + came[0].astype(F32)
    right = keep1[0] + came[1].astype(F32)
    total = jnp.concatenate([early[...], jnp.concatenate([left, right], axis=1)], axis=0)
    w = inverse[...]
    wh, th = w.astype(BF16), total.astype(BF16)
    wl = (w - wh.astype(F32)).astype(BF16)
    tl = (total - th.astype(F32)).astype(BF16)
    small = jnp.dot(wh, tl, preferred_element_type=F32) + jnp.dot(wl, th, preferred_element_type=F32)
    out[...] = jnp.dot(wh, th, preferred_element_type=F32) + small


def last(inverse, early, keeps, came):
    vmem = pl.BlockSpec(memory_space=pltpu.VMEM)
    return pl.pallas_call(
        last_kernel,
        out_shape=jax.ShapeDtypeStruct((inverse.shape[0], early.shape[1]), F32),
        in_specs=[vmem] * 5,
        out_specs=vmem,
        compiler_params=pltpu.CompilerParams(vmem_limit_bytes=16 * 2**20),
    )(inverse, early, *keeps, came)


def full_path(rows, cols, sketch, tiles, tile_user, tile_item, tile_count, item_owner, packed):
    n = packed.shape[1]
    r = lax.broadcasted_iota(jnp.int32, (n, n), 0)
    c = lax.broadcasted_iota(jnp.int32, (n, n), 1)
    mixed, side, tail = packed[:n], packed[n : 2 * n], packed[2 * n : 2 * n + 1]
    first = jnp.where(r >= c, mixed, mixed.T)
    second = jnp.where(r < c, mixed, jnp.where(r > c, mixed.T, tail))
    gram = jnp.block([[first, side.T], [side, second]])
    lower = jnp.linalg.cholesky(gram)
    basis = lax.linalg.triangular_solve(lower, sketch, left_side=False, lower=True, transpose_a=True).astype(BF16)
    have = {0: basis}
    for bit in bits_of(cols):
        for place in list(have):
            have[place | bit] = swap(have[place], "cols", cols, bit)
    slab = jnp.concatenate([have[i] for i in range(cols)], axis=0)
    col = lax.axis_index("cols")
    row = lax.axis_index("rows")
    per_piece = sketch.shape[0] // tiles.shape[2]
    owner = item_owner[0]
    tile_size = tiles.shape[2]

    def step(index, sums):
        user = tile_user[index]
        block = lax.bitwise_xor(user // per_piece, col) * per_piece + user % per_piece
        part_rows = lax.dynamic_slice_in_dim(slab, block * tile_size, tile_size, 0)
        part = lax.dot_general(part_rows, tiles[index], (((0,), (0,)), ((), ())), preferred_element_type=F32)
        place = lax.bitwise_xor(owner[tile_item[index]], row)
        now = lax.dynamic_index_in_dim(sums, place, 0, keepdims=False)
        return lax.dynamic_update_index_in_dim(sums, now + part, place, 0)

    totals = jnp.zeros((owner.shape[0], sketch.shape[1], tile_size), F32)
    totals = lax.fori_loop(0, tile_count[0], step, totals)
    for bit in bits_of(rows):
        totals = totals[:bit] + swap(totals[bit:], "rows", rows, bit)
    return totals[0]


def after(value, *others):
    return lax.optimization_barrier((value, *others))[0]


def exchange(lanes, rows):
    groups = []
    for bit in sorted({lane[2] for lane in lanes}):
        members = [i for i, lane in enumerate(lanes) if lane[2] == bit]
        sent = [lanes[i][1].reshape(-1, lanes[i][1].shape[2]) for i in members]
        groups.append((members, swap(jnp.concatenate(sent, axis=0), "rows", rows, 1 << bit)))
    return groups


def received(lanes, groups):
    got = [None] * len(lanes)
    for members, came in groups:
        first = 0
        for i in members:
            shape = lanes[i][1].shape
            size = shape[0] * shape[1]
            got[i] = came[first : first + size].reshape(shape)
            first += size
    return [lane[0] + g.astype(F32) for lane, g in zip(lanes, got)]


def split(total):
    half = total.shape[0] // 2
    return total[:half], total[half:].astype(BF16)


def body(rows, cols, sketch, tiles, tile_user, tile_item, tile_count, item_owner):
    row_bits = rows.bit_length() - 1
    first_order = tuple(range(row_bits))
    orders = (first_order, (1, 0) + first_order[2:])
    row = lax.axis_index("rows")
    col = lax.axis_index("cols")
    meta = jnp.stack([tile_count[0], row, col]).astype(jnp.int32)
    scalars = (tile_user, tile_item, item_owner[0], meta)
    far_bit, *near_bits = bits_of(cols)

    def spread(piece):
        have = {0: piece}
        for bit in near_bits:
            for place in list(have):
                have[place | bit] = swap(have[place], "cols", cols, bit)
        return [have[i] for i in range(cols // 2)]

    fence = lax.optimization_barrier
    far = far_bit
    flat, *chunks = split_sketch(sketch)
    near = list(zip(*[spread(c) for c in chunks]))
    crossed = [swap(c, "cols", cols, far) for c in chunks]
    packed = packed_gram(flat)
    for bit in near_bits:
        packed = packed + swap(packed, "cols", cols, bit)
    came = swap(packed, "rows", rows, 2)
    near[0] = (after(near[0][0], packed), *near[0][1:])
    sums = near_sums(scalars, near, tiles, rows)
    packed, came, *sums = fence((packed, came, *sums))
    packed = packed + came
    came = swap(packed, "rows", rows, 4)
    crossed[0] = after(crossed[0], packed)
    outs = far_sums(scalars, [[p] for p in spread(crossed[0])], sums[0], tiles, orders, EARLY_COST)
    packed, came, *outs = fence((packed, came, *outs))
    packed = packed + came
    came = swap(packed, "cols", cols, far)
    lanes = [(outs[2 * o], outs[2 * o + 1], order[0]) for o, order in enumerate(orders)]
    groups = exchange(lanes, rows)
    crossed[1] = after(crossed[1], packed)
    later = far_sums(scalars, [[p] for p in spread(crossed[1])], sums[1], tiles, orders, LATE_COST)
    flying = [g[1] for g in groups]
    packed, came, *rest = fence((packed, came, *flying, *later))
    groups = [(g[0], x) for g, x in zip(groups, rest)]
    later = rest[len(groups) :]
    packed = packed + came
    stages = [1] + [1 << b for b in range(3, row_bits)]

    totals = received(lanes, groups)
    late = [(later[2 * o], later[2 * o + 1]) for o in range(len(orders))]
    for step in range(1, row_bits + 1):
        lanes = []
        if step < row_bits:
            lanes += [(*split(t), order[step]) for t, order in zip(totals, orders)]
        lanes += [(*pair, order[step - 1]) for pair, order in zip(late, orders)]
        groups = exchange(lanes, rows)
        flying = [g[1] for g in groups]
        sends = [lane[1] for lane in lanes]
        if step > 1 and step <= len(stages) + 1:
            packed = packed + after(came, *sends)
        if step <= len(stages):
            came = swap(packed, "rows", rows, stages[step - 1])
        if step == len(stages) + 1:
            inverse, good = factor(after(packed, *sends))
            free = [i for i, g in enumerate(groups) if max(g[0]) < len(lanes) - len(orders)]
            inverse, *tied = fence((inverse, *[flying[i] for i in free]))
            for i, x in zip(free, tied):
                flying[i] = x
        groups = [(g[0], x) for g, x in zip(groups, flying)]
        if step < row_bits:
            new = received(lanes, groups)
            totals, new = new[: len(orders)], new[len(orders) :]
            late = [split(t) for t in new]
        if step == row_bits - 1:
            early = jnp.concatenate([t[0] for t in totals], axis=1)
    keeps = [lane[0] for lane in lanes]
    came = groups[0][1].reshape(len(lanes), *lanes[0][1].shape[1:])
    out = lax.cond(
        good[0] > 0,
        lambda: last(inverse, early, keeps, came),
        lambda: full_path(rows, cols, flat.T, tiles, tile_user, tile_item, tile_count, item_owner, packed),
    )
    return out[None, None]


def solution(mesh):
    placed = (
        P(("rows", "cols"), None),
        P(("rows", "cols"), None, None),
        P(("rows", "cols")),
        P(("rows", "cols")),
        P(("rows", "cols")),
        P("cols", None),
    )
    return jax.shard_map(
        functools.partial(body, mesh.shape["rows"], mesh.shape["cols"]),
        mesh=mesh,
        in_specs=placed,
        out_specs=P("rows", "cols", None, None),
        check_vma=False,
    )
```

```python
import functools

import jax
import jax.numpy as jnp
from jax import lax
from jax.experimental import pallas as pl
from jax.experimental.pallas import tpu as pltpu
from jax.sharding import PartitionSpec as P

F32 = jnp.float32
BF16 = jnp.bfloat16
HIGH = lax.Precision.HIGHEST
SLOTS = 12
SPARE = 4 * 2**20
GROUP = 4
NEAR_COST = 200 * 2**20
EARLY_COST = 1024
LATE_COST = 1024
FACTOR_COST = 200 * 2**20
CHUNKS = (176, 80)
NEWTON = 2


def bits_of(count):
    return [1 << b for b in reversed(range(count.bit_length() - 1))]


def swap(x, axis, count, bit):
    return lax.ppermute(x, axis, [(i, i ^ bit) for i in range(count)])


def places(order, parity):
    found = [parity << order[0]]
    for bit in reversed(order[1:]):
        found = found + [p | (1 << bit) for p in found]
    return found


def run_tiles(base, span, per_piece, users, items, owner, meta, tiles, slab, add, buf, sems, order):
    count, row, col = meta[0], meta[1], meta[2]

    def relative(t):
        user = users[t]
        return lax.bitwise_xor(user // per_piece, col) - base, lax.rem(user, per_piece)

    def choose(t, n):
        piece, _ = relative(t)
        order[n] = t
        return n + jnp.where((piece >= 0) & (piece < span), 1, 0)

    live = lax.fori_loop(0, count, choose, 0)

    def fetch(i):
        slot = lax.rem(i, SLOTS)
        return pltpu.make_async_copy(tiles.at[order[i]], buf.at[slot], sems.at[slot])

    for i in range(SLOTS):
        @pl.when(i < live)
        def _():
            fetch(i).start()

    def group(first, size):
        for q in range(size):
            fetch(first + q).wait()
        found = []
        for q in range(size):
            piece, part = relative(order[first + q])
            both = jnp.dot(
                slab[piece * per_piece + part],
                buf[lax.rem(first + q, SLOTS)],
                preferred_element_type=F32,
            )
            found.append(both)
        for q in range(size):
            add(lax.bitwise_xor(owner[items[order[first + q]]], row), found[q])
        for q in range(size):
            @pl.when(first + q + SLOTS < live)
            def _():
                fetch(first + q + SLOTS).start()

    def finish():
        groups = live // GROUP

        def many(g, _):
            group(g * GROUP, GROUP)
            return 0

        def one(i, _):
            group(i, 1)
            return 0

        lax.fori_loop(0, groups, many, 0)
        lax.fori_loop(groups * GROUP, live, one, 0)

    return finish


def split_kernel(sketch, flat, *chunks):
    flat[...] = sketch[...].T
    first = 0
    for chunk in chunks:
        kc = chunk.shape[0] // 2
        rows = flat[first : first + kc, :]
        high = rows.astype(BF16)
        chunk[:kc, :] = high
        chunk[kc:, :] = (rows - high.astype(F32)).astype(BF16)
        first += kc


def split_sketch(sketch):
    users, width = sketch.shape
    vmem = pl.BlockSpec(memory_space=pltpu.VMEM)
    return pl.pallas_call(
        split_kernel,
        out_shape=[jax.ShapeDtypeStruct((width, users), F32)]
        + [jax.ShapeDtypeStruct((2 * k, users), BF16) for k in CHUNKS],
        in_specs=[vmem],
        out_specs=[vmem] * (1 + len(CHUNKS)),
        compiler_params=pltpu.CompilerParams(vmem_limit_bytes=16 * 2**20),
    )(sketch)


def gram_kernel(flat, packed):
    n = packed.shape[1]
    top, low = flat[:n, :], flat[n:, :]
    second = mmt(low, low)
    r = lax.broadcasted_iota(jnp.int32, (n, n), 0)
    c = lax.broadcasted_iota(jnp.int32, (n, n), 1)
    packed[:n] = jnp.where(r >= c, mmt(top, top), second)
    packed[n : 2 * n] = mmt(low, top)
    tail = jnp.sum(jnp.where(r == c, second, 0.0), axis=0, keepdims=True)
    packed[2 * n :] = jnp.broadcast_to(tail, (8, n))


def packed_gram(flat):
    n = flat.shape[0] // 2
    vmem = pl.BlockSpec(memory_space=pltpu.VMEM)
    return pl.pallas_call(
        gram_kernel,
        out_shape=jax.ShapeDtypeStruct((2 * n + 8, n), F32),
        in_specs=[vmem],
        out_specs=vmem,
        compiler_params=pltpu.CompilerParams(vmem_limit_bytes=16 * 2**20),
    )(flat)


def fill(slab, pieces, per_piece):
    tile_size = slab.shape[2]
    for c, blocks in enumerate(pieces):
        first = 0
        for block in blocks:
            stop = first + block.shape[0]
            for h in range(per_piece):
                slab[c * per_piece + h, first:stop, :] = block[:, h * tile_size : (h + 1) * tile_size]
            first = stop


def near_kernel(span, blocks, users, items, owner, meta, *refs):
    pieces = [refs[i * blocks : (i + 1) * blocks] for i in range(span)]
    tiles = refs[span * blocks]
    sums = refs[span * blocks + 1 : -4]
    slab, buf, sems, order = refs[-4:]
    per_piece = refs[0].shape[1] // tiles.shape[1]

    def add(place, both):
        first = 0
        for part in sums:
            kc = part.shape[1]
            part[place] += both[first : first + kc] + both[first + kc : first + 2 * kc]
            first += 2 * kc

    finish = run_tiles(
        0, span, per_piece, users, items, owner, meta, tiles, slab, add, buf, sems, order
    )
    for part in sums:
        part[...] = jnp.zeros_like(part)
    fill(slab, pieces, per_piece)
    finish()


def far_kernel(span, blocks, orders, users, items, owner, meta, *refs):
    pieces = [refs[i * blocks : (i + 1) * blocks] for i in range(span)]
    start, tiles = refs[span * blocks], refs[span * blocks + 1]
    outs = refs[span * blocks + 2 : -5]
    slab, buf, sems, order, acc = refs[-5:]
    tile_size = tiles.shape[1]
    per_piece = refs[0].shape[1] // tile_size
    kc = start.shape[1]

    def add(place, both):
        acc[place] += both[:kc] + both[kc:]

    finish = run_tiles(
        span, span, per_piece, users, items, owner, meta, tiles, slab, add, buf, sems, order
    )
    acc[...] = start[...]
    fill(slab, pieces, per_piece)
    finish()
    width = tile_size // len(orders)
    for o, bits in enumerate(orders):
        cut = slice(o * width, (o + 1) * width)
        for k, place in enumerate(places(bits, 0)):
            outs[2 * o][k] = acc[place, :, cut]
        for k, place in enumerate(places(bits, 1)):
            outs[2 * o + 1][k] = acc[place, :, cut].astype(BF16)


def tile_call(kernel, scalars, pieces, extra, tiles, shapes, scratch, cost):
    users = scalars[0].shape[0]
    tile_size = tiles.shape[1]
    count = len(pieces) * pieces[0][0].shape[1] // tile_size
    depth = sum(block.shape[0] for block in pieces[0])
    pieces = [block for blocks in pieces for block in blocks]
    smem = pl.BlockSpec(memory_space=pltpu.SMEM)
    vmem = pl.BlockSpec(memory_space=pltpu.VMEM)
    slab = jax.ShapeDtypeStruct((count, depth, tile_size), BF16)
    buf = jax.ShapeDtypeStruct((SLOTS, tile_size, tile_size), BF16)
    held = sum(x.size * x.dtype.itemsize for x in (*pieces, *extra, *shapes, *scratch, slab, buf))
    return pl.pallas_call(
        kernel,
        out_shape=shapes,
        in_specs=[smem] * len(scalars)
        + [vmem] * (len(pieces) + len(extra))
        + [pl.BlockSpec(memory_space=pl.ANY)],
        out_specs=[vmem] * len(shapes),
        scratch_shapes=[
            pltpu.VMEM(slab.shape, BF16),
            pltpu.VMEM(buf.shape, BF16),
            pltpu.SemaphoreType.DMA((SLOTS,)),
            pltpu.SMEM((users,), jnp.int32),
        ]
        + [pltpu.VMEM(x.shape, x.dtype) for x in scratch],
        compiler_params=pltpu.CompilerParams(vmem_limit_bytes=held + SPARE),
        cost_estimate=pl.CostEstimate(flops=0, bytes_accessed=cost, transcendentals=0),
    )(*scalars, *pieces, *extra, tiles)


def near_sums(scalars, pieces, tiles, rows):
    tile_size = tiles.shape[1]
    shapes = [jax.ShapeDtypeStruct((rows, kc, tile_size), F32) for kc in CHUNKS]
    return tile_call(
        functools.partial(near_kernel, len(pieces), len(pieces[0])), scalars, pieces, [], tiles, shapes, [], NEAR_COST
    )


def far_sums(scalars, pieces, start, tiles, orders, cost):
    rows, kc, tile_size = start.shape
    width = tile_size // len(orders)
    shapes = []
    for _ in orders:
        shapes.append(jax.ShapeDtypeStruct((rows // 2, kc, width), F32))
        shapes.append(jax.ShapeDtypeStruct((rows // 2, kc, width), BF16))
    return tile_call(
        functools.partial(far_kernel, len(pieces), len(pieces[0]), orders),
        scalars,
        pieces,
        [start],
        tiles,
        shapes,
        [jax.ShapeDtypeStruct(start.shape, F32)],
        cost,
    )


def mm(a, b):
    return lax.dot_general(a, b, (((1,), (0,)), ((), ())), precision=HIGH, preferred_element_type=F32)


def mmt(a, b):
    return lax.dot_general(a, b, (((1,), (1,)), ((), ())), precision=HIGH, preferred_element_type=F32)


def factor_kernel(packed, inverse, good):
    n = packed.shape[1]
    r = lax.broadcasted_iota(jnp.int32, (n, n), 0)
    c = lax.broadcasted_iota(jnp.int32, (n, n), 1)
    mixed = packed[:n]
    flipped = mixed.T
    side = packed[n : 2 * n]
    tail = jnp.broadcast_to(packed[2 * n : 2 * n + 1], (n, n))
    first = jnp.where(r >= c, mixed, flipped)
    second = jnp.where(r < c, mixed, jnp.where(r > c, flipped, tail))
    gram = jnp.concatenate(
        [jnp.concatenate([first, side.T], axis=1), jnp.concatenate([side, second], axis=1)], axis=0
    )
    m = 2 * n
    rr = lax.broadcasted_iota(jnp.int32, (m, m), 0)
    cc = lax.broadcasted_iota(jnp.int32, (m, m), 1)
    on = rr == cc
    eye = jnp.where(on, 1.0, 0.0).astype(F32)
    low = jnp.where(rr > cc, 1.0, jnp.where(on, 0.5, 0.0)).astype(F32)
    diag = jnp.where(on, gram, 0.0)
    scale_row = lax.rsqrt(jnp.sum(diag, axis=0, keepdims=True))
    scale_col = lax.rsqrt(jnp.sum(diag, axis=1, keepdims=True))
    unit = gram * scale_row * scale_col
    off = unit - eye
    square = jnp.dot(off, off, preferred_element_type=F32)
    spread = jnp.max(jnp.sum(jnp.abs(jnp.dot(square, square, preferred_element_type=F32)), axis=1))
    w = eye - low * off
    for _ in range(NEWTON):
        err = mmt(mm(w, unit), w) - eye
        w = w - mm(low * err, w)
    last = jnp.max(jnp.sum(jnp.abs(err), axis=1))
    inflation = jnp.max(jnp.sum(w * w, axis=0))
    inverse[...] = w * scale_row
    good[0] = jnp.where((spread < 0.025) & (last < 0.01) & (inflation < 1.1), 1, 0)


def factor(packed):
    n = packed.shape[1]
    return pl.pallas_call(
        factor_kernel,
        out_shape=[jax.ShapeDtypeStruct((2 * n, 2 * n), F32), jax.ShapeDtypeStruct((1,), jnp.int32)],
        in_specs=[pl.BlockSpec(memory_space=pltpu.VMEM)],
        out_specs=[pl.BlockSpec(memory_space=pltpu.VMEM), pl.BlockSpec(memory_space=pltpu.SMEM)],
        compiler_params=pltpu.CompilerParams(vmem_limit_bytes=24 * 2**20),
        cost_estimate=pl.CostEstimate(
            flops=0, bytes_accessed=FACTOR_COST, transcendentals=0
        ),
    )(packed)


def last_kernel(inverse, early, keep0, keep1, came, out):
    left = keep0[0] + came[0].astype(F32)
    right = keep1[0] + came[1].astype(F32)
    total = jnp.concatenate([early[...], jnp.concatenate([left, right], axis=1)], axis=0)
    w = inverse[...]
    wh, th = w.astype(BF16), total.astype(BF16)
    wl = (w - wh.astype(F32)).astype(BF16)
    tl = (total - th.astype(F32)).astype(BF16)
    small = jnp.dot(wh, tl, preferred_element_type=F32) + jnp.dot(wl, th, preferred_element_type=F32)
    out[...] = jnp.dot(wh, th, preferred_element_type=F32) + small


def last(inverse, early, keeps, came):
    vmem = pl.BlockSpec(memory_space=pltpu.VMEM)
    return pl.pallas_call(
        last_kernel,
        out_shape=jax.ShapeDtypeStruct((inverse.shape[0], early.shape[1]), F32),
        in_specs=[vmem] * 5,
        out_specs=vmem,
        compiler_params=pltpu.CompilerParams(vmem_limit_bytes=16 * 2**20),
    )(inverse, early, *keeps, came)


def full_path(rows, cols, sketch, tiles, tile_user, tile_item, tile_count, item_owner, packed):
    n = packed.shape[1]
    r = lax.broadcasted_iota(jnp.int32, (n, n), 0)
    c = lax.broadcasted_iota(jnp.int32, (n, n), 1)
    mixed, side, tail = packed[:n], packed[n : 2 * n], packed[2 * n : 2 * n + 1]
    first = jnp.where(r >= c, mixed, mixed.T)
    second = jnp.where(r < c, mixed, jnp.where(r > c, mixed.T, tail))
    gram = jnp.block([[first, side.T], [side, second]])
    lower = jnp.linalg.cholesky(gram)
    basis = lax.linalg.triangular_solve(lower, sketch, left_side=False, lower=True, transpose_a=True).astype(BF16)
    have = {0: basis}
    for bit in bits_of(cols):
        for place in list(have):
            have[place | bit] = swap(have[place], "cols", cols, bit)
    slab = jnp.concatenate([have[i] for i in range(cols)], axis=0)
    col = lax.axis_index("cols")
    row = lax.axis_index("rows")
    per_piece = sketch.shape[0] // tiles.shape[2]
    owner = item_owner[0]
    tile_size = tiles.shape[2]

    def step(index, sums):
        user = tile_user[index]
        block = lax.bitwise_xor(user // per_piece, col) * per_piece + user % per_piece
        part_rows = lax.dynamic_slice_in_dim(slab, block * tile_size, tile_size, 0)
        part = lax.dot_general(part_rows, tiles[index], (((0,), (0,)), ((), ())), preferred_element_type=F32)
        place = lax.bitwise_xor(owner[tile_item[index]], row)
        now = lax.dynamic_index_in_dim(sums, place, 0, keepdims=False)
        return lax.dynamic_update_index_in_dim(sums, now + part, place, 0)

    totals = jnp.zeros((owner.shape[0], sketch.shape[1], tile_size), F32)
    totals = lax.fori_loop(0, tile_count[0], step, totals)
    for bit in bits_of(rows):
        totals = totals[:bit] + swap(totals[bit:], "rows", rows, bit)
    return totals[0]


def after(value, *others):
    return lax.optimization_barrier((value, *others))[0]


def exchange(lanes, rows):
    groups = []
    for bit in sorted({lane[2] for lane in lanes}):
        members = [i for i, lane in enumerate(lanes) if lane[2] == bit]
        sent = [lanes[i][1].reshape(-1, lanes[i][1].shape[2]) for i in members]
        groups.append((members, swap(jnp.concatenate(sent, axis=0), "rows", rows, 1 << bit)))
    return groups


def received(lanes, groups):
    got = [None] * len(lanes)
    for members, came in groups:
        first = 0
        for i in members:
            shape = lanes[i][1].shape
            size = shape[0] * shape[1]
            got[i] = came[first : first + size].reshape(shape)
            first += size
    return [lane[0] + g.astype(F32) for lane, g in zip(lanes, got)]


def split(total):
    half = total.shape[0] // 2
    return total[:half], total[half:].astype(BF16)


def body(rows, cols, sketch, tiles, tile_user, tile_item, tile_count, item_owner):
    row_bits = rows.bit_length() - 1
    first_order = tuple(range(row_bits))
    orders = (first_order, (1, 0) + first_order[2:])
    row = lax.axis_index("rows")
    col = lax.axis_index("cols")
    meta = jnp.stack([tile_count[0], row, col]).astype(jnp.int32)
    scalars = (tile_user, tile_item, item_owner[0], meta)
    far_bit, *near_bits = bits_of(cols)

    def spread(piece):
        have = {0: piece}
        for bit in near_bits:
            for place in list(have):
                have[place | bit] = swap(have[place], "cols", cols, bit)
        return [have[i] for i in range(cols // 2)]

    fence = lax.optimization_barrier
    far = far_bit
    flat, *chunks = split_sketch(sketch)
    near = list(zip(*[spread(c) for c in chunks]))
    crossed = [swap(c, "cols", cols, far) for c in chunks]
    packed = packed_gram(flat)
    for bit in near_bits:
        packed = packed + swap(packed, "cols", cols, bit)
    came = swap(packed, "rows", rows, 2)
    near[0] = (after(near[0][0], packed), *near[0][1:])
    sums = near_sums(scalars, near, tiles, rows)
    packed, came, *sums = fence((packed, came, *sums))
    packed = packed + came
    came = swap(packed, "rows", rows, 4)
    crossed[0] = after(crossed[0], packed)
    outs = far_sums(scalars, [[p] for p in spread(crossed[0])], sums[0], tiles, orders, EARLY_COST)
    packed, came, *outs = fence((packed, came, *outs))
    packed = packed + came
    came = swap(packed, "cols", cols, far)
    lanes = [(outs[2 * o], outs[2 * o + 1], order[0]) for o, order in enumerate(orders)]
    groups = exchange(lanes, rows)
    crossed[1] = after(crossed[1], packed)
    later = far_sums(scalars, [[p] for p in spread(crossed[1])], sums[1], tiles, orders, LATE_COST)
    flying = [g[1] for g in groups]
    packed, came, *rest = fence((packed, came, *flying, *later))
    groups = [(g[0], x) for g, x in zip(groups, rest)]
    later = rest[len(groups) :]
    packed = packed + came
    stages = [1] + [1 << b for b in range(3, row_bits)]

    totals = received(lanes, groups)
    late = [(later[2 * o], later[2 * o + 1]) for o in range(len(orders))]
    for step in range(1, row_bits + 1):
        lanes = []
        if step < row_bits:
            lanes += [(*split(t), order[step]) for t, order in zip(totals, orders)]
        lanes += [(*pair, order[step - 1]) for pair, order in zip(late, orders)]
        groups = exchange(lanes, rows)
        flying = [g[1] for g in groups]
        sends = [lane[1] for lane in lanes]
        if step > 1 and step <= len(stages) + 1:
            packed = packed + after(came, *sends)
        if step <= len(stages):
            came = swap(packed, "rows", rows, stages[step - 1])
        if step == len(stages) + 1:
            inverse, good = factor(after(packed, *sends))
            free = [i for i, g in enumerate(groups) if max(g[0]) < len(lanes) - len(orders)]
            inverse, *tied = fence((inverse, *[flying[i] for i in free]))
            for i, x in zip(free, tied):
                flying[i] = x
        groups = [(g[0], x) for g, x in zip(groups, flying)]
        if step < row_bits:
            new = received(lanes, groups)
            totals, new = new[: len(orders)], new[len(orders) :]
            late = [split(t) for t in new]
        if step == row_bits - 1:
            early = jnp.concatenate([t[0] for t in totals], axis=1)
    keeps = [lane[0] for lane in lanes]
    came = groups[0][1].reshape(len(lanes), *lanes[0][1].shape[1:])
    out = lax.cond(
        good[0] > 0,
        lambda: last(inverse, early, keeps, came),
        lambda: full_path(rows, cols, flat.T, tiles, tile_user, tile_item, tile_count, item_owner, packed),
    )
    return out[None, None]


def solution(mesh):
    placed = (
        P(("rows", "cols"), None),
        P(("rows", "cols"), None, None),
        P(("rows", "cols")),
        P(("rows", "cols")),
        P(("rows", "cols")),
        P("cols", None),
    )
    return jax.shard_map(
        functools.partial(body, mesh.shape["rows"], mesh.shape["cols"]),
        mesh=mesh,
        in_specs=placed,
        out_specs=P("rows", "cols", None, None),
        check_vma=False,
    )
```

```python
import functools

import jax
import jax.numpy as jnp
from jax import lax
from jax.experimental import pallas as pl
from jax.experimental.pallas import tpu as pltpu
from jax.sharding import PartitionSpec as P

F32 = jnp.float32
BF16 = jnp.bfloat16
HIGH = lax.Precision.HIGHEST
SLOTS = 12
SPARE = 4 * 2**20
GROUP = 4
NEAR_COST = 200 * 2**20
EARLY_COST = 1024
LATE_COST = 1024
FACTOR_COST = 200 * 2**20
CHUNKS = (192, 64)
NEWTON = 2


def bits_of(count):
    return [1 << b for b in reversed(range(count.bit_length() - 1))]


def swap(x, axis, count, bit):
    return lax.ppermute(x, axis, [(i, i ^ bit) for i in range(count)])


def places(order, parity):
    found = [parity << order[0]]
    for bit in reversed(order[1:]):
        found = found + [p | (1 << bit) for p in found]
    return found


def run_tiles(base, span, per_piece, users, items, owner, meta, tiles, slab, add, buf, sems, order):
    count, row, col = meta[0], meta[1], meta[2]

    def relative(t):
        user = users[t]
        return lax.bitwise_xor(user // per_piece, col) - base, lax.rem(user, per_piece)

    def choose(t, n):
        piece, _ = relative(t)
        order[n] = t
        return n + jnp.where((piece >= 0) & (piece < span), 1, 0)

    live = lax.fori_loop(0, count, choose, 0)

    def fetch(i):
        slot = lax.rem(i, SLOTS)
        return pltpu.make_async_copy(tiles.at[order[i]], buf.at[slot], sems.at[slot])

    for i in range(SLOTS):
        @pl.when(i < live)
        def _():
            fetch(i).start()

    def group(first, size):
        for q in range(size):
            fetch(first + q).wait()
        found = []
        for q in range(size):
            piece, part = relative(order[first + q])
            both = jnp.dot(
                slab[piece * per_piece + part],
                buf[lax.rem(first + q, SLOTS)],
                preferred_element_type=F32,
            )
            found.append(both)
        for q in range(size):
            add(lax.bitwise_xor(owner[items[order[first + q]]], row), found[q])
        for q in range(size):
            @pl.when(first + q + SLOTS < live)
            def _():
                fetch(first + q + SLOTS).start()

    def finish():
        groups = live // GROUP

        def many(g, _):
            group(g * GROUP, GROUP)
            return 0

        def one(i, _):
            group(i, 1)
            return 0

        lax.fori_loop(0, groups, many, 0)
        lax.fori_loop(groups * GROUP, live, one, 0)

    return finish


def split_kernel(sketch, flat, *chunks):
    flat[...] = sketch[...].T
    first = 0
    for chunk in chunks:
        kc = chunk.shape[0] // 2
        rows = flat[first : first + kc, :]
        high = rows.astype(BF16)
        chunk[:kc, :] = high
        chunk[kc:, :] = (rows - high.astype(F32)).astype(BF16)
        first += kc


def split_sketch(sketch):
    users, width = sketch.shape
    vmem = pl.BlockSpec(memory_space=pltpu.VMEM)
    return pl.pallas_call(
        split_kernel,
        out_shape=[jax.ShapeDtypeStruct((width, users), F32)]
        + [jax.ShapeDtypeStruct((2 * k, users), BF16) for k in CHUNKS],
        in_specs=[vmem],
        out_specs=[vmem] * (1 + len(CHUNKS)),
        compiler_params=pltpu.CompilerParams(vmem_limit_bytes=16 * 2**20),
    )(sketch)


def gram_kernel(flat, packed):
    n = packed.shape[1]
    top, low = flat[:n, :], flat[n:, :]
    second = mmt(low, low)
    r = lax.broadcasted_iota(jnp.int32, (n, n), 0)
    c = lax.broadcasted_iota(jnp.int32, (n, n), 1)
    packed[:n] = jnp.where(r >= c, mmt(top, top), second)
    packed[n : 2 * n] = mmt(low, top)
    tail = jnp.sum(jnp.where(r == c, second, 0.0), axis=0, keepdims=True)
    packed[2 * n :] = jnp.broadcast_to(tail, (8, n))


def packed_gram(flat):
    n = flat.shape[0] // 2
    vmem = pl.BlockSpec(memory_space=pltpu.VMEM)
    return pl.pallas_call(
        gram_kernel,
        out_shape=jax.ShapeDtypeStruct((2 * n + 8, n), F32),
        in_specs=[vmem],
        out_specs=vmem,
        compiler_params=pltpu.CompilerParams(vmem_limit_bytes=16 * 2**20),
    )(flat)


def fill(slab, pieces, per_piece):
    tile_size = slab.shape[2]
    for c, blocks in enumerate(pieces):
        first = 0
        for block in blocks:
            stop = first + block.shape[0]
            for h in range(per_piece):
                slab[c * per_piece + h, first:stop, :] = block[:, h * tile_size : (h + 1) * tile_size]
            first = stop


def near_kernel(span, blocks, users, items, owner, meta, *refs):
    pieces = [refs[i * blocks : (i + 1) * blocks] for i in range(span)]
    tiles = refs[span * blocks]
    sums = refs[span * blocks + 1 : -4]
    slab, buf, sems, order = refs[-4:]
    per_piece = refs[0].shape[1] // tiles.shape[1]

    def add(place, both):
        first = 0
        for part in sums:
            kc = part.shape[1]
            part[place] += both[first : first + kc] + both[first + kc : first + 2 * kc]
            first += 2 * kc

    finish = run_tiles(
        0, span, per_piece, users, items, owner, meta, tiles, slab, add, buf, sems, order
    )
    for part in sums:
        part[...] = jnp.zeros_like(part)
    fill(slab, pieces, per_piece)
    finish()


def far_kernel(span, blocks, orders, users, items, owner, meta, *refs):
    pieces = [refs[i * blocks : (i + 1) * blocks] for i in range(span)]
    start, tiles = refs[span * blocks], refs[span * blocks + 1]
    outs = refs[span * blocks + 2 : -5]
    slab, buf, sems, order, acc = refs[-5:]
    tile_size = tiles.shape[1]
    per_piece = refs[0].shape[1] // tile_size
    kc = start.shape[1]

    def add(place, both):
        acc[place] += both[:kc] + both[kc:]

    finish = run_tiles(
        span, span, per_piece, users, items, owner, meta, tiles, slab, add, buf, sems, order
    )
    acc[...] = start[...]
    fill(slab, pieces, per_piece)
    finish()
    width = tile_size // len(orders)
    for o, bits in enumerate(orders):
        cut = slice(o * width, (o + 1) * width)
        for k, place in enumerate(places(bits, 0)):
            outs[2 * o][k] = acc[place, :, cut]
        for k, place in enumerate(places(bits, 1)):
            outs[2 * o + 1][k] = acc[place, :, cut].astype(BF16)


def tile_call(kernel, scalars, pieces, extra, tiles, shapes, scratch, cost):
    users = scalars[0].shape[0]
    tile_size = tiles.shape[1]
    count = len(pieces) * pieces[0][0].shape[1] // tile_size
    depth = sum(block.shape[0] for block in pieces[0])
    pieces = [block for blocks in pieces for block in blocks]
    smem = pl.BlockSpec(memory_space=pltpu.SMEM)
    vmem = pl.BlockSpec(memory_space=pltpu.VMEM)
    slab = jax.ShapeDtypeStruct((count, depth, tile_size), BF16)
    buf = jax.ShapeDtypeStruct((SLOTS, tile_size, tile_size), BF16)
    held = sum(x.size * x.dtype.itemsize for x in (*pieces, *extra, *shapes, *scratch, slab, buf))
    return pl.pallas_call(
        kernel,
        out_shape=shapes,
        in_specs=[smem] * len(scalars)
        + [vmem] * (len(pieces) + len(extra))
        + [pl.BlockSpec(memory_space=pl.ANY)],
        out_specs=[vmem] * len(shapes),
        scratch_shapes=[
            pltpu.VMEM(slab.shape, BF16),
            pltpu.VMEM(buf.shape, BF16),
            pltpu.SemaphoreType.DMA((SLOTS,)),
            pltpu.SMEM((users,), jnp.int32),
        ]
        + [pltpu.VMEM(x.shape, x.dtype) for x in scratch],
        compiler_params=pltpu.CompilerParams(vmem_limit_bytes=held + SPARE),
        cost_estimate=pl.CostEstimate(flops=0, bytes_accessed=cost, transcendentals=0),
    )(*scalars, *pieces, *extra, tiles)


def near_sums(scalars, pieces, tiles, rows):
    tile_size = tiles.shape[1]
    shapes = [jax.ShapeDtypeStruct((rows, kc, tile_size), F32) for kc in CHUNKS]
    return tile_call(
        functools.partial(near_kernel, len(pieces), len(pieces[0])), scalars, pieces, [], tiles, shapes, [], NEAR_COST
    )


def far_sums(scalars, pieces, start, tiles, orders, cost):
    rows, kc, tile_size = start.shape
    width = tile_size // len(orders)
    shapes = []
    for _ in orders:
        shapes.append(jax.ShapeDtypeStruct((rows // 2, kc, width), F32))
        shapes.append(jax.ShapeDtypeStruct((rows // 2, kc, width), BF16))
    return tile_call(
        functools.partial(far_kernel, len(pieces), len(pieces[0]), orders),
        scalars,
        pieces,
        [start],
        tiles,
        shapes,
        [jax.ShapeDtypeStruct(start.shape, F32)],
        cost,
    )


def mm(a, b):
    return lax.dot_general(a, b, (((1,), (0,)), ((), ())), precision=HIGH, preferred_element_type=F32)


def mmt(a, b):
    return lax.dot_general(a, b, (((1,), (1,)), ((), ())), precision=HIGH, preferred_element_type=F32)


def factor_kernel(packed, inverse, good):
    n = packed.shape[1]
    r = lax.broadcasted_iota(jnp.int32, (n, n), 0)
    c = lax.broadcasted_iota(jnp.int32, (n, n), 1)
    mixed = packed[:n]
    flipped = mixed.T
    side = packed[n : 2 * n]
    tail = jnp.broadcast_to(packed[2 * n : 2 * n + 1], (n, n))
    first = jnp.where(r >= c, mixed, flipped)
    second = jnp.where(r < c, mixed, jnp.where(r > c, flipped, tail))
    gram = jnp.concatenate(
        [jnp.concatenate([first, side.T], axis=1), jnp.concatenate([side, second], axis=1)], axis=0
    )
    m = 2 * n
    rr = lax.broadcasted_iota(jnp.int32, (m, m), 0)
    cc = lax.broadcasted_iota(jnp.int32, (m, m), 1)
    on = rr == cc
    eye = jnp.where(on, 1.0, 0.0).astype(F32)
    low = jnp.where(rr > cc, 1.0, jnp.where(on, 0.5, 0.0)).astype(F32)
    diag = jnp.where(on, gram, 0.0)
    scale_row = lax.rsqrt(jnp.sum(diag, axis=0, keepdims=True))
    scale_col = lax.rsqrt(jnp.sum(diag, axis=1, keepdims=True))
    unit = gram * scale_row * scale_col
    off = unit - eye
    square = jnp.dot(off, off, preferred_element_type=F32)
    spread = jnp.max(jnp.sum(jnp.abs(jnp.dot(square, square, preferred_element_type=F32)), axis=1))
    w = eye - low * off
    for _ in range(NEWTON):
        err = mmt(mm(w, unit), w) - eye
        w = w - mm(low * err, w)
    last = jnp.max(jnp.sum(jnp.abs(err), axis=1))
    inflation = jnp.max(jnp.sum(w * w, axis=0))
    inverse[...] = w * scale_row
    good[0] = jnp.where((spread < 0.025) & (last < 0.01) & (inflation < 1.1), 1, 0)


def factor(packed):
    n = packed.shape[1]
    return pl.pallas_call(
        factor_kernel,
        out_shape=[jax.ShapeDtypeStruct((2 * n, 2 * n), F32), jax.ShapeDtypeStruct((1,), jnp.int32)],
        in_specs=[pl.BlockSpec(memory_space=pltpu.VMEM)],
        out_specs=[pl.BlockSpec(memory_space=pltpu.VMEM), pl.BlockSpec(memory_space=pltpu.SMEM)],
        compiler_params=pltpu.CompilerParams(vmem_limit_bytes=24 * 2**20),
        cost_estimate=pl.CostEstimate(
            flops=0, bytes_accessed=FACTOR_COST, transcendentals=0
        ),
    )(packed)


def last_kernel(inverse, early, keep0, keep1, came, out):
    left = keep0[0] + came[0].astype(F32)
    right = keep1[0] + came[1].astype(F32)
    total = jnp.concatenate([early[...], jnp.concatenate([left, right], axis=1)], axis=0)
    w = inverse[...]
    wh, th = w.astype(BF16), total.astype(BF16)
    wl = (w - wh.astype(F32)).astype(BF16)
    tl = (total - th.astype(F32)).astype(BF16)
    small = jnp.dot(wh, tl, preferred_element_type=F32) + jnp.dot(wl, th, preferred_element_type=F32)
    out[...] = jnp.dot(wh, th, preferred_element_type=F32) + small


def last(inverse, early, keeps, came):
    vmem = pl.BlockSpec(memory_space=pltpu.VMEM)
    return pl.pallas_call(
        last_kernel,
        out_shape=jax.ShapeDtypeStruct((inverse.shape[0], early.shape[1]), F32),
        in_specs=[vmem] * 5,
        out_specs=vmem,
        compiler_params=pltpu.CompilerParams(vmem_limit_bytes=16 * 2**20),
    )(inverse, early, *keeps, came)


def full_path(rows, cols, sketch, tiles, tile_user, tile_item, tile_count, item_owner, packed):
    n = packed.shape[1]
    r = lax.broadcasted_iota(jnp.int32, (n, n), 0)
    c = lax.broadcasted_iota(jnp.int32, (n, n), 1)
    mixed, side, tail = packed[:n], packed[n : 2 * n], packed[2 * n : 2 * n + 1]
    first = jnp.where(r >= c, mixed, mixed.T)
    second = jnp.where(r < c, mixed, jnp.where(r > c, mixed.T, tail))
    gram = jnp.block([[first, side.T], [side, second]])
    lower = jnp.linalg.cholesky(gram)
    basis = lax.linalg.triangular_solve(lower, sketch, left_side=False, lower=True, transpose_a=True).astype(BF16)
    have = {0: basis}
    for bit in bits_of(cols):
        for place in list(have):
            have[place | bit] = swap(have[place], "cols", cols, bit)
    slab = jnp.concatenate([have[i] for i in range(cols)], axis=0)
    col = lax.axis_index("cols")
    row = lax.axis_index("rows")
    per_piece = sketch.shape[0] // tiles.shape[2]
    owner = item_owner[0]
    tile_size = tiles.shape[2]

    def step(index, sums):
        user = tile_user[index]
        block = lax.bitwise_xor(user // per_piece, col) * per_piece + user % per_piece
        part_rows = lax.dynamic_slice_in_dim(slab, block * tile_size, tile_size, 0)
        part = lax.dot_general(part_rows, tiles[index], (((0,), (0,)), ((), ())), preferred_element_type=F32)
        place = lax.bitwise_xor(owner[tile_item[index]], row)
        now = lax.dynamic_index_in_dim(sums, place, 0, keepdims=False)
        return lax.dynamic_update_index_in_dim(sums, now + part, place, 0)

    totals = jnp.zeros((owner.shape[0], sketch.shape[1], tile_size), F32)
    totals = lax.fori_loop(0, tile_count[0], step, totals)
    for bit in bits_of(rows):
        totals = totals[:bit] + swap(totals[bit:], "rows", rows, bit)
    return totals[0]


def after(value, *others):
    return lax.optimization_barrier((value, *others))[0]


def exchange(lanes, rows):
    groups = []
    for bit in sorted({lane[2] for lane in lanes}):
        members = [i for i, lane in enumerate(lanes) if lane[2] == bit]
        sent = [lanes[i][1].reshape(-1, lanes[i][1].shape[2]) for i in members]
        groups.append((members, swap(jnp.concatenate(sent, axis=0), "rows", rows, 1 << bit)))
    return groups


def received(lanes, groups):
    got = [None] * len(lanes)
    for members, came in groups:
        first = 0
        for i in members:
            shape = lanes[i][1].shape
            size = shape[0] * shape[1]
            got[i] = came[first : first + size].reshape(shape)
            first += size
    return [lane[0] + g.astype(F32) for lane, g in zip(lanes, got)]


def split(total):
    half = total.shape[0] // 2
    return total[:half], total[half:].astype(BF16)


def body(rows, cols, sketch, tiles, tile_user, tile_item, tile_count, item_owner):
    row_bits = rows.bit_length() - 1
    first_order = tuple(range(row_bits))
    orders = (first_order, (1, 0) + first_order[2:])
    row = lax.axis_index("rows")
    col = lax.axis_index("cols")
    meta = jnp.stack([tile_count[0], row, col]).astype(jnp.int32)
    scalars = (tile_user, tile_item, item_owner[0], meta)
    far_bit, *near_bits = bits_of(cols)

    def spread(piece):
        have = {0: piece}
        for bit in near_bits:
            for place in list(have):
                have[place | bit] = swap(have[place], "cols", cols, bit)
        return [have[i] for i in range(cols // 2)]

    fence = lax.optimization_barrier
    far = far_bit
    flat, *chunks = split_sketch(sketch)
    near = list(zip(*[spread(c) for c in chunks]))
    crossed = [swap(c, "cols", cols, far) for c in chunks]
    packed = packed_gram(flat)
    for bit in near_bits:
        packed = packed + swap(packed, "cols", cols, bit)
    came = swap(packed, "rows", rows, 2)
    near[0] = (after(near[0][0], packed), *near[0][1:])
    sums = near_sums(scalars, near, tiles, rows)
    packed, came, *sums = fence((packed, came, *sums))
    packed = packed + came
    came = swap(packed, "rows", rows, 4)
    crossed[0] = after(crossed[0], packed)
    outs = far_sums(scalars, [[p] for p in spread(crossed[0])], sums[0], tiles, orders, EARLY_COST)
    packed, came, *outs = fence((packed, came, *outs))
    packed = packed + came
    came = swap(packed, "cols", cols, far)
    lanes = [(outs[2 * o], outs[2 * o + 1], order[0]) for o, order in enumerate(orders)]
    groups = exchange(lanes, rows)
    crossed[1] = after(crossed[1], packed)
    later = far_sums(scalars, [[p] for p in spread(crossed[1])], sums[1], tiles, orders, LATE_COST)
    flying = [g[1] for g in groups]
    packed, came, *rest = fence((packed, came, *flying, *later))
    groups = [(g[0], x) for g, x in zip(groups, rest)]
    later = rest[len(groups) :]
    packed = packed + came
    stages = [1] + [1 << b for b in range(3, row_bits)]

    totals = received(lanes, groups)
    late = [(later[2 * o], later[2 * o + 1]) for o in range(len(orders))]
    for step in range(1, row_bits + 1):
        lanes = []
        if step < row_bits:
            lanes += [(*split(t), order[step]) for t, order in zip(totals, orders)]
        lanes += [(*pair, order[step - 1]) for pair, order in zip(late, orders)]
        groups = exchange(lanes, rows)
        flying = [g[1] for g in groups]
        sends = [lane[1] for lane in lanes]
        if step > 1 and step <= len(stages) + 1:
            packed = packed + after(came, *sends)
        if step <= len(stages):
            came = swap(packed, "rows", rows, stages[step - 1])
        if step == len(stages) + 1:
            inverse, good = factor(after(packed, *sends))
            free = [i for i, g in enumerate(groups) if max(g[0]) < len(lanes) - len(orders)]
            inverse, *tied = fence((inverse, *[flying[i] for i in free]))
            for i, x in zip(free, tied):
                flying[i] = x
        groups = [(g[0], x) for g, x in zip(groups, flying)]
        if step < row_bits:
            new = received(lanes, groups)
            totals, new = new[: len(orders)], new[len(orders) :]
            late = [split(t) for t in new]
        if step == row_bits - 1:
            early = jnp.concatenate([t[0] for t in totals], axis=1)
    keeps = [lane[0] for lane in lanes]
    came = groups[0][1].reshape(len(lanes), *lanes[0][1].shape[1:])
    out = lax.cond(
        good[0] > 0,
        lambda: last(inverse, early, keeps, came),
        lambda: full_path(rows, cols, flat.T, tiles, tile_user, tile_item, tile_count, item_owner, packed),
    )
    return out[None, None]


def solution(mesh):
    placed = (
        P(("rows", "cols"), None),
        P(("rows", "cols"), None, None),
        P(("rows", "cols")),
        P(("rows", "cols")),
        P(("rows", "cols")),
        P("cols", None),
    )
    return jax.shard_map(
        functools.partial(body, mesh.shape["rows"], mesh.shape["cols"]),
        mesh=mesh,
        in_specs=placed,
        out_specs=P("rows", "cols", None, None),
        check_vma=False,
    )
```
